32 devices in a mesh: gx: 8 (over z, core), gy: 4 (over y, x).
Axes of the slice: x: 2, y: 2, z: 4, core: 2. Of those that a mesh axis runs over, the one named last changes fastest.
Arguments:
- velocity: float32 [2048, 16, 1024], P('gx', None, 'gy'), may hold values from -6 to 6
- lower_x: float32 [2048, 256], P('gx'), may hold values from 0 to 1, as said below
- upper_x: float32 [2048, 256], P('gx'), may hold values from 0 to 1, as said below
- lower_carry_x: float32 [2048], P('gx'), may hold values from 0 to 1.3
- upper_carry_x: float32 [2048], P('gx'), may hold values from 0 to 1.3
- lower_y: float32 [1024, 256], P('gy'), may hold values from 0 to 1, as said below
- upper_y: float32 [1024, 256], P('gy'), may hold values from 0 to 1, as said below
- lower_carry_y: float32 [1024], P('gy'), may hold values from 0 to 1.3
- upper_carry_y: float32 [1024], P('gy'), may hold values from 0 to 1.3
- wall_force: float32 [2048, 16, 128], P(('gx', 'gy')), may hold values from -6 to 6
- wall_owner: int32 [2048, 1], P(('gx', 'gy')), may hold values from 0 to 3; in each aligned block of 64 rows (0 to 63, 64 to 127, ...) at most 32 rows name the same one
- wall_offset: int32 [2048], P(('gx', 'gy')), may hold values from 0 to 511
- solid_mask: int32 [2048, 8], P('gx', 'gy'), may hold values 0 or 1
Outputs:
- advanced: float32 [2048, 16, 1024], P('gx', None, 'gy')
The draws below stay inside these ranges and needn't reach their ends.
Inputs may be any that keep to these rules, and one draw needn't show every extreme that they name: `wall_owner`: in the rows of one device no tile is named by more than 32 rows, a bound that some block reaches. `wall_offset`: the offset is row * 2 + block within the owner tile. `lower_x`: zero above the diagonal of each block of 256 rows. `upper_x`: zero below the diagonal of each block of 256 rows. `lower_y`: zero above the diagonal of each block of 256 rows. `upper_y`: zero below the diagonal of each block of 256 rows.
All inputs are finite; a program needn't handle non-finite values. No bound on the sum of `solid_mask` on one device may be relied on, other than what follows from the above.
Results may differ from the reference program's by a relative error of at most 0.00013.
Values sent between devices are 32-bit elements; how exact they have to be, the bound alone decides.
No kernel may reach another device: no remote copies, remote signals or barrier semaphores. Data moves between devices by JAX's collectives and lax.ppermute only.
A program may use at most 128 MiB of HBM per device.

```python
import math
import jax
import jax.numpy as jnp
import numpy as np
from jax import lax

CX = 256
CY = 256
P_SIZE = 16
BLOCKW = 128
WALL = 64
CAP = 32
NX = 2048
NY = 1024
ENTRIES = 2048
N_GX = 8
N_GY = 4


def triangle(key, total_rows, block_rows, lower):
    first, second = jax.random.split(key)
    row_ids = jnp.arange(total_rows)[:, None] % block_rows
    col_ids = jnp.arange(block_rows)[None, :]
    distance = row_ids - col_ids if lower else col_ids - row_ids
    diagonal = 0.5 + 0.3 * jax.random.uniform(first, (total_rows, block_rows), jnp.float32)
    rough = 0.5 + jax.random.uniform(second, (total_rows, block_rows), jnp.float32)
    beside = 0.03 * jnp.exp(-distance.astype(jnp.float32) / 64.0) * rough
    return jnp.where(distance == 0, diagonal, jnp.where(distance > 0, beside, 0.0)).astype(jnp.float32)


def carry_column(key, total_rows, block_rows, forward):
    first, second = jax.random.split(key)
    tiles = total_rows // block_rows
    retains = jnp.exp(jax.random.uniform(first, (tiles,), jnp.float32, jnp.log(0.8), jnp.log(0.98)))
    positions = jnp.arange(total_rows)
    retain = retains[positions // block_rows]
    inside = positions % block_rows
    reach = inside + 1 if forward else block_rows - inside
    rough = 0.7 + 0.6 * jax.random.uniform(second, (total_rows,), jnp.float32)
    values = retain ** (reach.astype(jnp.float32) / block_rows) * rough
    at_edge = inside == block_rows - 1 if forward else inside == 0
    return jnp.where(at_edge, retain, values).astype(jnp.float32)


def draw_lower_x(key, part):
    return triangle(key, NX, CX, True)


def draw_upper_x(key, part):
    return triangle(key, NX, CX, False)


def draw_lower_y(key, part):
    return triangle(key, NY, CY, True)


def draw_upper_y(key, part):
    return triangle(key, NY, CY, False)


def draw_lower_carry_x(key, part):
    return carry_column(key, NX, CX, True)


def draw_upper_carry_x(key, part):
    return carry_column(key, NX, CX, False)


def draw_lower_carry_y(key, part):
    return carry_column(key, NY, CY, True)


def draw_upper_carry_y(key, part):
    return carry_column(key, NY, CY, False)


def touch_ends(drawn, key, smallest, largest):
    spot = [jax.random.randint(jax.random.fold_in(key, axis), (), 0, length) for axis, length in enumerate(drawn.shape)]
    longest = drawn.shape.index(max(drawn.shape))
    neighbour = spot[:longest] + [(spot[longest] + 1) % drawn.shape[longest]] + spot[longest + 1:]
    return drawn.at[tuple(spot)].set(smallest).at[tuple(neighbour)].set(largest)


def steps_of(rng, extent, cuts, low, top_value):
    level = 1.0
    for position, blocks in cuts:
        draws = jax.random.uniform(jax.random.fold_in(jax.random.fold_in(rng, 6), position), (blocks,), jnp.float32, low / len(cuts), top_value / len(cuts))
        level = level * jnp.repeat(jnp.exp(draws), extent[position] // blocks).reshape((-1,) + (1,) * (len(extent) - 1 - position))
    return level


def deal_out(rng, own, number, rows, count, top, most, skew):
    order = jax.random.permutation(rng, count)
    crowded, ordinary = load_shares(count, rows * top, most, skew, True), load_shares(count, rows * top, most, skew, False)
    places = jnp.arange(count)

    def named(tallies, offset_by):
        used = int((tallies > 0).sum())
        fixed = max(1, used // 4)
        moved = fixed + (places - fixed + offset_by * (used - fixed)) % max(1, count - fixed)
        return jnp.zeros((count,), jnp.int32).at[order[jnp.where(places < fixed, places, moved)]].set(jnp.asarray(tallies, jnp.int32))

    tallies = jnp.where(number % 4 == 0, named(crowded, number // 4), named(ordinary, number - number // 4 - 1))
    mixed = jax.random.permutation(jax.random.fold_in(own, 3), count)
    source_of, taker = mixed[0:count // 2 * 2:2], mixed[1:count // 2 * 2:2]
    room = jnp.minimum(tallies[source_of] - 1, most - tallies[taker]) // 2
    room = jnp.where((source_of == order[0]) | (taker == order[0]) | (tallies[taker] == 0), 0, jnp.maximum(room, 0))
    moved = jax.random.randint(jax.random.fold_in(own, 4), (count // 2,), 0, 1 << 20) % (room + 1)
    tallies = tallies.at[source_of].add(-moved).at[taker].add(moved)
    labels = jnp.searchsorted(jnp.cumsum(tallies), jnp.arange(rows * top), side="right").astype(jnp.int32)
    table = labels.reshape(top, rows).T
    table = table[jax.random.permutation(jax.random.fold_in(own, 1), rows)]
    offset_by = jax.random.randint(jax.random.fold_in(own, 2), (rows, 1), 0, top)
    return jnp.take_along_axis(table, (jnp.arange(top)[None, :] + offset_by) % top, axis=1)


def load_shares(count, total, most, skew, full):
    loads = [(1 << 20) // math.isqrt(standing ** skew) + 1 for standing in range(1, count + 1)]
    largest = most if full else min(most, max(-(-total // count), total * loads[0] // sum(loads)))
    least = 1 if total - largest >= count - 1 else 0
    counts, rest = [largest] + [least] * (count - 1), total - largest - least * (count - 1)
    while rest > 0:
        candidates = [i for i in range(1, count) if counts[i] < largest] or [i for i in range(1, count) if counts[i] < most]
        mass, budget = sum([loads[i] for i in candidates]), rest
        for i in candidates:
            more = min(most - counts[i], max(1, budget * loads[i] // mass), rest)
            counts[i] = counts[i] + more
            rest = rest - more
    return np.array(counts)


def scatter_about(key, dims, spread, limit, cuts=(), kind=jnp.bfloat16):
    result = jax.random.normal(key, dims, jnp.float32) * spread
    if len(cuts) > 0:
        result = steps_of(key, dims, cuts, -0.22, 0.18) * result
    return jnp.clip(result, min=-limit, max=limit).astype(kind)


def setup_inputs(seed: int = 0) -> dict:
    seeds = jax.random.split(jax.random.key(seed), 14)
    velocity = scatter_about(seeds[0], (NX, P_SIZE, NY), 1.0, 6.0, ((0, 8), (2, 4)), jnp.float32)
    lower_x = draw_lower_x(jax.random.fold_in(seeds[13], 71), 0)
    upper_x = draw_upper_x(jax.random.fold_in(seeds[13], 71), 0)
    lower_carry_x = draw_lower_carry_x(jax.random.fold_in(seeds[13], 71), 0)
    upper_carry_x = draw_upper_carry_x(jax.random.fold_in(seeds[13], 71), 0)
    lower_y = draw_lower_y(jax.random.fold_in(seeds[13], 71), 0)
    upper_y = draw_upper_y(jax.random.fold_in(seeds[13], 71), 0)
    lower_carry_y = draw_lower_carry_y(jax.random.fold_in(seeds[13], 71), 0)
    upper_carry_y = draw_upper_carry_y(jax.random.fold_in(seeds[13], 71), 0)
    wall_force = scatter_about(seeds[9], (ENTRIES, P_SIZE, BLOCKW), 1.0, 6.0, ((0, 32),), jnp.float32)
    wall_owner_keys = jax.random.split(jax.random.fold_in(seeds[10], 1), ENTRIES // WALL)
    wall_owner_turns = jax.random.permutation(jax.random.fold_in(seeds[10], 3), ENTRIES // WALL)
    wall_owner = jax.vmap(lambda own, number: deal_out(jax.random.fold_in(seeds[10], 2), own, number, WALL, N_GY, 1, CAP, 2))(wall_owner_keys, wall_owner_turns).reshape((ENTRIES, 1))
    wall_offset = touch_ends(jax.random.randint(seeds[11], (ENTRIES,), 0, CX * (CY // BLOCKW)), jax.random.fold_in(seeds[11], 1), 0, (CX * (CY // BLOCKW)) - 1).astype(jnp.int32)
    solid_mask = touch_ends((jax.random.randint(seeds[12], (NX, NY // BLOCKW), 0, 4) < 1).astype(jnp.int32), jax.random.fold_in(seeds[12], 1), 0, 1)
    return dict(velocity=velocity, lower_x=lower_x, upper_x=upper_x, lower_carry_x=lower_carry_x, upper_carry_x=upper_carry_x, lower_y=lower_y, upper_y=upper_y, lower_carry_y=lower_carry_y, upper_carry_y=upper_carry_y, wall_force=wall_force, wall_owner=wall_owner, wall_offset=wall_offset, solid_mask=solid_mask)


def forward_step(incoming, pieces):
    matrix, vector, column = pieces
    swept = jnp.dot(matrix, vector, precision=lax.Precision.HIGHEST, preferred_element_type=jnp.float32) + column[:, None] * incoming[None, :]
    return swept[-1], swept


def backward_step(incoming, pieces):
    matrix, vector, column = pieces
    swept = jnp.dot(matrix, vector, precision=lax.Precision.HIGHEST, preferred_element_type=jnp.float32) + column[:, None] * incoming[None, :]
    return swept[0], swept


def right_step(incoming, pieces):
    matrix, vector, column = pieces
    swept = jnp.dot(vector, matrix.T, precision=lax.Precision.HIGHEST, preferred_element_type=jnp.float32) + incoming[:, None] * column[None, :]
    return swept[:, -1], swept


def left_step(incoming, pieces):
    matrix, vector, column = pieces
    swept = jnp.dot(vector, matrix.T, precision=lax.Precision.HIGHEST, preferred_element_type=jnp.float32) + incoming[:, None] * column[None, :]
    return swept[:, 0], swept


def reference(velocity, lower_x, upper_x, lower_carry_x, upper_carry_x, lower_y, upper_y, lower_carry_y, upper_carry_y, wall_force, wall_owner, wall_offset, solid_mask):
    nblock = CY // BLOCKW
    entries = wall_force.shape[0]
    strip = (jnp.arange(entries, dtype=jnp.int32) // WALL) // N_GY
    row_ids = (strip * CX + wall_offset // nblock).astype(jnp.int32)
    block_ids = (wall_owner[:, 0] * nblock + wall_offset % nblock).astype(jnp.int32)
    forcing = jnp.zeros((NX, P_SIZE, NY // BLOCKW, BLOCKW), jnp.float32).at[row_ids, :, block_ids, :].add(wall_force)
    forcing = forcing.reshape(NX, P_SIZE, NY)
    padded = jnp.pad(velocity, ((0, 0), (0, 0), (1, 1)))
    explicit_y = velocity + 0.5 * (padded[:, :, 2:] + padded[:, :, :-2] - 2.0 * velocity) + forcing
    blocks = explicit_y.reshape(N_GX, CX, P_SIZE * NY)
    zero_row = jnp.zeros((P_SIZE * NY,), jnp.float32)
    unused, swept_x = lax.scan(forward_step, zero_row, (lower_x.reshape(N_GX, CX, CX), blocks, lower_carry_x.reshape(N_GX, CX)))
    unused, halfway = lax.scan(backward_step, zero_row, (upper_x.reshape(N_GX, CX, CX), swept_x, upper_carry_x.reshape(N_GX, CX)), reverse=True)
    halfway = halfway.reshape(NX, P_SIZE, NY)
    padded = jnp.pad(halfway, ((1, 1), (0, 0), (0, 0)))
    explicit_x = halfway + 0.5 * (padded[2:] + padded[:-2] - 2.0 * halfway)
    columns = explicit_x.reshape(NX * P_SIZE, N_GY, CY).transpose(1, 0, 2)
    zero_col = jnp.zeros((NX * P_SIZE,), jnp.float32)
    unused, swept_y = lax.scan(right_step, zero_col, (lower_y.reshape(N_GY, CY, CY), columns, lower_carry_y.reshape(N_GY, CY)))
    unused, implicit = lax.scan(left_step, zero_col, (upper_y.reshape(N_GY, CY, CY), swept_y, upper_carry_y.reshape(N_GY, CY)), reverse=True)
    implicit = implicit.transpose(1, 0, 2).reshape(NX, P_SIZE, NY // BLOCKW, BLOCKW)
    fluid = (solid_mask == 0)[:, None, :, None]
    return jnp.where(fluid, implicit, jnp.float32(0.0)).reshape(NX, P_SIZE, NY)
```

```python
import functools

import jax
import jax.numpy as jnp
from jax import lax
from jax.experimental import pallas as pl
from jax.experimental.pallas import tpu as pltpu
from jax.sharding import PartitionSpec as P

F32 = jnp.float32
BF16 = jnp.bfloat16
HIGHEST = lax.Precision.HIGHEST
VMEM = pl.BlockSpec(memory_space=pltpu.VMEM)
SMEM = pl.BlockSpec(memory_space=pltpu.SMEM)
ANY = pl.BlockSpec(memory_space=pl.ANY)


def f32_dot(left, right, dims):
    return lax.dot_general(left, right, (dims, ((), ())), precision=HIGHEST, preferred_element_type=F32)


def split(value):
    high = value.astype(BF16)
    return high, (value - high.astype(F32)).astype(BF16)


def left_of(value, axis):
    high, low = split(value)
    return jnp.concatenate([high, low, high], axis=axis)


def right_of(value, axis):
    high, low = split(value)
    return jnp.concatenate([high, high, low], axis=axis)


def bf16_dot(left, right, dims):
    return lax.dot_general(left, right, (dims, ((), ())), preferred_element_type=F32)


def params(vmem_mib, side_effects=False):
    return pltpu.CompilerParams(vmem_limit_bytes=vmem_mib << 20)


def call(kernel, out_shape, in_specs, vmem_mib, out_specs=None, scratch=(), flops=0, moved=0, **more):
    if out_specs is None:
        out_specs = jax.tree.map(lambda _: VMEM, out_shape)
    return pl.pallas_call(
        kernel,
        out_shape=out_shape,
        in_specs=in_specs,
        out_specs=out_specs,
        scratch_shapes=list(scratch),
        compiler_params=params(vmem_mib),
        cost_estimate=pl.CostEstimate(flops=flops, bytes_accessed=moved, transcendentals=0),
        **more,
    )


def struct(*shape, dtype=F32):
    return jax.ShapeDtypeStruct(shape, dtype)


def pack_kernel(count, room, me_ref, owner_ref, offset_ref, force_ref, *refs):
    outs, places, taken = refs[:count], refs[count], refs[count + 1]
    walls = force_ref.shape[0]
    for shift in range(count):
        outs[shift][...] = jnp.zeros_like(outs[shift])
        taken[shift] = 0
    places[...] = jnp.full_like(places, -1.0)
    lanes = lax.broadcasted_iota(jnp.int32, places.shape[1:], 1)
    rows = lax.broadcasted_iota(jnp.int32, places.shape[1:], 0)

    def step(entry, carry):
        shift = lax.rem(owner_ref[entry] - me_ref[0] + count, count)
        slot = taken[shift]
        taken[shift] = slot + 1
        for s in range(count):

            @pl.when(shift == s)
            def _():
                outs[s][pl.ds(slot, 1)] = force_ref[pl.ds(entry, 1)]

        here = (lanes == slot) & (rows == 0)
        places[pl.ds(shift, 1)] = jnp.where(here, offset_ref[entry].astype(F32), places[shift])[None]
        return carry

    lax.fori_loop(0, walls, step, 0)


def pack(me, owner, offset, force, count, room):
    shape = (room,) + force.shape[1:]
    return call(
        functools.partial(pack_kernel, count, room),
        [struct(*shape) for _ in range(count)] + [struct(count, 8, 256)],
        [SMEM, SMEM, SMEM, VMEM],
        8,
        scratch=[pltpu.SMEM((count,), jnp.int32)],
        moved=2 * force.size * 4,
    )(me, owner, offset, force)


def row(ref, index):
    base = index // 8 * 8
    return ref[base : base + 8, :][index - base : index - base + 1]


def half_shift_lanes(value):
    length = value.shape[1]
    at = lax.broadcasted_iota(jnp.int32, value.shape, 1)
    before = jnp.where(at == 0, 0.0, pltpu.roll(value, 1, 1))
    after = jnp.where(at == length - 1, 0.0, pltpu.roll(value, length - 1, 1))
    return 0.5 * (before + after)


def half_shift_rows(value):
    length = value.shape[0]
    at = lax.broadcasted_iota(jnp.int32, value.shape, 0)
    before = jnp.where(at == 0, 0.0, pltpu.roll(value, 1, 0))
    after = jnp.where(at == length - 1, 0.0, pltpu.roll(value, length - 1, 0))
    return 0.5 * (before + after)


def factor_kernel(lx, ux, lcx, ucx, ly, uy, lcy, ucy, mx, my, aux, xrows, yrows, frows, scal):
    rows_x, rows_y = lx.shape[0], ly.shape[0]
    both = f32_dot(ux[...], lx[...], ((1,), (0,)))
    mx[...] = left_of(half_shift_rows(both), 1)
    both_y = f32_dot(uy[...], ly[...], ((1,), (0,)))
    my[...] = left_of(both_y.T, 0)
    zero = jnp.zeros((1, rows_x), F32)
    lc, uc = lcx[...], ucx[...]
    pad = jnp.zeros((7, rows_x), F32)
    u_lc = f32_dot(jnp.concatenate([lc, pad], 0), ux[...], ((1,), (1,)))[0:1]
    at = lax.broadcasted_iota(jnp.int32, (1, rows_x), 1)
    c0 = half_shift_lanes(u_lc)
    c1 = half_shift_lanes(uc) + jnp.where(at == rows_x - 1, 0.5, 0.0)
    c2 = jnp.where(at == 0, 0.5, 0.0)
    xrows[...] = jnp.concatenate([c0, c1, c2, zero, zero, zero, zero, zero], 0)
    lcv, ucv = lcy[...], ucy[...]
    pad_y = jnp.zeros((7, rows_y), F32)
    uy_lc = f32_dot(jnp.concatenate([lcv, pad_y], 0), uy[...], ((1,), (1,)))[0:1]
    f0 = row(ly, rows_y - 1)
    f1 = both_y[0:8][0:1]
    zero_y = jnp.zeros((1, rows_y), F32)
    turned = both_y.T
    m0, m1 = 0.5 * turned[0:8][0:1], 0.5 * turned[rows_y - 8 : rows_y][7:8]
    yrows[...] = jnp.concatenate([uy_lc, ucv, m0, m1, f0, f1, zero_y, zero_y], 0)
    lane = lax.broadcasted_iota(jnp.int32, (rows_y, 128), 1)
    cols = jnp.concatenate([f0, f1, pad_y[:6]], 0).T
    aux[...] = left_of(jnp.where(lane < 64, cols[:, 0:1], cols[:, 1:2]), 0)
    frows[...] = jnp.concatenate([row(lx, rows_x - 1), both[0:8][0:1], zero, zero, zero, zero, zero, zero], 0)

    def spread(value, index, width):
        return jnp.broadcast_to(value[:, index : index + 1], (1, width))

    last = row(ux, rows_x - 1)
    scal[0:8, :] = jnp.concatenate(
        [
            spread(lc, rows_x - 1, rows_x),
            spread(u_lc, 0, rows_x),
            spread(uc, 0, rows_x),
            spread(last, rows_x - 1, rows_x),
            spread(uc, rows_x - 1, rows_x),
            zero,
            zero,
            zero,
        ],
        0,
    )
    scal[8:16, :] = jnp.concatenate(
        [
            spread(lcv, rows_y - 1, rows_x),
            spread(uy_lc, 0, rows_x),
            spread(ucv, 0, rows_x),
            zero,
            zero,
            zero,
            zero,
            zero,
        ],
        0,
    )


def factors(lx, ux, lcx, ucx, ly, uy, lcy, ucy):
    rows, cols = lx.shape[0], ly.shape[0]
    return call(
        factor_kernel,
        [
            struct(rows, 3 * rows, dtype=BF16),
            struct(3 * cols, cols, dtype=BF16),
            struct(3 * cols, 128, dtype=BF16),
            struct(8, rows),
            struct(8, cols),
            struct(8, rows),
            struct(16, rows),
        ],
        [VMEM] * 8,
        16,
        flops=6 * 4 * rows**3,
        moved=8 * rows * rows * 4,
    )(lx, ux, lcx[None, :], ucx[None, :], ly, uy, lcy[None, :], ucy[None, :])


def explicit_kernel(chunk, func_ref, v_ref, e_ref, edge_ref):
    step = pl.program_id(0)
    planes, cols = v_ref.shape[1:]

    @pl.when(step == 0)
    def _():
        edge_ref[...] = jnp.zeros_like(edge_ref)

    low, high = edge_ref[0], edge_ref[1]
    for i in range(chunk):
        value = half_shift_lanes(v_ref[i])
        for b in range(e_ref.shape[0]):
            e_ref[b, i * planes : (i + 1) * planes, :] = value[:, b * 128 : (b + 1) * 128]
        low = low + func_ref[0, step * chunk + i] * value
        high = high + func_ref[1, step * chunk + i] * value
    edge_ref[0] = low
    edge_ref[1] = high


def explicit(velocity, func):
    rows, planes, cols = velocity.shape
    chunk = 32
    return pl.pallas_call(
        functools.partial(explicit_kernel, chunk),
        grid=(rows // chunk,),
        out_shape=[struct(cols // 128, rows * planes, 128), struct(2, planes, cols)],
        in_specs=[SMEM, pl.BlockSpec((chunk, planes, cols), lambda i: (i, 0, 0))],
        out_specs=[
            pl.BlockSpec((cols // 128, chunk * planes, 128), lambda i: (0, i, 0)),
            pl.BlockSpec((2, planes, cols), lambda i: (0, 0, 0)),
        ],
        compiler_params=params(8),
        cost_estimate=pl.CostEstimate(flops=8 * velocity.size, bytes_accessed=8 * velocity.size, transcendentals=0),
    )(func, velocity)


def x_edge_kernel(count, me_ref, table_ref, func_ref, edge_ref, frows, scal, halo_l, halo_r, *refs):
    payload, out = refs[:count], refs[count]
    planes, cols = edge_ref.shape[1:]
    width = payload[0].shape[2]
    nblock = cols // width
    room = payload[0].shape[0]
    low, high = edge_ref[0], edge_ref[1]
    at = lax.broadcasted_iota(jnp.int32, (planes, cols), 1)
    f0, f1 = frows[0:1, :], frows[1:2, :]
    keep_l = jnp.where(me_ref[0] > 0, 0.5, 0.0)
    keep_r = jnp.where(me_ref[0] < count - 1, 0.5, 0.0)
    hl, hr = halo_l[0:planes, :], halo_r[0:planes, :]
    for f, which in ((f0, 0), (f1, 1)):
        first = keep_l * jnp.sum(hl * f, axis=1, keepdims=True)
        last = keep_r * jnp.sum(hr * f, axis=1, keepdims=True)
        add = jnp.where(at == 0, first, 0.0) + jnp.where(at == cols - 1, last, 0.0)
        if which == 0:
            low = low + add
        else:
            high = high + add
    out[0:planes, :] = low
    out[planes : 2 * planes, :] = high
    out[2 * planes : 2 * planes + 8, :] = scal[0:8, :]
    for s in range(count):

        def step(slot, carry):
            place = table_ref[s * room + slot]

            @pl.when(place >= 0)
            def _():
                line = place // nblock
                lane = pl.ds(pl.multiple_of((place % nblock) * width, width), width)
                value = payload[s][slot]
                out[0:planes, lane] = out[0:planes, lane] + func_ref[0, line] * value
                out[planes : 2 * planes, lane] = out[planes : 2 * planes, lane] + func_ref[1, line] * value

            return carry

        lax.fori_loop(0, room, step, 0)


def x_edges(me, table, func, edge, frows, scal, halo_l, halo_r, payload):
    planes, cols = edge.shape[1:]
    count = len(payload)
    return call(
        functools.partial(x_edge_kernel, count),
        struct(2 * planes + 8, cols),
        [SMEM, SMEM, SMEM] + [VMEM] * (5 + count),
        8,
        moved=sum(p.size for p in payload) * 4,
    )(me, table, func, edge, frows, scal, halo_l, halo_r, *payload)


def sweep_kernel(count, me_ref, table_ref, mx, my, aux, yrows, halo_l, halo_r, e_hbm, *refs):
    payload, (w_ref, s_ref, zh_ref, e_ref, sem) = refs[:count], refs[count:]
    planes = w_ref.shape[0]
    rows = w_ref.shape[1]
    cols = w_ref.shape[2]
    copy = pltpu.make_async_copy(e_hbm, e_ref, sem)
    copy.start()
    width = payload[0].shape[2]
    nblock = cols // width
    room = payload[0].shape[0]
    keep_l = jnp.where(me_ref[0] > 0, 1.0, 0.0)
    keep_r = jnp.where(me_ref[0] < count - 1, 1.0, 0.0)
    halo = jnp.concatenate([keep_l * halo_l[0:planes, :], keep_r * halo_r[0:planes, :]], 0)
    zh = bf16_dot(right_of(halo, 1), mx[...], ((1,), (1,)))
    zh_ref[...] = zh
    copy.wait()
    for s in range(count):

        def step(slot, carry):
            place = table_ref[s * room + slot]

            @pl.when(place >= 0)
            def _():
                half, base = place % nblock, pl.multiple_of((place // nblock) * planes, planes)
                e_ref[half, pl.ds(base, planes), :] = e_ref[half, pl.ds(base, planes), :] + payload[s][slot]

            return carry

        lax.fori_loop(0, room, step, 0)
    lane = lax.broadcasted_iota(jnp.int32, (rows, 128), 1)

    def plane(p, total):
        here = [e_ref[b, pl.ds(p, rows, stride=planes), :] for b in range(nblock)]
        z = bf16_dot(mx[...], right_of(jnp.concatenate(here, 1), 0), ((1,), (0,)))
        zc = right_of(z, 1)
        w_ref[p] = bf16_dot(zc, my[...], ((1,), (0,)))
        t = bf16_dot(zc, aux[...], ((1,), (0,)))
        return jnp.where((lane == p) | (lane == 64 + p), t, total)

    total = lax.fori_loop(0, planes, plane, jnp.zeros((rows, 128), F32))
    turned = total.T
    low, high = turned[0:planes], turned[64 : 64 + planes]
    f0, f1 = yrows[4:5, :], yrows[5:6, :]
    zl, zr = zh[0:planes], zh[planes : 2 * planes]
    s_ref[0:planes, :] = low + 0.5 * (zl * f0[:, 0:1] + zr * f0[:, cols - 1 : cols])
    s_ref[planes : 2 * planes, :] = high + 0.5 * (zl * f1[:, 0:1] + zr * f1[:, cols - 1 : cols])


def sweep(me, table, mx, my, aux, yrows, halo_l, halo_r, e, payload, shape):
    rows, planes, cols = shape
    count = len(payload)
    return call(
        functools.partial(sweep_kernel, count),
        [struct(planes, rows, cols), struct(2 * planes, rows), struct(2 * planes, rows)],
        [SMEM, SMEM] + [VMEM] * 6 + [ANY] + [VMEM] * count,
        24,
        scratch=[pltpu.VMEM(e.shape, F32), pltpu.SemaphoreType.DMA],
        flops=3 * 2 * 2 * e.size * rows,
        moved=2 * e.size * 4,
    )(me, table, mx, my, aux, yrows, halo_l, halo_r, e, *payload)


def chain(parts, count, me, planes, f_in):
    lanes = parts.shape[2]
    zero = jnp.zeros((planes, lanes), F32)
    f, mine_f = zero, zero
    for k in range(count):
        f_in[k] = f
        mine_f = jnp.where(k == me, f, mine_f)
        scal = parts[k, 2 * planes : 2 * planes + 8, :]
        f = parts[k, 0:planes, :] + scal[0:1] * f
    g, mine_g, before = zero, zero, zero
    for k in range(count - 1, -1, -1):
        scal = parts[k, 2 * planes : 2 * planes + 8, :]
        mine_g = jnp.where(k == me, g, mine_g)
        if k + 1 < count:
            before = jnp.where(k + 1 == me, scal[3:4] * f_in[k + 1] + scal[4:5] * g, before)
        g = parts[k, planes : 2 * planes, :] + scal[1:2] * f_in[k] + scal[2:3] * g
    return mine_f, mine_g, before


def gather_parts(me, parts, received):
    count = len(received)
    for shift in range(count):
        parts[pl.ds(lax.rem(me - shift + count, count), 1)] = received[shift][...][None]


def x_join_kernel(count, me_ref, my, xrows, yrows, scal, s_ref, *refs):
    received, (out, moved, parts, f_in) = refs[:count], refs[count:]
    me = me_ref[0]
    planes = s_ref.shape[0] // 2
    gather_parts(me, parts, received)
    in_f, in_b, before = chain(parts, count, me, planes, f_in)
    low, high = s_ref[0:planes, :], s_ref[planes : 2 * planes, :]
    f0, f1 = yrows[4:5, :], yrows[5:6, :]
    for index, value in enumerate((in_f, in_b, before)):
        c = xrows[index : index + 1, :]
        low = low + jnp.sum(value * f0, axis=1, keepdims=True) * c
        high = high + jnp.sum(value * f1, axis=1, keepdims=True) * c
    out[0:planes, :] = low
    out[planes : 2 * planes, :] = high
    out[2 * planes : 2 * planes + 8, :] = scal[8:16, :]
    moved[...] = bf16_dot(right_of(jnp.concatenate([in_f, in_b, before], 0), 1), my[...], ((1,), (0,)))


def x_join(me, my, xrows, yrows, scal, s, received):
    count = len(received)
    height, cols = received[0].shape
    planes, rows = s.shape[0] // 2, s.shape[1]
    return call(
        functools.partial(x_join_kernel, count),
        [struct(2 * planes + 8, rows), struct(3 * planes, cols)],
        [SMEM] + [VMEM] * (5 + count),
        8,
        scratch=[pltpu.VMEM((count, height, cols), F32), pltpu.VMEM((count, planes, cols), F32)],
        moved=count * height * cols * 4,
    )(me, my, xrows, yrows, scal, s, *received)


def finish_kernel(count, part, me_ref, xrows, yrows, moved, solid, zh_ref, w_hbm, *refs):
    received, (out_hbm, parts, f_in, both, w_ref, out_ref, w_sem, out_sem) = refs[:count], refs[count:]
    me = me_ref[0]
    planes, rows, cols = w_ref.shape
    halves = out_ref.shape[0]

    def w_copy(k):
        span = pl.ds(k * part, part)
        return pltpu.make_async_copy(w_hbm.at[:, span, :], w_ref.at[:, span, :], w_sem.at[k])

    def out_copy(k, b):
        span = pl.ds(k * part * planes, part * planes)
        return pltpu.make_async_copy(out_ref.at[b, span, :], out_hbm.at[span, pl.ds(b * 128, 128)], out_sem.at[k, b])

    steps = rows // part
    for k in range(steps):
        w_copy(k).start()
    gather_parts(me, parts, received)
    in_f, in_b, _ = chain(parts, count, me, planes, f_in)
    both[0] = in_f
    both[1] = in_b
    y = yrows[0:4, :]
    width = cols // solid.shape[1]
    for k in range(steps):
        lo = k * part
        c = xrows[0:3, lo : lo + part]
        fluid = [jnp.broadcast_to(solid[lo : lo + part, b * 128 // width : b * 128 // width + 1] == 0, (part, 128)) for b in range(halves)]
        w_copy(k).wait()
        for p in range(planes):
            left = jnp.concatenate(
                [
                    c,
                    both[0, p : p + 1, lo : lo + part],
                    both[1, p : p + 1, lo : lo + part],
                    zh_ref[p : p + 1, lo : lo + part],
                    zh_ref[planes + p : planes + p + 1, lo : lo + part],
                    jnp.zeros((1, part), F32),
                ],
                0,
            )
            right = jnp.concatenate(
                [
                    moved[p : p + 1, :],
                    moved[planes + p : planes + p + 1, :],
                    moved[2 * planes + p : 2 * planes + p + 1, :],
                    y,
                    jnp.zeros((1, cols), F32),
                ],
                0,
            )
            lh = left.astype(BF16).astype(F32)
            rh = right.astype(BF16).astype(F32)
            lc = jnp.concatenate([lh, lh, left - lh], 0).astype(BF16)
            rc = jnp.concatenate([rh, right - rh, rh], 0).astype(BF16)
            value = w_ref[p, lo : lo + part, :] + bf16_dot(lc, rc, ((0,), (0,)))
            for b in range(halves):
                out_ref[b, pl.ds(lo * planes + p, part, stride=planes), :] = jnp.where(
                    fluid[b], value[:, b * 128 : (b + 1) * 128], 0.0
                )
        for b in range(halves):
            out_copy(k, b).start()
    for k in range(steps):
        for b in range(halves):
            out_copy(k, b).wait()


def finish(me, xrows, yrows, moved, solid, zh, w, received):
    count = len(received)
    height = received[0].shape[0]
    planes, rows, cols = w.shape
    part, halves = 128, cols // 128
    out = call(
        functools.partial(finish_kernel, count, part),
        struct(rows * planes, cols),
        [SMEM] + [VMEM] * 5 + [ANY] + [VMEM] * count,
        20,
        out_specs=ANY,
        scratch=[
            pltpu.VMEM((count, height, rows), F32),
            pltpu.VMEM((count, planes, rows), F32),
            pltpu.VMEM((2, planes, rows), F32),
            pltpu.VMEM((planes, rows, cols), F32),
            pltpu.VMEM((halves, rows * planes, 128), F32),
            pltpu.SemaphoreType.DMA((rows // part,)),
            pltpu.SemaphoreType.DMA((rows // part, halves)),
        ],
        flops=2 * 24 * w.size,
        moved=8 * w.size,
    )(me, xrows, yrows, moved, solid, zh, w, *received)
    return out.reshape(rows, planes, cols)


def rotate(value, axis, shift):
    count = lax.axis_size(axis)
    return lax.ppermute(value, axis, [(i, (i + shift) % count) for i in range(count)])


def on_device(
    velocity,
    lower_x,
    upper_x,
    lower_carry_x,
    upper_carry_x,
    lower_y,
    upper_y,
    lower_carry_y,
    upper_carry_y,
    wall_force,
    wall_owner,
    wall_offset,
    solid_mask,
):
    rows, planes, cols = velocity.shape
    walls = wall_force.shape[0]
    n_x, n_y = lax.axis_size("gx"), lax.axis_size("gy")
    me_x = lax.axis_index("gx").astype(jnp.int32).reshape(1)
    me_y = lax.axis_index("gy").astype(jnp.int32).reshape(1)
    room = 2 * walls // n_y
    *packed, places = pack(me_y, wall_owner[:, 0], wall_offset, wall_force, n_y, room)
    payload = [packed[0]] + [rotate(packed[s], "gy", s) for s in range(1, n_y)]
    first, last = velocity[:, :, 0].T, velocity[:, :, cols - 1].T
    edge_of = {1: last, n_y - 1: first}
    side = [None] + [
        rotate(jnp.concatenate([edge_of.get(s, jnp.zeros_like(first)), places[s]], 0), "gy", s) for s in range(1, n_y)
    ]
    table = jnp.concatenate([places[0, 0, :room]] + [side[s][planes, :room] for s in range(1, n_y)]).astype(jnp.int32)
    halo_l, halo_r = side[1], side[n_y - 1]
    mx, my, aux, xrows, yrows, frows, scal = factors(
        lower_x, upper_x, lower_carry_x, upper_carry_x, lower_y, upper_y, lower_carry_y, upper_carry_y
    )
    func = frows[0:2]
    e, edge = explicit(velocity, func)
    mine = x_edges(me_y, table, func, edge, frows, scal, halo_l, halo_r, payload)
    received = [mine] + [rotate(mine, "gx", s) for s in range(1, n_x)]
    w, s_edge, zh = sweep(me_y, table, mx, my, aux, yrows, halo_l, halo_r, e, payload, velocity.shape)
    mine, moved = x_join(me_x, my, xrows, yrows, scal, s_edge, received)
    received = [mine] + [rotate(mine, "gy", s) for s in range(1, n_y)]
    return finish(me_y, xrows, yrows, moved, solid_mask, zh, w, received)


def solution(mesh):
    placed = (
        P("gx", None, "gy"),
        P("gx", None),
        P("gx", None),
        P("gx"),
        P("gx"),
        P("gy", None),
        P("gy", None),
        P("gy"),
        P("gy"),
        P(("gx", "gy"), None, None),
        P(("gx", "gy"), None),
        P(("gx", "gy")),
        P("gx", "gy"),
    )
    return jax.shard_map(
        on_device, mesh=mesh, in_specs=placed, out_specs=P("gx", None, "gy"), check_vma=False
    )
```

```python
import functools

import jax
import jax.numpy as jnp
from jax import lax
from jax.experimental import pallas as pl
from jax.experimental.pallas import tpu as pltpu
from jax.sharding import PartitionSpec as P

F32 = jnp.float32
BF16 = jnp.bfloat16
HIGHEST = lax.Precision.HIGHEST
VMEM = pl.BlockSpec(memory_space=pltpu.VMEM)
SMEM = pl.BlockSpec(memory_space=pltpu.SMEM)
HBM = pl.BlockSpec(memory_space=pltpu.HBM)
LANES = 128


def f32_dot(left, right, dims):
    return lax.dot_general(left, right, (dims, ((), ())), precision=HIGHEST, preferred_element_type=F32)


def split(value):
    high = value.astype(BF16)
    return high, (value - high.astype(F32)).astype(BF16)


def left_of(value, axis):
    high, low = split(value)
    return jnp.concatenate([high, low, high], axis=axis)


def right_of(value, axis):
    high, low = split(value)
    return jnp.concatenate([high, high, low], axis=axis)


def bf16_dot(left, right, dims):
    return lax.dot_general(left, right, (dims, ((), ())), preferred_element_type=F32)


def params(vmem_mib, side_effects=False):
    return pltpu.CompilerParams(vmem_limit_bytes=vmem_mib << 20)


def call(kernel, out_shape, in_specs, vmem_mib, out_specs=None, scratch=(), flops=0, moved=0, **more):
    if out_specs is None:
        out_specs = jax.tree.map(lambda _: VMEM, out_shape)
    return pl.pallas_call(
        kernel,
        out_shape=out_shape,
        in_specs=in_specs,
        out_specs=out_specs,
        scratch_shapes=list(scratch),
        compiler_params=params(vmem_mib),
        cost_estimate=pl.CostEstimate(flops=flops, bytes_accessed=moved, transcendentals=0),
        **more,
    )


def struct(*shape, dtype=F32):
    return jax.ShapeDtypeStruct(shape, dtype)


def sort_walls(count, room, me, owner_ref, value_of, table, taken):
    for shift in range(count):
        taken[shift] = shift * room

    def step(entry, carry):
        shift = owner_ref[entry] - me
        shift = jnp.where(shift < 0, shift + count, shift)
        slot = taken[shift]
        taken[shift] = slot + 1
        table[slot] = value_of(entry)
        return carry

    lax.fori_loop(0, owner_ref.shape[0], step, 0, unroll=8)


def extras(rows, shift, count):
    return (rows // LANES if shift in (1, count - 1) else 0) + 1


def pack_kernel(count, room, chunk, owner_ref, offset_ref, force_hbm, v_hbm, *refs):
    outs, (force_ref, v_ref, table, taken, sem, v_sem) = refs[:count], refs[count:]
    walls = owner_ref.shape[0]
    rows, planes, cols = v_ref.shape
    me = lax.axis_index("gy")
    steps = rows // chunk
    copy = pltpu.make_async_copy(force_hbm, force_ref.at[pl.ds(0, walls)], sem)
    copy.start()

    def v_copy(k):
        span = pl.ds(k * chunk, chunk)
        return pltpu.make_async_copy(v_hbm.at[span], v_ref.at[span], v_sem.at[k])

    for k in range(steps):
        v_copy(k).start()
    force_ref[walls] = jnp.zeros(force_ref.shape[1:], F32)
    for slot in range(count * room):
        table[slot] = walls
    sort_walls(count, room, me, owner_ref, lambda entry: entry, table, taken)
    copy.wait()
    lane = lax.broadcasted_iota(jnp.int32, (planes, LANES), 1)
    for shift in list(range(1, count)) + [0]:
        places = jnp.full((planes, LANES), -1, jnp.int32)
        for slot in range(room):
            entry = table[shift * room + slot]
            outs[shift][slot] = force_ref[entry]
            place = jnp.where(entry < walls, offset_ref[jnp.minimum(entry, walls - 1)], -1)
            places = jnp.where(lane == slot, place, places)
        outs[shift][outs[shift].shape[0] - 1] = places.astype(F32)
    for block in range(rows // LANES):
        first, last = jnp.zeros((planes, LANES), F32), jnp.zeros((planes, LANES), F32)
        for x in range(LANES):
            at = block * LANES + x
            if at % chunk == 0:
                v_copy(at // chunk).wait()
            first = jnp.where(lane == x, pltpu.roll(v_ref[at, :, 0:LANES], x, 1), first)
            last = jnp.where(lane == x, pltpu.roll(v_ref[at, :, cols - LANES : cols], (x + 1) % LANES, 1), last)
        outs[1][room + block] = last
        outs[count - 1][room + block] = first


def pack(owner, offset, force, velocity, count, room):
    walls, planes, width = force.shape
    rows = velocity.shape[0]
    chunk = 64
    return call(
        functools.partial(pack_kernel, count, room, chunk),
        [struct(room + extras(rows, s, count), planes, width) for s in range(count)],
        [SMEM, SMEM, HBM, HBM],
        8,
        scratch=[
            pltpu.VMEM((walls + 1, planes, width), F32),
            pltpu.VMEM(velocity.shape, F32),
            pltpu.SMEM((count * room,), jnp.int32),
            pltpu.SMEM((count,), jnp.int32),
            pltpu.SemaphoreType.DMA,
            pltpu.SemaphoreType.DMA((rows // chunk,)),
        ],
    )(owner, offset, force, velocity)


def row(ref, index):
    base = index // 8 * 8
    return ref[base : base + 8, :][index - base : index - base + 1]


def half_shift_lanes(value):
    length = value.shape[1]
    at = lax.broadcasted_iota(jnp.int32, value.shape, 1)
    before = jnp.where(at == 0, 0.0, pltpu.roll(value, 1, 1))
    after = jnp.where(at == length - 1, 0.0, pltpu.roll(value, length - 1, 1))
    return 0.5 * (before + after)


def half_shift_rows(value):
    length = value.shape[0]
    at = lax.broadcasted_iota(jnp.int32, value.shape, 0)
    before = jnp.where(at == 0, 0.0, pltpu.roll(value, 1, 0))
    after = jnp.where(at == length - 1, 0.0, pltpu.roll(value, length - 1, 0))
    return 0.5 * (before + after)


def factor_kernel(lx, ux, lcx, ucx, ly, uy, lcy, ucy, mx, my, aux, my_t, aux_t, xrows, yrows, frows, scal):
    rows_x, rows_y = lx.shape[0], ly.shape[0]
    both = f32_dot(ux[...], lx[...], ((1,), (0,)))
    mx[...] = left_of(half_shift_rows(both), 1)
    both_y = f32_dot(uy[...], ly[...], ((1,), (0,)))
    turned = both_y.T
    my[...] = left_of(turned, 0)
    my_t[...] = left_of(half_shift_rows(turned), 0)
    zero = jnp.zeros((1, rows_x), F32)
    lc, uc = lcx[...], ucx[...]
    pad = jnp.zeros((7, rows_x), F32)
    u_lc = f32_dot(jnp.concatenate([lc, pad], 0), ux[...], ((1,), (1,)))[0:1]
    at = lax.broadcasted_iota(jnp.int32, (1, rows_x), 1)
    c0 = half_shift_lanes(u_lc)
    c1 = half_shift_lanes(uc) + jnp.where(at == rows_x - 1, 0.5, 0.0)
    c2 = jnp.where(at == 0, 0.5, 0.0)
    xrows[...] = jnp.concatenate([c0, c1, c2, zero, zero, zero, zero, zero], 0)
    lcv, ucv = lcy[...], ucy[...]
    pad_y = jnp.zeros((7, rows_y), F32)
    uy_lc = f32_dot(jnp.concatenate([lcv, pad_y], 0), uy[...], ((1,), (1,)))[0:1]
    f0 = row(ly, rows_y - 1)
    f1 = both_y[0:8][0:1]
    zero_y = jnp.zeros((1, rows_y), F32)
    m0, m1 = 0.5 * turned[0:8][0:1], 0.5 * turned[rows_y - 8 : rows_y][7:8]
    yrows[...] = jnp.concatenate([uy_lc, ucv, m0, m1, f0, f1, zero_y, zero_y], 0)
    lane = lax.broadcasted_iota(jnp.int32, (rows_y, 128), 1)
    cols = jnp.concatenate([f0, f1, pad_y[:6]], 0).T
    spread_cols = jnp.where(lane < 64, cols[:, 0:1], cols[:, 1:2])
    aux[...] = left_of(spread_cols, 0)
    aux_t[...] = left_of(half_shift_rows(spread_cols), 0)
    frows[...] = jnp.concatenate([row(lx, rows_x - 1), both[0:8][0:1], zero, zero, zero, zero, zero, zero], 0)

    def spread(value, index, width):
        return jnp.broadcast_to(value[:, index : index + 1], (1, width))

    last = row(ux, rows_x - 1)
    scal[0:8, :] = jnp.concatenate(
        [
            spread(lc, rows_x - 1, rows_x),
            spread(u_lc, 0, rows_x),
            spread(uc, 0, rows_x),
            spread(last, rows_x - 1, rows_x),
            spread(uc, rows_x - 1, rows_x),
            zero,
            zero,
            zero,
        ],
        0,
    )
    scal[8:16, :] = jnp.concatenate(
        [
            spread(lcv, rows_y - 1, rows_x),
            spread(uy_lc, 0, rows_x),
            spread(ucv, 0, rows_x),
            zero,
            zero,
            zero,
            zero,
            zero,
        ],
        0,
    )


def factors(lx, ux, lcx, ucx, ly, uy, lcy, ucy):
    rows, cols = lx.shape[0], ly.shape[0]
    return call(
        factor_kernel,
        [
            struct(rows, 3 * rows, dtype=BF16),
            struct(3 * cols, cols, dtype=BF16),
            struct(3 * cols, 128, dtype=BF16),
            struct(3 * cols, cols, dtype=BF16),
            struct(3 * cols, 128, dtype=BF16),
            struct(8, rows),
            struct(8, cols),
            struct(8, rows),
            struct(16, rows),
        ],
        [VMEM] * 8,
        8,
    )(lx, ux, lcx[None, :], ucx[None, :], ly, uy, lcy[None, :], ucy[None, :])


def velocity_kernel(func_ref, my_t, aux_t, v_hbm, high_ref, low_ref, s_ref, edge_ref, v_ref, sem):
    rows, planes, cols = v_ref.shape
    steps = sem.shape[0]
    chunk = rows // steps
    group = planes

    def copy(k):
        span = pl.ds(k * chunk, chunk)
        return pltpu.make_async_copy(v_hbm.at[span], v_ref.at[span], sem.at[k])

    for k in range(steps):
        copy(k).start()
    lane = lax.broadcasted_iota(jnp.int32, (group, LANES), 1)
    lower, upper = jnp.zeros((planes, cols), F32), jnp.zeros((planes, cols), F32)
    for k in range(steps):
        copy(k).wait()
        for i in range(k * chunk, (k + 1) * chunk):
            value = v_ref[i]
            lower = lower + func_ref[0, i] * value
            upper = upper + func_ref[1, i] * value
        flat = right_of(v_ref[k * chunk : (k + 1) * chunk].reshape(chunk * planes, cols), 1)
        r = bf16_dot(flat, my_t[...], ((1,), (0,)))
        t = bf16_dot(flat, aux_t[...], ((1,), (0,)))
        for g in range(chunk // group):
            here = slice(g * group * planes, (g + 1) * group * planes)
            x = slice(k * chunk + g * group, k * chunk + (g + 1) * group)
            turned = jnp.swapaxes(r[here].reshape(group, planes, cols), 0, 1)
            high, low = split(turned)
            high_ref[:, x, :] = high
            low_ref[:, x, :] = low
            picked = jnp.swapaxes(t[here].reshape(group, planes, LANES), 0, 1)
            total = jnp.zeros((group, LANES), F32)
            for p in range(planes):
                total = jnp.where((lane == p) | (lane == 64 + p), picked[p], total)
            s_ref[x, :] = total
    edge_ref[0] = half_shift_lanes(lower)
    edge_ref[1] = half_shift_lanes(upper)


def velocity_part(func, my_t, aux_t, velocity):
    rows, planes, cols = velocity.shape
    chunk = 64
    return call(
        velocity_kernel,
        [
            struct(planes, rows, cols, dtype=BF16),
            struct(planes, rows, cols, dtype=BF16),
            struct(rows, LANES),
            struct(2, planes, cols),
        ],
        [SMEM, VMEM, VMEM, HBM],
        16,
        scratch=[pltpu.VMEM(velocity.shape, F32), pltpu.SemaphoreType.DMA((rows // chunk,))],
    )(func, my_t, aux_t, velocity)


def halos(count, room, rows, payload):
    me = lax.axis_index("gy")
    blocks = rows // LANES

    def column(s, there):
        value = jnp.concatenate([payload[s][room + b] for b in range(blocks)], 1)
        return jnp.where(there, value, 0.0)

    return column(1, me > 0), column(count - 1, me < count - 1)


def x_edge_kernel(count, room, table_ref, func_ref, edge_ref, frows, scal, *refs):
    payload, out = refs[:count], refs[count]
    planes, cols = edge_ref.shape[1:]
    width = payload[0].shape[2]
    nblock = cols // width
    low, high = edge_ref[0], edge_ref[1]
    at = lax.broadcasted_iota(jnp.int32, (planes, cols), 1)
    f0, f1 = frows[0:1, :], frows[1:2, :]
    hl, hr = halos(count, room, frows.shape[1], payload)
    for f, which in ((f0, 0), (f1, 1)):
        first = 0.5 * jnp.sum(hl * f, axis=1, keepdims=True)
        last = 0.5 * jnp.sum(hr * f, axis=1, keepdims=True)
        add = jnp.where(at == 0, first, 0.0) + jnp.where(at == cols - 1, last, 0.0)
        if which == 0:
            low = low + add
        else:
            high = high + add
    out[2 * planes : 2 * planes + 8, :] = scal[0:8, :]
    sums = [jnp.zeros((planes, width), F32) for _ in range(2 * nblock)]
    for s in range(count):

        def step(slot, sums):
            sums = list(sums)
            place = jnp.maximum(table_ref[s * room + slot], 0)
            line, half = place // nblock, place % nblock
            value = payload[s][slot]
            for f in range(2):
                weight = func_ref[f, line]
                for b in range(nblock):
                    sums[f * nblock + b] += jnp.where(half == b, weight, 0.0) * value
            return tuple(sums)

        sums = lax.fori_loop(0, room, step, tuple(sums), unroll=8)
    out[0:planes, :] = low + jnp.concatenate(sums[:nblock], 1)
    out[planes : 2 * planes, :] = high + jnp.concatenate(sums[nblock:], 1)


def x_edges(table, func, edge, frows, scal, payload, room):
    planes, cols = edge.shape[1:]
    count = len(payload)
    return call(
        functools.partial(x_edge_kernel, count, room),
        struct(2 * planes + 8, cols),
        [SMEM, SMEM] + [VMEM] * (3 + count),
        8,
    )(table, func, edge, frows, scal, *payload)


def sweep_kernel(count, room, mx, my, aux, yrows, high_ref, low_ref, sv_ref, *refs):
    payload, (w_ref, s_ref, zh_ref, wall_ref) = refs[:count], refs[count:]
    planes, rows, cols = w_ref.shape
    slots, width = wall_ref.shape[1:]
    nblock = cols // width
    hl, hr = halos(count, room, rows, payload)
    m = mx[...]
    zh = bf16_dot(right_of(jnp.concatenate([hl, hr], 0), 1), m, ((1,), (1,)))
    zh_ref[...] = zh
    lane8 = lax.broadcasted_iota(jnp.int32, (8, LANES), 1)
    places = jnp.full((8, slots), -1.0, F32)
    for s in range(count):
        here = payload[s][payload[s].shape[0] - 1][0:8]
        if s:
            here = pltpu.roll(here, s * room, 1)
        places = jnp.where((lane8 >= s * room) & (lane8 < (s + 1) * room), here, places)
    line = jnp.floor(places * (1.0 / nblock))
    half = places - nblock * line
    column = half.T
    row_ids = lax.broadcasted_iota(jnp.int32, (rows, slots), 0).astype(F32)
    chosen = jnp.where(row_ids == line[0:1], 1.0, 0.0).astype(BF16)
    sel_high = bf16_dot(m[:, 0:rows], chosen, ((1,), (0,))).astype(BF16)
    sel_low = bf16_dot(m[:, rows : 2 * rows], chosen, ((1,), (0,))).astype(BF16)
    left = jnp.concatenate([m, sel_high, sel_low, sel_high], 1)
    keep = [jnp.broadcast_to(column[:, 0:1] == b, (slots, width)) for b in range(nblock)]
    for s in range(count):
        step = min(room, 16)
        for g in range(room // step):
            value = jnp.swapaxes(payload[s][g * step : (g + 1) * step], 0, 1)
            wall_ref[:, s * room + g * step : s * room + (g + 1) * step, :] = value
    lane = lax.broadcasted_iota(jnp.int32, (slots, LANES), 1)
    total = jnp.zeros((slots, LANES), F32)
    for p in range(planes):
        wall = wall_ref[p]
        wc = right_of(jnp.concatenate([jnp.where(k, wall, 0.0) for k in keep], 1), 1)
        r = right_of(bf16_dot(wc, my[...], ((1,), (0,))), 0)
        t = bf16_dot(wc, aux[...], ((1,), (0,)))
        total = jnp.where((lane == p) | (lane == 64 + p), t, total)
        high = high_ref[p]
        w_ref[p] = bf16_dot(left, jnp.concatenate([high, high, low_ref[p], r], 0), ((1,), (0,)))
    turned = bf16_dot(left, jnp.concatenate([right_of(sv_ref[...], 0), right_of(total, 0)], 0), ((1,), (0,))).T
    low, high = turned[0:planes], turned[64 : 64 + planes]
    f0, f1 = yrows[4:5, :], yrows[5:6, :]
    zl, zr = zh[0:planes], zh[planes : 2 * planes]
    s_ref[0:planes, :] = low + 0.5 * (zl * f0[:, 0:1] + zr * f0[:, cols - 1 : cols])
    s_ref[planes : 2 * planes, :] = high + 0.5 * (zl * f1[:, 0:1] + zr * f1[:, cols - 1 : cols])


def sweep(mx, my, aux, yrows, high, low, sv, payload, room):
    planes, rows, cols = high.shape
    count, width = len(payload), payload[0].shape[2]
    return call(
        functools.partial(sweep_kernel, count, room),
        [struct(planes, rows, cols), struct(2 * planes, rows), struct(2 * planes, rows)],
        [VMEM] * (7 + count),
        16,
        scratch=[pltpu.VMEM((planes, count * room, width), F32)],
    )(mx, my, aux, yrows, high, low, sv, *payload)


def chain(parts, count, me, planes, f_in):
    lanes = parts.shape[2]
    zero = jnp.zeros((planes, lanes), F32)
    f, mine_f = zero, zero
    for k in range(count):
        f_in[k] = f
        mine_f = jnp.where(k == me, f, mine_f)
        f = parts[k, 0:planes, :] + parts[k, 2 * planes : 2 * planes + 1, :] * f
    g, mine_g = zero, zero
    for k in range(count - 1, -1, -1):
        scal = parts[k, 2 * planes : 2 * planes + 8, :]
        mine_g = jnp.where(k == me, g, mine_g)
        g = parts[k, planes : 2 * planes, :] + scal[1:2] * f_in[k] + scal[2:3] * g
    return mine_f, mine_g


def pair_kernel(mine, other, out):
    planes = (mine.shape[0] - 8) // 2
    odd = lax.rem(lax.axis_index("gx"), 2) == 1
    left = jnp.where(odd, other[...], mine[...])
    right = jnp.where(odd, mine[...], other[...])
    out[...] = joined(left, right, planes)


def joined(left, right, planes):
    a, b, s = left[0:planes], left[planes : 2 * planes], left[2 * planes :]
    c, d, t = right[0:planes], right[planes : 2 * planes], right[2 * planes :]
    l0, c0, u0 = s[0:1], s[1:2], s[2:3]
    l1, c1, u1 = t[0:1], t[1:2], t[2:3]
    return jnp.concatenate(
        [c + l1 * a, b + u0 * (d + c1 * a), l0 * l1, c0 + u0 * c1 * l0, u0 * u1, t[3:8]],
        0,
    )


def pair(mine, other):
    return call(pair_kernel, struct(*mine.shape), [VMEM, VMEM], 8)(mine, other)


def gather_parts(me, parts, received):
    count = len(received)
    for shift in range(count):
        parts[pl.ds(lax.rem(me - shift + count, count), 1)] = received[shift][...][None]


def x_join_kernel(count, my, xrows, yrows, scal, s_ref, mine_ref, other_ref, *refs):
    received, (out, moved, parts, f_in) = refs[:count], refs[count:]
    me = lax.axis_index("gx")
    place = lax.div(me, 2)
    odd = lax.rem(me, 2) == 1
    planes = s_ref.shape[0] // 2
    gather_parts(place, parts, received)
    f, g = chain(parts, count, place, planes, f_in)
    mine, other = mine_ref[...], other_ref[...]
    left, right = jnp.where(odd, other, mine), jnp.where(odd, mine, other)
    a, ls = left[0:planes], left[2 * planes :]
    d, rs = right[planes : 2 * planes], right[2 * planes :]
    f_mid = a + ls[0:1] * f
    g_mid = d + rs[1:2] * f_mid + rs[2:3] * g
    in_f, in_b = jnp.where(odd, f_mid, f), jnp.where(odd, g, g_mid)
    ms = mine[2 * planes :]
    first = mine[planes : 2 * planes] + ms[1:2] * in_f + ms[2:3] * in_b
    before_s = jnp.where(odd, ls, parts[jnp.maximum(place - 1, 0), 2 * planes : 2 * planes + 8, :])
    before = jnp.where(me > 0, before_s[3:4] * in_f + before_s[4:5] * first, 0.0)
    low, high = s_ref[0:planes, :], s_ref[planes : 2 * planes, :]
    f0, f1 = yrows[4:5, :], yrows[5:6, :]
    for index, value in enumerate((in_f, in_b, before)):
        c = xrows[index : index + 1, :]
        low = low + jnp.sum(value * f0, axis=1, keepdims=True) * c
        high = high + jnp.sum(value * f1, axis=1, keepdims=True) * c
    out[0:planes, :] = low
    out[planes : 2 * planes, :] = high
    out[2 * planes : 2 * planes + 8, :] = scal[8:16, :]
    moved[...] = bf16_dot(right_of(jnp.concatenate([in_f, in_b, before], 0), 1), my[...], ((1,), (0,)))


def x_join(my, xrows, yrows, scal, s, mine, other, received):
    count = len(received)
    height, cols = received[0].shape
    planes, rows = s.shape[0] // 2, s.shape[1]
    return call(
        functools.partial(x_join_kernel, count),
        [struct(2 * planes + 8, rows), struct(3 * planes, cols)],
        [VMEM] * (7 + count),
        8,
        scratch=[pltpu.VMEM((count, height, cols), F32), pltpu.VMEM((count, planes, cols), F32)],
    )(my, xrows, yrows, scal, s, mine, other, *received)


def finish_kernel(count, part, xrows, yrows, moved, solid, zh_ref, w_ref, *refs):
    received, (out_hbm, parts, f_in, both, value_ref, out_ref, out_sem) = refs[:count], refs[count:]
    me = lax.axis_index("gy")
    planes, rows, cols = w_ref.shape
    halves = out_ref.shape[0]

    def out_copy(k, b):
        span = pl.ds(k * part * planes, part * planes)
        return pltpu.make_async_copy(out_ref.at[b, span, :], out_hbm.at[span, pl.ds(b * 128, 128)], out_sem.at[k, b])

    steps = rows // part
    gather_parts(me, parts, received)
    in_f, in_b = chain(parts, count, me, planes, f_in)
    both[0] = in_f
    both[1] = in_b
    y = yrows[0:4, :]
    width = cols // solid.shape[0]
    for k in range(steps):
        lo = k * part
        c = xrows[0:3, lo : lo + part]
        marks = jnp.concatenate([solid[:, lo : lo + part].astype(F32), jnp.zeros((8 - solid.shape[0], part), F32)], 0).T
        fluid = [jnp.broadcast_to(marks[:, b * LANES // width : b * LANES // width + 1] == 0.0, (part, LANES)) for b in range(halves)]
        for p in range(planes):
            left = jnp.concatenate(
                [
                    c,
                    both[0, p : p + 1, lo : lo + part],
                    both[1, p : p + 1, lo : lo + part],
                    zh_ref[p : p + 1, lo : lo + part],
                    zh_ref[planes + p : planes + p + 1, lo : lo + part],
                    jnp.zeros((1, part), F32),
                ],
                0,
            )
            right = jnp.concatenate(
                [
                    moved[p : p + 1, :],
                    moved[planes + p : planes + p + 1, :],
                    moved[2 * planes + p : 2 * planes + p + 1, :],
                    y,
                    jnp.zeros((1, cols), F32),
                ],
                0,
            )
            lh = left.astype(BF16).astype(F32)
            rh = right.astype(BF16).astype(F32)
            lc = jnp.concatenate([lh, lh, left - lh], 0).astype(BF16)
            rc = jnp.concatenate([rh, right - rh, rh], 0).astype(BF16)
            value = w_ref[p, lo : lo + part, :] + bf16_dot(lc, rc, ((0,), (0,)))
            for b in range(halves):
                value_ref[b, p] = jnp.where(fluid[b], value[:, b * LANES : (b + 1) * LANES], 0.0)
        for b in range(halves):
            for g in range(part // planes):
                turned = jnp.swapaxes(value_ref[b, :, g * planes : (g + 1) * planes, :], 0, 1)
                at = (lo + g * planes) * planes
                out_ref[b, at : at + planes * planes, :] = turned.reshape(planes * planes, LANES)
        for b in range(halves):
            out_copy(k, b).start()
    for k in range(steps):
        for b in range(halves):
            out_copy(k, b).wait()


def finish(xrows, yrows, moved, solid, zh, w, received):
    count = len(received)
    height = received[0].shape[0]
    planes, rows, cols = w.shape
    part, halves = 128, cols // 128
    out = call(
        functools.partial(finish_kernel, count, part),
        struct(rows * planes, cols),
        [VMEM] * (6 + count),
        12,
        out_specs=HBM,
        scratch=[
            pltpu.VMEM((count, height, rows), F32),
            pltpu.VMEM((count, planes, rows), F32),
            pltpu.VMEM((2, planes, rows), F32),
            pltpu.VMEM((halves, planes, part, LANES), F32),
            pltpu.VMEM((halves, rows * planes, 128), F32),
            pltpu.SemaphoreType.DMA((rows // part, halves)),
        ],
    )(xrows, yrows, moved, solid, zh, w, *received)
    return out.reshape(rows, planes, cols)


def rotate(value, axis, shift):
    count = lax.axis_size(axis)
    return lax.ppermute(value, axis, [(i, (i + shift) % count) for i in range(count)])


def on_device(
    velocity,
    lower_x,
    upper_x,
    lower_carry_x,
    upper_carry_x,
    lower_y,
    upper_y,
    lower_carry_y,
    upper_carry_y,
    wall_force,
    wall_owner,
    wall_offset,
    solid_mask,
):
    rows, planes, cols = velocity.shape
    walls = wall_force.shape[0]
    n_x, n_y = lax.axis_size("gx"), lax.axis_size("gy")
    room = 2 * walls // n_y
    owner = wall_owner[:, 0]
    packed = pack(owner, wall_offset, wall_force, velocity, n_y, room)
    payload = [packed[0]] + [rotate(packed[s], "gy", s) for s in range(1, n_y)]
    table = jnp.concatenate([v[-1, 0, :room] for v in payload]).astype(jnp.int32)
    mx, my, aux, my_t, aux_t, xrows, yrows, frows, scal = factors(
        lower_x, upper_x, lower_carry_x, upper_carry_x, lower_y, upper_y, lower_carry_y, upper_carry_y
    )
    func = frows[0:2]
    high, low, sv, edge = velocity_part(func, my_t, aux_t, velocity)
    mine = x_edges(table, func, edge, frows, scal, payload, room)
    other = lax.ppermute(mine, "gx", [(i, i ^ 1) for i in range(n_x)])
    both = pair(mine, other)
    received = [both] + [rotate(both, "gx", 2 * s) for s in range(1, n_x // 2)]
    w, s_edge, zh = sweep(mx, my, aux, yrows, high, low, sv, payload, room)
    mine, moved = x_join(my, xrows, yrows, scal, s_edge, mine, other, received)
    received = [mine] + [rotate(mine, "gy", s) for s in range(1, n_y)]
    return finish(xrows, yrows, moved, solid_mask.T, zh, w, received)


def solution(mesh):
    placed = (
        P("gx", None, "gy"),
        P("gx", None),
        P("gx", None),
        P("gx"),
        P("gx"),
        P("gy", None),
        P("gy", None),
        P("gy"),
        P("gy"),
        P(("gx", "gy"), None, None),
        P(("gx", "gy"), None),
        P(("gx", "gy")),
        P("gx", "gy"),
    )
    return jax.shard_map(
        on_device, mesh=mesh, in_specs=placed, out_specs=P("gx", None, "gy"), check_vma=False
    )
```

```python
import functools

import jax
import jax.numpy as jnp
from jax import lax
from jax.experimental import pallas as pl
from jax.experimental.pallas import tpu as pltpu
from jax.sharding import PartitionSpec as P

F32 = jnp.float32
BF16 = jnp.bfloat16
HIGHEST = lax.Precision.HIGHEST
VMEM = pl.BlockSpec(memory_space=pltpu.VMEM)
SMEM = pl.BlockSpec(memory_space=pltpu.SMEM)
HBM = pl.BlockSpec(memory_space=pltpu.HBM)
LANES = 128


def f32_dot(left, right, dims):
    return lax.dot_general(left, right, (dims, ((), ())), precision=HIGHEST, preferred_element_type=F32)


def split(value):
    high = value.astype(BF16)
    return high, (value - high.astype(F32)).astype(BF16)


def left_of(value, axis):
    high, low = split(value)
    return jnp.concatenate([high, low, high], axis=axis)


def right_of(value, axis):
    high, low = split(value)
    return jnp.concatenate([high, high, low], axis=axis)


def bf16_dot(left, right, dims):
    return lax.dot_general(left, right, (dims, ((), ())), preferred_element_type=F32)


def params(vmem_mib, side_effects=False):
    return pltpu.CompilerParams(vmem_limit_bytes=vmem_mib << 20)


def pin(value):
    return pltpu.with_memory_space_constraint(value, pltpu.HBM)


def call(kernel, out_shape, in_specs, vmem_mib, out_specs=None, scratch=(), flops=0, moved=0, **more):
    if out_specs is None:
        out_specs = jax.tree.map(lambda _: VMEM, out_shape)
    return pl.pallas_call(
        kernel,
        out_shape=out_shape,
        in_specs=in_specs,
        out_specs=out_specs,
        scratch_shapes=list(scratch),
        compiler_params=params(vmem_mib),
        cost_estimate=pl.CostEstimate(flops=flops, bytes_accessed=moved, transcendentals=0),
        **more,
    )


def struct(*shape, dtype=F32):
    return jax.ShapeDtypeStruct(shape, dtype)


def sort_walls(count, room, me, walls, owner_ref, table, taken):
    for shift in range(count):
        taken[shift] = shift * room

    def step(entry, carry):
        shift = owner_ref[entry] - me
        shift = jnp.where(shift < 0, shift + count, shift)
        slot = taken[shift]
        taken[shift] = slot + 1
        table[slot] = entry
        return carry

    lax.fori_loop(0, walls, step, 0, unroll=8)


def pack_kernel(count, room, owner_ref, offset_ref, force_hbm, *refs):
    outs, (force_ref, table, taken, sem) = refs[:count], refs[count:]
    walls = force_hbm.shape[0]
    planes, width = force_hbm.shape[1:]
    me = lax.axis_index("gy")
    copy = pltpu.make_async_copy(force_hbm, force_ref.at[pl.ds(0, walls)], sem)
    copy.start()
    force_ref[walls] = jnp.zeros(force_ref.shape[1:], F32)
    for slot in range(count * room):
        table[slot] = walls
    sort_walls(count, room, me, walls, owner_ref, table, taken)
    copy.wait()
    lane = lax.broadcasted_iota(jnp.int32, (planes, LANES), 1)
    for shift in list(range(1, count)) + [0]:
        places = jnp.full((planes, LANES), -1, jnp.int32)
        for slot in range(room):
            entry = table[shift * room + slot]
            outs[shift][slot] = force_ref[entry]
            place = jnp.where(entry < walls, offset_ref[jnp.minimum(entry, walls - 1)], -1)
            places = jnp.where(lane == slot, place, places)
        outs[shift][room] = places.astype(F32)


def pack(owner, offset, force, count, room):
    walls, planes, width = force.shape
    return call(
        functools.partial(pack_kernel, count, room),
        [struct(room + 1, planes, width) for s in range(count)],
        [SMEM, SMEM, HBM],
        8,
        scratch=[
            pltpu.VMEM((walls + 1, planes, width), F32),
            pltpu.SMEM((count * room,), jnp.int32),
            pltpu.SMEM((count,), jnp.int32),
            pltpu.SemaphoreType.DMA,
        ],
    )(pin(owner), pin(offset), pin(force))


def row(ref, index):
    base = index // 8 * 8
    return ref[base : base + 8, :][index - base : index - base + 1]


def half_shift_lanes(value):
    length = value.shape[1]
    at = lax.broadcasted_iota(jnp.int32, value.shape, 1)
    before = jnp.where(at == 0, 0.0, pltpu.roll(value, 1, 1))
    after = jnp.where(at == length - 1, 0.0, pltpu.roll(value, length - 1, 1))
    return 0.5 * (before + after)


def half_shift_rows(value):
    length = value.shape[0]
    at = lax.broadcasted_iota(jnp.int32, value.shape, 0)
    before = jnp.where(at == 0, 0.0, pltpu.roll(value, 1, 0))
    after = jnp.where(at == length - 1, 0.0, pltpu.roll(value, length - 1, 0))
    return 0.5 * (before + after)


def factor_kernel(chunk, v_hbm, *refs):
    given, (mx, my, aux, my_t, aux_t, xrows, yrows, frows, scal) = refs[:8], refs[8:17]
    v_ref, edge_ref, first_ref, last_ref = refs[17:21]
    fetched, (weight, sem, v_sem, weight_sem) = refs[21:29], refs[29:]
    rows, planes, cols = v_ref.shape
    copies = [pltpu.make_async_copy(given[i], fetched[i], sem.at[i]) for i in range(8)]
    for copy in copies:
        copy.start()

    def v_copy(k):
        span = pl.ds(k * chunk, chunk)
        return pltpu.make_async_copy(v_hbm.at[span], v_ref.at[span], v_sem.at[k])

    for k in range(rows // chunk):
        v_copy(k).start()
    for copy in copies:
        copy.wait()
    lx, ux, lcx, ucx, ly, uy, lcy, ucy = fetched
    rows_x, rows_y = lx.shape[0], ly.shape[0]
    both = f32_dot(ux[...], lx[...], ((1,), (0,)))
    zero = jnp.zeros((1, rows_x), F32)
    frows[...] = jnp.concatenate([row(lx, rows_x - 1), both[0:8][0:1], zero, zero, zero, zero, zero, zero], 0)
    to_scalars = pltpu.make_async_copy(frows, weight, weight_sem)
    to_scalars.start()
    mx[...] = left_of(half_shift_rows(both), 1)
    both_y = f32_dot(uy[...], ly[...], ((1,), (0,)))
    turned = both_y.T
    my[...] = left_of(turned, 0)
    my_t[...] = left_of(half_shift_rows(turned), 0)
    lc, uc = lcx[...], ucx[...]
    pad = jnp.zeros((7, rows_x), F32)
    u_lc = f32_dot(jnp.concatenate([lc, pad], 0), ux[...], ((1,), (1,)))[0:1]
    at = lax.broadcasted_iota(jnp.int32, (1, rows_x), 1)
    c0 = half_shift_lanes(u_lc)
    c1 = half_shift_lanes(uc) + jnp.where(at == rows_x - 1, 0.5, 0.0)
    c2 = jnp.where(at == 0, 0.5, 0.0)
    xrows[...] = jnp.concatenate([c0, c1, c2, zero, zero, zero, zero, zero], 0)
    lcv, ucv = lcy[...], ucy[...]
    pad_y = jnp.zeros((7, rows_y), F32)
    uy_lc = f32_dot(jnp.concatenate([lcv, pad_y], 0), uy[...], ((1,), (1,)))[0:1]
    f0 = row(ly, rows_y - 1)
    f1 = both_y[0:8][0:1]
    zero_y = jnp.zeros((1, rows_y), F32)
    m0, m1 = 0.5 * turned[0:8][0:1], 0.5 * turned[rows_y - 8 : rows_y][7:8]
    yrows[...] = jnp.concatenate([uy_lc, ucv, m0, m1, f0, f1, zero_y, zero_y], 0)
    lane_y = lax.broadcasted_iota(jnp.int32, (rows_y, 128), 1)
    pair_of = jnp.concatenate([f0, f1, pad_y[:6]], 0).T
    spread_cols = jnp.where(lane_y < 64, pair_of[:, 0:1], pair_of[:, 1:2])
    aux[...] = left_of(spread_cols, 0)
    aux_t[...] = left_of(half_shift_rows(spread_cols), 0)

    def spread(value, index, width):
        return jnp.broadcast_to(value[:, index : index + 1], (1, width))

    last = row(ux, rows_x - 1)
    scal[0:8, :] = jnp.concatenate(
        [
            spread(lc, rows_x - 1, rows_x),
            spread(u_lc, 0, rows_x),
            spread(uc, 0, rows_x),
            spread(last, rows_x - 1, rows_x),
            spread(uc, rows_x - 1, rows_x),
            zero,
            zero,
            zero,
        ],
        0,
    )
    scal[8:16, :] = jnp.concatenate(
        [
            spread(lcv, rows_y - 1, rows_x),
            spread(uy_lc, 0, rows_x),
            spread(ucv, 0, rows_x),
            zero,
            zero,
            zero,
            zero,
            zero,
        ],
        0,
    )


    to_scalars.wait()
    lane = lax.broadcasted_iota(jnp.int32, (planes, LANES), 1)
    lower, upper = jnp.zeros((planes, cols), F32), jnp.zeros((planes, cols), F32)
    for block in range(rows // LANES):
        first, last = jnp.zeros((planes, LANES), F32), jnp.zeros((planes, LANES), F32)
        for x in range(LANES):
            at = block * LANES + x
            if at % chunk == 0:
                v_copy(at // chunk).wait()
            value = v_ref[at]
            lower = lower + weight[0, at] * value
            upper = upper + weight[1, at] * value
            first = jnp.where(lane == x, pltpu.roll(value[:, 0:LANES], x, 1), first)
            last = jnp.where(lane == x, pltpu.roll(value[:, cols - LANES : cols], (x + 1) % LANES, 1), last)
        first_ref[:, block * LANES : (block + 1) * LANES] = first
        last_ref[:, block * LANES : (block + 1) * LANES] = last
    edge_ref[0] = half_shift_lanes(lower)
    edge_ref[1] = half_shift_lanes(upper)


def factors(velocity, lx, ux, lcx, ucx, ly, uy, lcy, ucy):
    rows, planes, cols = velocity.shape
    chunk = 64
    given = (lx, ux, lcx[None, :], ucx[None, :], ly, uy, lcy[None, :], ucy[None, :])
    return call(
        functools.partial(factor_kernel, chunk),
        [
            struct(rows, 3 * rows, dtype=BF16),
            struct(3 * cols, cols, dtype=BF16),
            struct(3 * cols, 128, dtype=BF16),
            struct(3 * cols, cols, dtype=BF16),
            struct(3 * cols, 128, dtype=BF16),
            struct(8, rows),
            struct(8, cols),
            struct(8, rows),
            struct(16, rows),
            struct(rows, planes, cols),
            struct(2, planes, cols),
            struct(planes, rows),
            struct(planes, rows),
        ],
        [HBM] * 9,
        8,
        scratch=[pltpu.VMEM(g.shape, F32) for g in given]
        + [
            pltpu.SMEM((8, rows), F32),
            pltpu.SemaphoreType.DMA((8,)),
            pltpu.SemaphoreType.DMA((rows // chunk,)),
            pltpu.SemaphoreType.DMA,
        ],
    )(pin(velocity), *[pin(g) for g in given])


def velocity_kernel(chunk, mx, my_t, aux_t, v_ref, w_ref, s_ref, high_ref, low_ref):
    rows, planes, cols = v_ref.shape
    group = planes
    lane = lax.broadcasted_iota(jnp.int32, (group, LANES), 1)
    for k in range(rows // chunk):
        flat = right_of(v_ref[k * chunk : (k + 1) * chunk].reshape(chunk * planes, cols), 1)
        r = bf16_dot(flat, my_t[...], ((1,), (0,)))
        t = bf16_dot(flat, aux_t[...], ((1,), (0,)))
        for g in range(chunk // group):
            here = slice(g * group * planes, (g + 1) * group * planes)
            x = slice(k * chunk + g * group, k * chunk + (g + 1) * group)
            turned = jnp.swapaxes(r[here].reshape(group, planes, cols), 0, 1)
            high, low = split(turned)
            high_ref[:, x, :] = high
            low_ref[:, x, :] = low
            picked = jnp.swapaxes(t[here].reshape(group, planes, LANES), 0, 1)
            total = jnp.zeros((group, LANES), F32)
            for p in range(planes):
                total = jnp.where((lane == p) | (lane == 64 + p), picked[p], total)
            s_ref[x, :] = total
    for p in range(planes):
        high = high_ref[p]
        w_ref[p] = bf16_dot(mx[...], jnp.concatenate([high, high, low_ref[p]], 0), ((1,), (0,)))


def velocity_part(mx, my_t, aux_t, velocity):
    rows, planes, cols = velocity.shape
    return call(
        functools.partial(velocity_kernel, 64),
        [struct(planes, rows, cols), struct(rows, LANES)],
        [VMEM] * 4,
        16,
        scratch=[pltpu.VMEM((planes, rows, cols), BF16), pltpu.VMEM((planes, rows, cols), BF16)],
    )(mx, my_t, aux_t, velocity)


def halos(count, left_ref, right_ref):
    me = lax.axis_index("gy")
    return jnp.where(me > 0, left_ref[...], 0.0), jnp.where(me < count - 1, right_ref[...], 0.0)


def x_edge_kernel(count, room, edge_ref, frows, scal, left_ref, right_ref, *refs):
    payload, (out, chosen_ref, wall_ref) = refs[:count], refs[count:]
    planes, slots, cols = wall_ref.shape
    rows = frows.shape[1]
    width = payload[0].shape[2]
    nblock = cols // width
    lane8 = lax.broadcasted_iota(jnp.int32, (8, slots), 1)
    places = jnp.full((8, slots), -1.0, F32)
    for s in range(count):
        here = payload[s][room][0:8]
        if s:
            here = pltpu.roll(here, s * room, 1)
        places = jnp.where((lane8 >= s * room) & (lane8 < (s + 1) * room), here, places)
    line = jnp.floor(places * (1.0 / nblock))
    half = places - nblock * line
    row_ids = lax.broadcasted_iota(jnp.int32, (rows, slots), 0).astype(F32)
    chosen = jnp.where(row_ids == line[0:1], 1.0, 0.0)
    chosen_ref[...] = chosen.astype(BF16)
    weight = f32_dot(frows[...], chosen, ((1,), (0,)))
    sub8 = lax.broadcasted_iota(jnp.int32, (8, slots), 0)
    column = jnp.where(sub8 == 2, half, weight).T
    step = min(room, 16)
    for s in range(count):
        for g in range(room // step):
            at = slice(s * room + g * step, s * room + (g + 1) * step)
            value = jnp.swapaxes(payload[s][g * step : (g + 1) * step], 0, 1)
            for b in range(nblock):
                keep = jnp.broadcast_to(column[at, 2:3] == b, (step, width))
                wall_ref[:, at, b * width : (b + 1) * width] = jnp.where(keep[None], value, 0.0)
    at = lax.broadcasted_iota(jnp.int32, (planes, cols), 1)
    hl, hr = halos(count, left_ref, right_ref)
    for f in range(2):
        func = frows[f : f + 1, :]
        first = 0.5 * jnp.sum(hl * func, axis=1, keepdims=True)
        last = 0.5 * jnp.sum(hr * func, axis=1, keepdims=True)
        out[f * planes : (f + 1) * planes, :] = (
            edge_ref[f] + jnp.where(at == 0, first, 0.0) + jnp.where(at == cols - 1, last, 0.0)
        )
    spread = [jnp.broadcast_to(column[:, f : f + 1], (slots, LANES)) for f in range(2)]
    for p in range(planes):
        for b in range(cols // LANES):
            lanes = slice(b * LANES, (b + 1) * LANES)
            value = wall_ref[p, :, lanes]
            for f in range(2):
                at = f * planes + p
                out[at : at + 1, lanes] = out[at : at + 1, lanes] + jnp.sum(value * spread[f], axis=0, keepdims=True)
    out[2 * planes : 2 * planes + 8, :] = scal[0:8, :]


def x_edges(edge, frows, scal, left, right, payload, room):
    planes, cols = edge.shape[1:]
    count, rows = len(payload), frows.shape[1]
    slots = count * room
    return call(
        functools.partial(x_edge_kernel, count, room),
        [struct(2 * planes + 8, cols), struct(rows, slots, dtype=BF16), struct(planes, slots, cols)],
        [VMEM] * (5 + count),
        8,
    )(edge, frows, scal, left, right, *payload)


def wall_kernel(count, mx, aux, yrows, sv_ref, left_ref, right_ref, chosen_ref, wall_ref, s_ref, zh_ref, sel_ref):
    planes, slots, cols = wall_ref.shape
    rows = mx.shape[0]
    hl, hr = halos(count, left_ref, right_ref)
    m = mx[...]
    zh = bf16_dot(right_of(jnp.concatenate([hl, hr], 0), 1), m, ((1,), (1,)))
    zh_ref[...] = zh
    chosen = chosen_ref[...]
    sel_high = bf16_dot(m[:, 0:rows], chosen, ((1,), (0,))).astype(BF16)
    sel_low = bf16_dot(m[:, rows : 2 * rows], chosen, ((1,), (0,))).astype(BF16)
    sel = jnp.concatenate([sel_high, sel_low, sel_high], 1)
    sel_ref[...] = sel
    lane = lax.broadcasted_iota(jnp.int32, (slots, LANES), 1)
    total = jnp.zeros((slots, LANES), F32)
    some = 8
    for q in range(0, planes, some):
        flat = wall_ref[q : q + some].reshape(some * slots, cols)
        t = bf16_dot(right_of(flat, 1), aux[...], ((1,), (0,)))
        for i in range(some):
            p = q + i
            total = jnp.where((lane == p) | (lane == 64 + p), t[i * slots : (i + 1) * slots], total)
    left = jnp.concatenate([m, sel], 1)
    turned = bf16_dot(left, jnp.concatenate([right_of(sv_ref[...], 0), right_of(total, 0)], 0), ((1,), (0,))).T
    low, high = turned[0:planes], turned[64 : 64 + planes]
    f0, f1 = yrows[4:5, :], yrows[5:6, :]
    zl, zr = zh[0:planes], zh[planes : 2 * planes]
    s_ref[0:planes, :] = low + 0.5 * (zl * f0[:, 0:1] + zr * f0[:, cols - 1 : cols])
    s_ref[planes : 2 * planes, :] = high + 0.5 * (zl * f1[:, 0:1] + zr * f1[:, cols - 1 : cols])


def wall_edges(count, mx, aux, yrows, sv, left, right, chosen, wall):
    rows = mx.shape[0]
    planes, slots, cols = wall.shape
    return call(
        functools.partial(wall_kernel, count),
        [struct(2 * planes, rows), struct(2 * planes, rows), struct(rows, 3 * slots, dtype=BF16)],
        [VMEM] * 8,
        8,
    )(mx, aux, yrows, sv, left, right, chosen, wall)


def wall_sweep_kernel(my, sel, wall_ref, v_ref, w_ref):
    planes, slots, cols = wall_ref.shape
    some = 8
    for q in range(0, planes, some):
        flat = wall_ref[q : q + some].reshape(some * slots, cols)
        r = bf16_dot(right_of(flat, 1), my[...], ((1,), (0,)))
        for i in range(some):
            here = right_of(r[i * slots : (i + 1) * slots], 0)
            w_ref[q + i] = v_ref[q + i] + bf16_dot(sel[...], here, ((1,), (0,)))


def wall_sweep(my, sel, wall, w):
    return call(
        wall_sweep_kernel,
        struct(*w.shape),
        [VMEM] * 4,
        8,
        input_output_aliases={3: 0},
    )(my, sel, wall, w)


def chain(parts, count, me, planes, f_in):
    lanes = parts.shape[2]
    zero = jnp.zeros((planes, lanes), F32)
    f, mine_f = zero, zero
    for k in range(count):
        f_in[k] = f
        mine_f = jnp.where(k == me, f, mine_f)
        f = parts[k, 0:planes, :] + parts[k, 2 * planes : 2 * planes + 1, :] * f
    g, mine_g = zero, zero
    for k in range(count - 1, -1, -1):
        scal = parts[k, 2 * planes : 2 * planes + 8, :]
        mine_g = jnp.where(k == me, g, mine_g)
        g = parts[k, planes : 2 * planes, :] + scal[1:2] * f_in[k] + scal[2:3] * g
    return mine_f, mine_g


def pair_kernel(mine, other, out):
    planes = (mine.shape[0] - 8) // 2
    odd = lax.rem(lax.axis_index("gx"), 2) == 1
    left = jnp.where(odd, other[...], mine[...])
    right = jnp.where(odd, mine[...], other[...])
    out[...] = joined(left, right, planes)


def joined(left, right, planes):
    a, b, s = left[0:planes], left[planes : 2 * planes], left[2 * planes :]
    c, d, t = right[0:planes], right[planes : 2 * planes], right[2 * planes :]
    l0, c0, u0 = s[0:1], s[1:2], s[2:3]
    l1, c1, u1 = t[0:1], t[1:2], t[2:3]
    return jnp.concatenate(
        [c + l1 * a, b + u0 * (d + c1 * a), l0 * l1, c0 + u0 * c1 * l0, u0 * u1, t[3:8]],
        0,
    )


def pair(mine, other):
    return call(pair_kernel, struct(*mine.shape), [VMEM, VMEM], 8)(mine, other)


def gather_parts(me, parts, received):
    count = len(received)
    for shift in range(count):
        parts[pl.ds(lax.rem(me - shift + count, count), 1)] = received[shift][...][None]


def x_join_kernel(count, my, xrows, yrows, scal, s_ref, mine_ref, other_ref, *refs):
    received, (out, moved, parts, f_in) = refs[:count], refs[count:]
    me = lax.axis_index("gx")
    place = lax.div(me, 2)
    odd = lax.rem(me, 2) == 1
    planes = s_ref.shape[0] // 2
    gather_parts(place, parts, received)
    f, g = chain(parts, count, place, planes, f_in)
    mine, other = mine_ref[...], other_ref[...]
    left, right = jnp.where(odd, other, mine), jnp.where(odd, mine, other)
    a, ls = left[0:planes], left[2 * planes :]
    d, rs = right[planes : 2 * planes], right[2 * planes :]
    f_mid = a + ls[0:1] * f
    g_mid = d + rs[1:2] * f_mid + rs[2:3] * g
    in_f, in_b = jnp.where(odd, f_mid, f), jnp.where(odd, g, g_mid)
    ms = mine[2 * planes :]
    first = mine[planes : 2 * planes] + ms[1:2] * in_f + ms[2:3] * in_b
    before_s = jnp.where(odd, ls, parts[jnp.maximum(place - 1, 0), 2 * planes : 2 * planes + 8, :])
    before = jnp.where(me > 0, before_s[3:4] * in_f + before_s[4:5] * first, 0.0)
    low, high = s_ref[0:planes, :], s_ref[planes : 2 * planes, :]
    f0, f1 = yrows[4:5, :], yrows[5:6, :]
    for index, value in enumerate((in_f, in_b, before)):
        c = xrows[index : index + 1, :]
        low = low + jnp.sum(value * f0, axis=1, keepdims=True) * c
        high = high + jnp.sum(value * f1, axis=1, keepdims=True) * c
    out[0:planes, :] = low
    out[planes : 2 * planes, :] = high
    out[2 * planes : 2 * planes + 8, :] = scal[8:16, :]
    moved[...] = bf16_dot(right_of(jnp.concatenate([in_f, in_b, before], 0), 1), my[...], ((1,), (0,)))


def x_join(my, xrows, yrows, scal, s, mine, other, received):
    count = len(received)
    height, cols = received[0].shape
    planes, rows = s.shape[0] // 2, s.shape[1]
    return call(
        functools.partial(x_join_kernel, count),
        [struct(2 * planes + 8, rows), struct(3 * planes, cols)],
        [VMEM] * (7 + count),
        8,
        scratch=[pltpu.VMEM((count, height, cols), F32), pltpu.VMEM((count, planes, cols), F32)],
    )(my, xrows, yrows, scal, s, mine, other, *received)


def finish_kernel(count, part, xrows, yrows, moved, solid, zh_ref, w_ref, *refs):
    received, (out_hbm, parts, f_in, both, value_ref, out_ref, out_sem) = refs[:count], refs[count:]
    me = lax.axis_index("gy")
    planes, rows, cols = w_ref.shape
    halves = out_ref.shape[0]

    piece = 32 * planes

    def out_copy(k, b):
        span = pl.ds(k * piece, piece)
        return pltpu.make_async_copy(out_ref.at[b, span, :], out_hbm.at[span, pl.ds(b * LANES, LANES)], out_sem.at[k, b])

    steps = rows // part
    gather_parts(me, parts, received)
    in_f, in_b = chain(parts, count, me, planes, f_in)
    both[0] = in_f
    both[1] = in_b
    y = yrows[0:4, :]
    width = cols // solid.shape[0]
    for k in range(steps):
        lo = k * part
        c = xrows[0:3, lo : lo + part]
        marks = jnp.concatenate([solid[:, lo : lo + part].astype(F32), jnp.zeros((8 - solid.shape[0], part), F32)], 0).T
        fluid = [jnp.broadcast_to(marks[:, b * LANES // width : b * LANES // width + 1] == 0.0, (part, LANES)) for b in range(halves)]
        for p in range(planes):
            left = jnp.concatenate(
                [
                    c,
                    both[0, p : p + 1, lo : lo + part],
                    both[1, p : p + 1, lo : lo + part],
                    zh_ref[p : p + 1, lo : lo + part],
                    zh_ref[planes + p : planes + p + 1, lo : lo + part],
                    jnp.zeros((1, part), F32),
                ],
                0,
            )
            right = jnp.concatenate(
                [
                    moved[p : p + 1, :],
                    moved[planes + p : planes + p + 1, :],
                    moved[2 * planes + p : 2 * planes + p + 1, :],
                    y,
                    jnp.zeros((1, cols), F32),
                ],
                0,
            )
            lh = left.astype(BF16).astype(F32)
            rh = right.astype(BF16).astype(F32)
            lc = jnp.concatenate([lh, lh, left - lh], 0).astype(BF16)
            rc = jnp.concatenate([rh, right - rh, rh], 0).astype(BF16)
            value = w_ref[p, lo : lo + part, :] + bf16_dot(lc, rc, ((0,), (0,)))
            for b in range(halves):
                value_ref[b, p] = jnp.where(fluid[b], value[:, b * LANES : (b + 1) * LANES], 0.0)
        for g in range(part // planes):
            at = (lo + g * planes) * planes
            for b in range(halves):
                turned = jnp.swapaxes(value_ref[b, :, g * planes : (g + 1) * planes, :], 0, 1)
                out_ref[b, at : at + planes * planes, :] = turned.reshape(planes * planes, LANES)
                if (at + planes * planes) % piece == 0:
                    out_copy(at // piece, b).start()
    for k in range(rows * planes // piece):
        for b in range(halves):
            out_copy(k, b).wait()


def finish(xrows, yrows, moved, solid, zh, w, received):
    count = len(received)
    height = received[0].shape[0]
    planes, rows, cols = w.shape
    part, halves = 128, cols // 128
    out = call(
        functools.partial(finish_kernel, count, part),
        struct(rows * planes, cols),
        [VMEM] * (6 + count),
        12,
        out_specs=HBM,
        scratch=[
            pltpu.VMEM((count, height, rows), F32),
            pltpu.VMEM((count, planes, rows), F32),
            pltpu.VMEM((2, planes, rows), F32),
            pltpu.VMEM((halves, planes, part, LANES), F32),
            pltpu.VMEM((halves, rows * planes, 128), F32),
            pltpu.SemaphoreType.DMA((rows // 32, halves)),
        ],
    )(xrows, yrows, moved, solid, zh, w, *received)
    return out.reshape(rows, planes, cols)


def rotate(value, axis, shift):
    count = lax.axis_size(axis)
    return lax.ppermute(value, axis, [(i, (i + shift) % count) for i in range(count)])


def on_device(
    velocity,
    lower_x,
    upper_x,
    lower_carry_x,
    upper_carry_x,
    lower_y,
    upper_y,
    lower_carry_y,
    upper_carry_y,
    wall_force,
    wall_owner,
    wall_offset,
    solid_mask,
):
    rows, planes, cols = velocity.shape
    walls = wall_force.shape[0]
    n_x, n_y = lax.axis_size("gx"), lax.axis_size("gy")
    room = 2 * walls // n_y
    packed = pack(wall_owner[:, 0], wall_offset, wall_force, n_y, room)
    payload = [packed[0]] + [rotate(packed[s], "gy", s) for s in range(1, n_y)]
    mx, my, aux, my_t, aux_t, xrows, yrows, frows, scal, v, edge, first, last = factors(
        velocity,
        lower_x,
        upper_x,
        lower_carry_x,
        upper_carry_x,
        lower_y,
        upper_y,
        lower_carry_y,
        upper_carry_y,
    )
    left, right = rotate(last, "gy", 1), rotate(first, "gy", -1)
    w, sv = velocity_part(mx, my_t, aux_t, v)
    w, sv, edge = lax.optimization_barrier((w, sv, edge))
    mine, chosen, wall = x_edges(edge, frows, scal, left, right, payload, room)
    other = lax.ppermute(mine, "gx", [(i, i ^ 1) for i in range(n_x)])
    both = pair(mine, other)
    received = [both] + [rotate(both, "gx", 2 * s) for s in range(1, n_x // 2)]
    s_edge, zh, sel = wall_edges(n_y, mx, aux, yrows, sv, left, right, chosen, wall)
    mine, moved = x_join(my, xrows, yrows, scal, s_edge, mine, other, received)
    received = [mine] + [rotate(mine, "gy", s) for s in range(1, n_y)]
    w = wall_sweep(my, sel, wall, w)
    return finish(xrows, yrows, moved, solid_mask.T, zh, w, received)


def solution(mesh):
    placed = (
        P("gx", None, "gy"),
        P("gx", None),
        P("gx", None),
        P("gx"),
        P("gx"),
        P("gy", None),
        P("gy", None),
        P("gy"),
        P("gy"),
        P(("gx", "gy"), None, None),
        P(("gx", "gy"), None),
        P(("gx", "gy")),
        P("gx", "gy"),
    )
    return jax.shard_map(
        on_device, mesh=mesh, in_specs=placed, out_specs=P("gx", None, "gy"), check_vma=False
    )
```

```python
import functools

import jax
import jax.numpy as jnp
from jax import lax
from jax.experimental import pallas as pl
from jax.experimental.pallas import tpu as pltpu
from jax.sharding import PartitionSpec as P

F32 = jnp.float32
BF16 = jnp.bfloat16
HIGHEST = lax.Precision.HIGHEST
VMEM = pl.BlockSpec(memory_space=pltpu.VMEM)
SMEM = pl.BlockSpec(memory_space=pltpu.SMEM)
HBM = pl.BlockSpec(memory_space=pltpu.HBM)
LANES = 128
GROUP = 4


def f32_dot(left, right, dims):
    return lax.dot_general(left, right, (dims, ((), ())), precision=HIGHEST, preferred_element_type=F32)


def split(value):
    high = value.astype(BF16)
    return high, (value - high.astype(F32)).astype(BF16)


def left_of(value, axis):
    high, low = split(value)
    return jnp.concatenate([high, low, high], axis=axis)


def right_of(value, axis):
    high, low = split(value)
    return jnp.concatenate([high, high, low], axis=axis)


def bf16_dot(left, right, dims):
    return lax.dot_general(left, right, (dims, ((), ())), preferred_element_type=F32)


def params(vmem_mib, side_effects=False):
    return pltpu.CompilerParams(vmem_limit_bytes=vmem_mib << 20)


def pin(value):
    return pltpu.with_memory_space_constraint(value, pltpu.HBM)


def call(kernel, out_shape, in_specs, vmem_mib, out_specs=None, scratch=(), flops=0, moved=0, **more):
    if out_specs is None:
        out_specs = jax.tree.map(lambda _: VMEM, out_shape)
    return pl.pallas_call(
        kernel,
        out_shape=out_shape,
        in_specs=in_specs,
        out_specs=out_specs,
        scratch_shapes=list(scratch),
        compiler_params=params(vmem_mib),
        cost_estimate=pl.CostEstimate(flops=flops, bytes_accessed=moved, transcendentals=0),
        **more,
    )


def struct(*shape, dtype=F32):
    return jax.ShapeDtypeStruct(shape, dtype)


def sort_walls(count, room, me, walls, owner_ref, table, taken):
    for shift in range(count):
        taken[shift] = shift * room

    def step(entry, carry):
        shift = owner_ref[entry] - me
        shift = jnp.where(shift < 0, shift + count, shift)
        slot = taken[shift]
        taken[shift] = slot + 1
        table[slot] = entry
        return carry

    lax.fori_loop(0, walls, step, 0, unroll=8)


def pack_kernel(count, room, owner_ref, offset_ref, force_hbm, *refs):
    outs, (force_ref, table, taken, sem) = refs[:count], refs[count:]
    walls = force_hbm.shape[0]
    planes, width = force_hbm.shape[1:]
    me = lax.axis_index("gy")
    copy = pltpu.make_async_copy(force_hbm, force_ref.at[pl.ds(0, walls)], sem)
    copy.start()
    force_ref[walls] = jnp.zeros(force_ref.shape[1:], F32)
    for slot in range(count * room):
        table[slot] = walls
    sort_walls(count, room, me, walls, owner_ref, table, taken)
    copy.wait()
    lane = lax.broadcasted_iota(jnp.int32, (planes, LANES), 1)
    for shift in list(range(1, count)) + [0]:
        places = jnp.full((planes, LANES), -1, jnp.int32)
        for slot in range(room):
            entry = table[shift * room + slot]
            outs[shift][slot] = force_ref[entry]
            place = jnp.where(entry < walls, offset_ref[jnp.minimum(entry, walls - 1)], -1)
            places = jnp.where(lane == slot, place, places)
        outs[shift][room] = places.astype(F32)


def pack(owner, offset, force, count, room):
    walls, planes, width = force.shape
    return call(
        functools.partial(pack_kernel, count, room),
        [struct(room + 1, planes, width) for s in range(count)],
        [SMEM, SMEM, HBM],
        8,
        scratch=[
            pltpu.VMEM((walls + 1, planes, width), F32),
            pltpu.SMEM((count * room,), jnp.int32),
            pltpu.SMEM((count,), jnp.int32),
            pltpu.SemaphoreType.DMA,
        ],
    )(pin(owner), pin(offset), pin(force))


def row(ref, index):
    base = index // 8 * 8
    return ref[base : base + 8, :][index - base : index - base + 1]


def half_shift_lanes(value):
    length = value.shape[1]
    at = lax.broadcasted_iota(jnp.int32, value.shape, 1)
    before = jnp.where(at == 0, 0.0, pltpu.roll(value, 1, 1))
    after = jnp.where(at == length - 1, 0.0, pltpu.roll(value, length - 1, 1))
    return 0.5 * (before + after)


def half_shift_rows(value):
    length = value.shape[0]
    at = lax.broadcasted_iota(jnp.int32, value.shape, 0)
    before = jnp.where(at == 0, 0.0, pltpu.roll(value, 1, 0))
    after = jnp.where(at == length - 1, 0.0, pltpu.roll(value, length - 1, 0))
    return 0.5 * (before + after)


def factor_kernel(v_hbm, *refs):
    given, (mx, my, aux, my_t, aux_t, xrows, yrows, frows, scal) = refs[:8], refs[8:17]
    v_ref, edge_ref, first_ref, last_ref = refs[17:21]
    fetched, (sem, v_sem) = refs[21:29], refs[29:]
    planes, rows, cols = v_ref.shape
    copies = [pltpu.make_async_copy(given[i], fetched[i], sem.at[i]) for i in range(8)]
    for copy in copies:
        copy.start()

    def v_copy(p):
        return pltpu.make_async_copy(v_hbm.at[:, p, :], v_ref.at[p], v_sem.at[p])

    for p in range(planes):
        v_copy(p).start()
    for copy in copies:
        copy.wait()
    lx, ux, lcx, ucx, ly, uy, lcy, ucy = fetched
    rows_x, rows_y = lx.shape[0], ly.shape[0]
    both = f32_dot(ux[...], lx[...], ((1,), (0,)))
    zero = jnp.zeros((1, rows_x), F32)
    frows[...] = jnp.concatenate([row(lx, rows_x - 1), both[0:8][0:1], zero, zero, zero, zero, zero, zero], 0)
    mx[...] = left_of(half_shift_rows(both), 1)
    both_y = f32_dot(uy[...], ly[...], ((1,), (0,)))
    turned = both_y.T
    my[...] = left_of(turned, 0)
    my_t[...] = left_of(half_shift_rows(turned), 0)
    lc, uc = lcx[...], ucx[...]
    pad = jnp.zeros((7, rows_x), F32)
    u_lc = f32_dot(jnp.concatenate([lc, pad], 0), ux[...], ((1,), (1,)))[0:1]
    at = lax.broadcasted_iota(jnp.int32, (1, rows_x), 1)
    c0 = half_shift_lanes(u_lc)
    c1 = half_shift_lanes(uc) + jnp.where(at == rows_x - 1, 0.5, 0.0)
    c2 = jnp.where(at == 0, 0.5, 0.0)
    xrows[...] = jnp.concatenate([c0, c1, c2, zero, zero, zero, zero, zero], 0)
    lcv, ucv = lcy[...], ucy[...]
    pad_y = jnp.zeros((7, rows_y), F32)
    uy_lc = f32_dot(jnp.concatenate([lcv, pad_y], 0), uy[...], ((1,), (1,)))[0:1]
    f0 = row(ly, rows_y - 1)
    f1 = both_y[0:8][0:1]
    zero_y = jnp.zeros((1, rows_y), F32)
    m0, m1 = 0.5 * turned[0:8][0:1], 0.5 * turned[rows_y - 8 : rows_y][7:8]
    yrows[...] = jnp.concatenate([uy_lc, ucv, m0, m1, f0, f1, zero_y, zero_y], 0)
    lane_y = lax.broadcasted_iota(jnp.int32, (rows_y, 128), 1)
    pair_of = jnp.concatenate([f0, f1, pad_y[:6]], 0).T
    spread_cols = jnp.where(lane_y < 64, pair_of[:, 0:1], pair_of[:, 1:2])
    aux[...] = left_of(spread_cols, 0)
    aux_t[...] = left_of(half_shift_rows(spread_cols), 0)

    def spread(value, index, width):
        return jnp.broadcast_to(value[:, index : index + 1], (1, width))

    last = row(ux, rows_x - 1)
    scal[0:8, :] = jnp.concatenate(
        [
            spread(lc, rows_x - 1, rows_x),
            spread(u_lc, 0, rows_x),
            spread(uc, 0, rows_x),
            spread(last, rows_x - 1, rows_x),
            spread(uc, rows_x - 1, rows_x),
            zero,
            zero,
            zero,
        ],
        0,
    )
    scal[8:16, :] = jnp.concatenate(
        [
            spread(lcv, rows_y - 1, rows_x),
            spread(uy_lc, 0, rows_x),
            spread(ucv, 0, rows_x),
            zero,
            zero,
            zero,
            zero,
            zero,
        ],
        0,
    )


    column = frows[...].T
    weights = [jnp.broadcast_to(column[:, f : f + 1], (rows, LANES)) for f in range(2)]
    lane = lax.broadcasted_iota(jnp.int32, (rows, LANES), 1)
    ends = jnp.zeros((rows, LANES), F32)
    for p in range(planes):
        if p % GROUP == 0:
            for here in range(p, p + GROUP):
                v_copy(here).wait()
        for b in range(cols // LANES):
            lanes = slice(b * LANES, (b + 1) * LANES)
            value = v_ref[p, :, lanes]
            for f in range(2):
                edge_ref[f, p : p + 1, lanes] = jnp.sum(value * weights[f], axis=0, keepdims=True)
        ends = jnp.where(lane == p, pltpu.roll(v_ref[p, :, 0:LANES], p, 1), ends)
        to = planes + p
        ends = jnp.where(lane == to, pltpu.roll(v_ref[p, :, cols - LANES : cols], (to + 1) % LANES, 1), ends)
    for f in range(2):
        edge_ref[f] = half_shift_lanes(edge_ref[f])
    turned_ends = ends.T
    first_ref[...] = turned_ends[0:planes]
    last_ref[...] = turned_ends[planes : 2 * planes]


def factors(velocity, lx, ux, lcx, ucx, ly, uy, lcy, ucy):
    rows, planes, cols = velocity.shape
    given = (lx, ux, lcx[None, :], ucx[None, :], ly, uy, lcy[None, :], ucy[None, :])
    return call(
        factor_kernel,
        [
            struct(rows, 3 * rows, dtype=BF16),
            struct(3 * cols, cols, dtype=BF16),
            struct(3 * cols, 128, dtype=BF16),
            struct(3 * cols, cols, dtype=BF16),
            struct(3 * cols, 128, dtype=BF16),
            struct(8, rows),
            struct(8, cols),
            struct(8, rows),
            struct(16, rows),
            struct(planes, rows, cols),
            struct(2, planes, cols),
            struct(planes, rows),
            struct(planes, rows),
        ],
        [HBM] * 9,
        8,
        scratch=[pltpu.VMEM(g.shape, F32) for g in given]
        + [
            pltpu.SemaphoreType.DMA((8,)),
            pltpu.SemaphoreType.DMA((planes,)),
        ],
    )(pin(velocity), *[pin(g) for g in given])


def velocity_kernel(some, mx, my_t, aux_t, v_ref, w_ref, s_ref):
    planes, rows, cols = v_ref.shape
    lane = lax.broadcasted_iota(jnp.int32, (rows, LANES), 1)
    total = jnp.zeros((rows, LANES), F32)
    for q in range(0, planes, some):
        flat = right_of(v_ref[q : q + some].reshape(some * rows, cols), 1)
        r = bf16_dot(flat, my_t[...], ((1,), (0,)))
        t = bf16_dot(flat, aux_t[...], ((1,), (0,)))
        for i in range(some):
            p = q + i
            here = slice(i * rows, (i + 1) * rows)
            total = jnp.where((lane == p) | (lane == 64 + p), t[here], total)
            w_ref[p] = bf16_dot(mx[...], right_of(r[here], 0), ((1,), (0,)))
    s_ref[...] = total


def velocity_part(mx, my_t, aux_t, velocity):
    planes, rows, cols = velocity.shape
    return call(
        functools.partial(velocity_kernel, 4),
        [struct(planes, rows, cols), struct(rows, LANES)],
        [VMEM] * 4,
        16,
    )(mx, my_t, aux_t, velocity)


def halos(count, left_ref, right_ref):
    me = lax.axis_index("gy")
    return jnp.where(me > 0, left_ref[...], 0.0), jnp.where(me < count - 1, right_ref[...], 0.0)


def x_edge_kernel(count, room, edge_ref, frows, scal, left_ref, right_ref, *refs):
    payload, (out, chosen_ref, wall_ref) = refs[:count], refs[count:]
    planes, slots, cols = wall_ref.shape
    rows = frows.shape[1]
    width = payload[0].shape[2]
    nblock = cols // width
    lane8 = lax.broadcasted_iota(jnp.int32, (8, slots), 1)
    places = jnp.full((8, slots), -1.0, F32)
    for s in range(count):
        here = payload[s][room][0:8]
        if s:
            here = pltpu.roll(here, s * room, 1)
        places = jnp.where((lane8 >= s * room) & (lane8 < (s + 1) * room), here, places)
    line = jnp.floor(places * (1.0 / nblock))
    half = places - nblock * line
    row_ids = lax.broadcasted_iota(jnp.int32, (rows, slots), 0).astype(F32)
    chosen = jnp.where(row_ids == line[0:1], 1.0, 0.0)
    chosen_ref[...] = chosen.astype(BF16)
    weight = f32_dot(frows[...], chosen, ((1,), (0,)))
    sub8 = lax.broadcasted_iota(jnp.int32, (8, slots), 0)
    column = jnp.where(sub8 == 2, half, weight).T
    step = min(room, 16)
    for s in range(count):
        for g in range(room // step):
            at = slice(s * room + g * step, s * room + (g + 1) * step)
            value = jnp.swapaxes(payload[s][g * step : (g + 1) * step], 0, 1)
            for b in range(nblock):
                keep = jnp.broadcast_to(column[at, 2:3] == b, (step, width))
                wall_ref[:, at, b * width : (b + 1) * width] = jnp.where(keep[None], value, 0.0)
    at = lax.broadcasted_iota(jnp.int32, (planes, cols), 1)
    hl, hr = halos(count, left_ref, right_ref)
    for f in range(2):
        func = frows[f : f + 1, :]
        first = 0.5 * jnp.sum(hl * func, axis=1, keepdims=True)
        last = 0.5 * jnp.sum(hr * func, axis=1, keepdims=True)
        out[f * planes : (f + 1) * planes, :] = (
            edge_ref[f] + jnp.where(at == 0, first, 0.0) + jnp.where(at == cols - 1, last, 0.0)
        )
    spread = [jnp.broadcast_to(column[:, f : f + 1], (slots, LANES)) for f in range(2)]
    for p in range(planes):
        for b in range(cols // LANES):
            lanes = slice(b * LANES, (b + 1) * LANES)
            value = wall_ref[p, :, lanes]
            for f in range(2):
                at = f * planes + p
                out[at : at + 1, lanes] = out[at : at + 1, lanes] + jnp.sum(value * spread[f], axis=0, keepdims=True)
    out[2 * planes : 2 * planes + 8, :] = scal[0:8, :]


def x_edges(edge, frows, scal, left, right, payload, room):
    planes, cols = edge.shape[1:]
    count, rows = len(payload), frows.shape[1]
    slots = count * room
    return call(
        functools.partial(x_edge_kernel, count, room),
        [struct(2 * planes + 8, cols), struct(rows, slots, dtype=BF16), struct(planes, slots, cols)],
        [VMEM] * (5 + count),
        8,
    )(edge, frows, scal, left, right, *payload)


def wall_kernel(count, mx, my, aux, yrows, sv_ref, left_ref, right_ref, chosen_ref, wall_ref, s_ref, zh_ref, sel_ref, high_ref, low_ref):
    planes, slots, cols = wall_ref.shape
    rows = mx.shape[0]
    hl, hr = halos(count, left_ref, right_ref)
    m = mx[...]
    zh = bf16_dot(right_of(jnp.concatenate([hl, hr], 0), 1), m, ((1,), (1,)))
    zh_ref[...] = zh
    chosen = chosen_ref[...]
    sel_high = bf16_dot(m[:, 0:rows], chosen, ((1,), (0,))).astype(BF16)
    sel_low = bf16_dot(m[:, rows : 2 * rows], chosen, ((1,), (0,))).astype(BF16)
    sel = jnp.concatenate([sel_high, sel_low, sel_high], 1)
    sel_ref[...] = sel
    lane = lax.broadcasted_iota(jnp.int32, (slots, LANES), 1)
    total = jnp.zeros((slots, LANES), F32)
    some = 8
    for q in range(0, planes, some):
        flat = wall_ref[q : q + some].reshape(some * slots, cols)
        wc = right_of(flat, 1)
        t = bf16_dot(wc, aux[...], ((1,), (0,)))
        high, low = split(bf16_dot(wc, my[...], ((1,), (0,))))
        high_ref[q : q + some] = high.reshape(some, slots, cols)
        low_ref[q : q + some] = low.reshape(some, slots, cols)
        for i in range(some):
            p = q + i
            total = jnp.where((lane == p) | (lane == 64 + p), t[i * slots : (i + 1) * slots], total)
    left = jnp.concatenate([m, sel], 1)
    turned = bf16_dot(left, jnp.concatenate([right_of(sv_ref[...], 0), right_of(total, 0)], 0), ((1,), (0,))).T
    low, high = turned[0:planes], turned[64 : 64 + planes]
    f0, f1 = yrows[4:5, :], yrows[5:6, :]
    zl, zr = zh[0:planes], zh[planes : 2 * planes]
    s_ref[0:planes, :] = low + 0.5 * (zl * f0[:, 0:1] + zr * f0[:, cols - 1 : cols])
    s_ref[planes : 2 * planes, :] = high + 0.5 * (zl * f1[:, 0:1] + zr * f1[:, cols - 1 : cols])


def wall_edges(count, mx, my, aux, yrows, sv, left, right, chosen, wall):
    rows = mx.shape[0]
    planes, slots, cols = wall.shape
    return call(
        functools.partial(wall_kernel, count),
        [struct(2 * planes, rows), struct(2 * planes, rows), struct(rows, 3 * slots, dtype=BF16)]
        + [struct(*wall.shape, dtype=BF16)] * 2,
        [VMEM] * 9,
        8,
    )(mx, my, aux, yrows, sv, left, right, chosen, wall)


def wall_sweep_kernel(sel, high_ref, low_ref, v_ref, w_ref):
    for p in range(w_ref.shape[0]):
        high = high_ref[p]
        w_ref[p] = v_ref[p] + bf16_dot(sel[...], jnp.concatenate([high, high, low_ref[p]], 0), ((1,), (0,)))


def wall_sweep(sel, high, low, w):
    return call(
        wall_sweep_kernel,
        struct(*w.shape),
        [VMEM] * 4,
        8,
        input_output_aliases={3: 0},
    )(sel, high, low, w)


def chain(parts, count, me, planes, f_in):
    lanes = parts.shape[2]
    zero = jnp.zeros((planes, lanes), F32)
    f, mine_f = zero, zero
    for k in range(count):
        f_in[k] = f
        mine_f = jnp.where(k == me, f, mine_f)
        f = parts[k, 0:planes, :] + parts[k, 2 * planes : 2 * planes + 1, :] * f
    g, mine_g = zero, zero
    for k in range(count - 1, -1, -1):
        scal = parts[k, 2 * planes : 2 * planes + 8, :]
        mine_g = jnp.where(k == me, g, mine_g)
        g = parts[k, planes : 2 * planes, :] + scal[1:2] * f_in[k] + scal[2:3] * g
    return mine_f, mine_g


def pair_kernel(mine, other, out):
    planes = (mine.shape[0] - 8) // 2
    odd = lax.rem(lax.axis_index("gx"), 2) == 1
    left = jnp.where(odd, other[...], mine[...])
    right = jnp.where(odd, mine[...], other[...])
    out[...] = joined(left, right, planes)


def joined(left, right, planes):
    a, b, s = left[0:planes], left[planes : 2 * planes], left[2 * planes :]
    c, d, t = right[0:planes], right[planes : 2 * planes], right[2 * planes :]
    l0, c0, u0 = s[0:1], s[1:2], s[2:3]
    l1, c1, u1 = t[0:1], t[1:2], t[2:3]
    return jnp.concatenate(
        [c + l1 * a, b + u0 * (d + c1 * a), l0 * l1, c0 + u0 * c1 * l0, u0 * u1, t[3:8]],
        0,
    )


def pair(mine, other):
    return call(pair_kernel, struct(*mine.shape), [VMEM, VMEM], 8)(mine, other)


def gather_parts(me, parts, received):
    count = len(received)
    for shift in range(count):
        parts[pl.ds(lax.rem(me - shift + count, count), 1)] = received[shift][...][None]


def x_join_kernel(count, my, xrows, yrows, scal, s_ref, mine_ref, other_ref, *refs):
    received, (out, moved, parts, f_in) = refs[:count], refs[count:]
    me = lax.axis_index("gx")
    place = lax.div(me, 2)
    odd = lax.rem(me, 2) == 1
    planes = s_ref.shape[0] // 2
    gather_parts(place, parts, received)
    f, g = chain(parts, count, place, planes, f_in)
    mine, other = mine_ref[...], other_ref[...]
    left, right = jnp.where(odd, other, mine), jnp.where(odd, mine, other)
    a, ls = left[0:planes], left[2 * planes :]
    d, rs = right[planes : 2 * planes], right[2 * planes :]
    f_mid = a + ls[0:1] * f
    g_mid = d + rs[1:2] * f_mid + rs[2:3] * g
    in_f, in_b = jnp.where(odd, f_mid, f), jnp.where(odd, g, g_mid)
    ms = mine[2 * planes :]
    first = mine[planes : 2 * planes] + ms[1:2] * in_f + ms[2:3] * in_b
    before_s = jnp.where(odd, ls, parts[jnp.maximum(place - 1, 0), 2 * planes : 2 * planes + 8, :])
    before = jnp.where(me > 0, before_s[3:4] * in_f + before_s[4:5] * first, 0.0)
    low, high = s_ref[0:planes, :], s_ref[planes : 2 * planes, :]
    f0, f1 = yrows[4:5, :], yrows[5:6, :]
    for index, value in enumerate((in_f, in_b, before)):
        c = xrows[index : index + 1, :]
        low = low + jnp.sum(value * f0, axis=1, keepdims=True) * c
        high = high + jnp.sum(value * f1, axis=1, keepdims=True) * c
    out[0:planes, :] = low
    out[planes : 2 * planes, :] = high
    out[2 * planes : 2 * planes + 8, :] = scal[8:16, :]
    moved[...] = bf16_dot(right_of(jnp.concatenate([in_f, in_b, before], 0), 1), my[...], ((1,), (0,)))


def x_join(my, xrows, yrows, scal, s, mine, other, received):
    count = len(received)
    height, cols = received[0].shape
    planes, rows = s.shape[0] // 2, s.shape[1]
    return call(
        functools.partial(x_join_kernel, count),
        [struct(2 * planes + 8, rows), struct(3 * planes, cols)],
        [VMEM] * (7 + count),
        8,
        scratch=[pltpu.VMEM((count, height, cols), F32), pltpu.VMEM((count, planes, cols), F32)],
    )(my, xrows, yrows, scal, s, mine, other, *received)


def finish_kernel(count, xrows, yrows, moved, solid, zh_ref, w_ref, *refs):
    received, (out_hbm, parts, f_in, out_ref, out_sem) = refs[:count], refs[count:]
    me = lax.axis_index("gy")
    planes, rows, cols = w_ref.shape

    def out_copy(p):
        return pltpu.make_async_copy(out_ref.at[p], out_hbm.at[:, p, :], out_sem.at[p])

    gather_parts(me, parts, received)
    in_f, in_b = chain(parts, count, me, planes, f_in)
    y = yrows[0:4, :]
    c = xrows[0:3, :]
    nblock = solid.shape[0]
    marks = jnp.concatenate([solid[...].astype(F32), jnp.zeros((8 - nblock, rows), F32)], 0).T
    width = cols // nblock
    fluid = jnp.concatenate([jnp.broadcast_to(marks[:, b : b + 1] == 0.0, (rows, width)) for b in range(nblock)], 1)
    zero = jnp.zeros((1, rows), F32)
    zero_y = jnp.zeros((1, cols), F32)
    for p in range(planes):
        left = jnp.concatenate(
            [c, in_f[p : p + 1], in_b[p : p + 1], zh_ref[p : p + 1, :], zh_ref[planes + p : planes + p + 1, :], zero], 0
        )
        right = jnp.concatenate(
            [
                moved[p : p + 1, :],
                moved[planes + p : planes + p + 1, :],
                moved[2 * planes + p : 2 * planes + p + 1, :],
                y,
                zero_y,
            ],
            0,
        )
        lh = left.astype(BF16).astype(F32)
        rh = right.astype(BF16).astype(F32)
        lc = jnp.concatenate([lh, lh, left - lh], 0).astype(BF16)
        rc = jnp.concatenate([rh, right - rh, rh], 0).astype(BF16)
        value = w_ref[p] + bf16_dot(lc, rc, ((0,), (0,)))
        out_ref[p] = jnp.where(fluid, value, 0.0)
        if (p + 1) % GROUP == 0:
            for done in range(p + 1 - GROUP, p + 1):
                out_copy(done).start()
    for p in range(planes):
        out_copy(p).wait()


def finish(xrows, yrows, moved, solid, zh, w, received):
    count = len(received)
    height = received[0].shape[0]
    planes, rows, cols = w.shape
    return call(
        functools.partial(finish_kernel, count),
        struct(rows, planes, cols),
        [VMEM] * (6 + count),
        12,
        out_specs=HBM,
        scratch=[
            pltpu.VMEM((count, height, rows), F32),
            pltpu.VMEM((count, planes, rows), F32),
            pltpu.VMEM((planes, rows, cols), F32),
            pltpu.SemaphoreType.DMA((planes,)),
        ],
    )(xrows, yrows, moved, solid, zh, w, *received)


def rotate(value, axis, shift):
    count = lax.axis_size(axis)
    return lax.ppermute(value, axis, [(i, (i + shift) % count) for i in range(count)])


def on_device(
    velocity,
    lower_x,
    upper_x,
    lower_carry_x,
    upper_carry_x,
    lower_y,
    upper_y,
    lower_carry_y,
    upper_carry_y,
    wall_force,
    wall_owner,
    wall_offset,
    solid_mask,
):
    rows, planes, cols = velocity.shape
    walls = wall_force.shape[0]
    n_x, n_y = lax.axis_size("gx"), lax.axis_size("gy")
    room = 2 * walls // n_y
    packed = pack(wall_owner[:, 0], wall_offset, wall_force, n_y, room)
    payload = [packed[0]] + [rotate(packed[s], "gy", s) for s in range(1, n_y)]
    mx, my, aux, my_t, aux_t, xrows, yrows, frows, scal, v, edge, first, last = factors(
        velocity,
        lower_x,
        upper_x,
        lower_carry_x,
        upper_carry_x,
        lower_y,
        upper_y,
        lower_carry_y,
        upper_carry_y,
    )
    left, right = rotate(last, "gy", 1), rotate(first, "gy", -1)
    w, sv = velocity_part(mx, my_t, aux_t, v)
    w, sv, edge = lax.optimization_barrier((w, sv, edge))
    mine, chosen, wall = x_edges(edge, frows, scal, left, right, payload, room)
    other = lax.ppermute(mine, "gx", [(i, i ^ 1) for i in range(n_x)])
    both = pair(mine, other)
    received = [both] + [rotate(both, "gx", 2 * s) for s in range(1, n_x // 2)]
    s_edge, zh, sel, high, low = wall_edges(n_y, mx, my, aux, yrows, sv, left, right, chosen, wall)
    mine, moved = x_join(my, xrows, yrows, scal, s_edge, mine, other, received)
    received = [mine] + [rotate(mine, "gy", s) for s in range(1, n_y)]
    w = wall_sweep(sel, high, low, w)
    return finish(xrows, yrows, moved, solid_mask.T, zh, w, received)


def solution(mesh):
    placed = (
        P("gx", None, "gy"),
        P("gx", None),
        P("gx", None),
        P("gx"),
        P("gx"),
        P("gy", None),
        P("gy", None),
        P("gy"),
        P("gy"),
        P(("gx", "gy"), None, None),
        P(("gx", "gy"), None),
        P(("gx", "gy")),
        P("gx", "gy"),
    )
    return jax.shard_map(
        on_device, mesh=mesh, in_specs=placed, out_specs=P("gx", None, "gy"), check_vma=False
    )
```

```python
import functools

import jax
import jax.numpy as jnp
from jax import lax
from jax.experimental import pallas as pl
from jax.experimental.pallas import tpu as pltpu
from jax.sharding import PartitionSpec as P

F32 = jnp.float32
BF16 = jnp.bfloat16
HIGHEST = lax.Precision.HIGHEST
VMEM = pl.BlockSpec(memory_space=pltpu.VMEM)
SMEM = pl.BlockSpec(memory_space=pltpu.SMEM)
HBM = pl.BlockSpec(memory_space=pltpu.HBM)
LANES = 128
GROUP = 4


def f32_dot(left, right, dims):
    return lax.dot_general(left, right, (dims, ((), ())), precision=HIGHEST, preferred_element_type=F32)


def split(value):
    high = value.astype(BF16)
    return high, (value - high.astype(F32)).astype(BF16)


def left_of(value, axis):
    high, low = split(value)
    return jnp.concatenate([high, low, high], axis=axis)


def right_of(value, axis):
    high, low = split(value)
    return jnp.concatenate([high, high, low], axis=axis)


def bf16_dot(left, right, dims):
    return lax.dot_general(left, right, (dims, ((), ())), preferred_element_type=F32)


def params(vmem_mib, side_effects=False):
    return pltpu.CompilerParams(vmem_limit_bytes=vmem_mib << 20)


def pin(value):
    return pltpu.with_memory_space_constraint(value, pltpu.HBM)


def call(kernel, out_shape, in_specs, vmem_mib, out_specs=None, scratch=(), flops=0, moved=0, **more):
    if out_specs is None:
        out_specs = jax.tree.map(lambda _: VMEM, out_shape)
    return pl.pallas_call(
        kernel,
        out_shape=out_shape,
        in_specs=in_specs,
        out_specs=out_specs,
        scratch_shapes=list(scratch),
        compiler_params=params(vmem_mib),
        cost_estimate=pl.CostEstimate(flops=flops, bytes_accessed=moved, transcendentals=0),
        **more,
    )


def struct(*shape, dtype=F32):
    return jax.ShapeDtypeStruct(shape, dtype)


def sort_walls(count, room, me, walls, owner_ref, table, taken):
    for shift in range(count):
        taken[shift] = shift * room

    def step(entry, carry):
        shift = owner_ref[entry] ^ me
        slot = taken[shift]
        taken[shift] = slot + 1
        table[slot] = entry
        return carry

    lax.fori_loop(0, walls, step, 0, unroll=8)


def pack_kernel(count, room, owner_ref, offset_ref, force_ref, *refs):
    outs, (table, taken) = refs[:count], refs[count:]
    walls, planes, width = force_ref.shape
    me = lax.axis_index("gy")
    for slot in range(count * room):
        table[slot] = walls
    sort_walls(count, room, me, walls, owner_ref, table, taken)
    lane = lax.broadcasted_iota(jnp.int32, (planes, LANES), 1)
    for shift in list(range(1, count)) + [0]:
        places = jnp.full((planes, LANES), -1, jnp.int32)
        for slot in range(room):
            entry = table[shift * room + slot]
            real = jnp.minimum(entry, walls - 1)
            outs[shift][slot] = jnp.where(entry < walls, force_ref[real], 0.0)
            places = jnp.where(lane == slot, jnp.where(entry < walls, offset_ref[real], -1), places)
        outs[shift][room] = places.astype(F32)


def pack(owner, offset, force, count, room):
    walls, planes, width = force.shape
    return call(
        functools.partial(pack_kernel, count, room),
        [struct(room + 1, planes, width) for s in range(count)],
        [SMEM, SMEM, VMEM],
        8,
        scratch=[pltpu.SMEM((count * room,), jnp.int32), pltpu.SMEM((count,), jnp.int32)],
    )(pin(owner), pin(offset), pin(force))


def row(ref, index):
    base = index // 8 * 8
    return ref[base : base + 8, :][index - base : index - base + 1]


def half_shift_lanes(value):
    length = value.shape[1]
    at = lax.broadcasted_iota(jnp.int32, value.shape, 1)
    before = jnp.where(at == 0, 0.0, pltpu.roll(value, 1, 1))
    after = jnp.where(at == length - 1, 0.0, pltpu.roll(value, length - 1, 1))
    return 0.5 * (before + after)


def half_shift_rows(value):
    length = value.shape[0]
    at = lax.broadcasted_iota(jnp.int32, value.shape, 0)
    before = jnp.where(at == 0, 0.0, pltpu.roll(value, 1, 0))
    after = jnp.where(at == length - 1, 0.0, pltpu.roll(value, length - 1, 0))
    return 0.5 * (before + after)


def factor_kernel(v_hbm, *refs):
    given, (mx, my, aux, my_t, aux_t, xrows, yrows, frows, scal) = refs[:8], refs[8:17]
    v_ref, edge_ref, first_ref, last_ref = refs[17:21]
    fetched, (sem, v_sem) = refs[21:29], refs[29:]
    planes, rows, cols = v_ref.shape
    copies = [pltpu.make_async_copy(given[i], fetched[i], sem.at[i]) for i in range(8)]
    for copy in copies:
        copy.start()

    def v_copy(p):
        return pltpu.make_async_copy(v_hbm.at[:, p, :], v_ref.at[p], v_sem.at[p])

    for p in range(planes):
        v_copy(p).start()
    for copy in copies:
        copy.wait()
    lx, ux, lcx, ucx, ly, uy, lcy, ucy = fetched
    rows_x, rows_y = lx.shape[0], ly.shape[0]
    both = bf16_dot(right_of(ux[...], 1), left_of(lx[...], 0), ((1,), (0,)))
    zero = jnp.zeros((1, rows_x), F32)
    frows[...] = jnp.concatenate([row(lx, rows_x - 1), both[0:8][0:1], zero, zero, zero, zero, zero, zero], 0)
    mx[...] = left_of(half_shift_rows(both), 1)
    both_y = bf16_dot(right_of(uy[...], 1), left_of(ly[...], 0), ((1,), (0,)))
    turned = both_y.T
    my[...] = left_of(turned, 0)
    my_t[...] = left_of(half_shift_rows(turned), 0)
    lc, uc = lcx[...], ucx[...]
    pad = jnp.zeros((7, rows_x), F32)
    u_lc = f32_dot(jnp.concatenate([lc, pad], 0), ux[...], ((1,), (1,)))[0:1]
    at = lax.broadcasted_iota(jnp.int32, (1, rows_x), 1)
    c0 = half_shift_lanes(u_lc)
    c1 = half_shift_lanes(uc) + jnp.where(at == rows_x - 1, 0.5, 0.0)
    c2 = jnp.where(at == 0, 0.5, 0.0)
    xrows[...] = jnp.concatenate([c0, c1, c2, zero, zero, zero, zero, zero], 0)
    lcv, ucv = lcy[...], ucy[...]
    pad_y = jnp.zeros((7, rows_y), F32)
    uy_lc = f32_dot(jnp.concatenate([lcv, pad_y], 0), uy[...], ((1,), (1,)))[0:1]
    f0 = row(ly, rows_y - 1)
    f1 = both_y[0:8][0:1]
    zero_y = jnp.zeros((1, rows_y), F32)
    m0, m1 = 0.5 * turned[0:8][0:1], 0.5 * turned[rows_y - 8 : rows_y][7:8]
    yrows[...] = jnp.concatenate([uy_lc, ucv, m0, m1, f0, f1, zero_y, zero_y], 0)
    lane_y = lax.broadcasted_iota(jnp.int32, (rows_y, 128), 1)
    pair_of = jnp.concatenate([f0, f1, pad_y[:6]], 0).T
    spread_cols = jnp.where(lane_y < 64, pair_of[:, 0:1], pair_of[:, 1:2])
    aux[...] = left_of(spread_cols, 0)
    aux_t[...] = left_of(half_shift_rows(spread_cols), 0)

    def spread(value, index, width):
        return jnp.broadcast_to(value[:, index : index + 1], (1, width))

    last = row(ux, rows_x - 1)
    scal[0:8, :] = jnp.concatenate(
        [
            spread(lc, rows_x - 1, rows_x),
            spread(u_lc, 0, rows_x),
            spread(uc, 0, rows_x),
            spread(last, rows_x - 1, rows_x),
            spread(uc, rows_x - 1, rows_x),
            zero,
            zero,
            zero,
        ],
        0,
    )
    scal[8:16, :] = jnp.concatenate(
        [
            spread(lcv, rows_y - 1, rows_x),
            spread(uy_lc, 0, rows_x),
            spread(ucv, 0, rows_x),
            zero,
            zero,
            zero,
            zero,
            zero,
        ],
        0,
    )


    column = frows[...].T
    weights = [jnp.broadcast_to(column[:, f : f + 1], (rows, LANES)) for f in range(2)]
    lane = lax.broadcasted_iota(jnp.int32, (rows, LANES), 1)
    ends = jnp.zeros((rows, LANES), F32)
    for p in range(planes):
        if p % GROUP == 0:
            for here in range(p, p + GROUP):
                v_copy(here).wait()
        for b in range(cols // LANES):
            lanes = slice(b * LANES, (b + 1) * LANES)
            value = v_ref[p, :, lanes]
            for f in range(2):
                edge_ref[f, p : p + 1, lanes] = jnp.sum(value * weights[f], axis=0, keepdims=True)
        ends = jnp.where(lane == p, pltpu.roll(v_ref[p, :, 0:LANES], p, 1), ends)
        to = planes + p
        ends = jnp.where(lane == to, pltpu.roll(v_ref[p, :, cols - LANES : cols], (to + 1) % LANES, 1), ends)
    for f in range(2):
        edge_ref[f] = half_shift_lanes(edge_ref[f])
    turned_ends = ends.T
    first_ref[...] = turned_ends[0:planes]
    last_ref[...] = turned_ends[planes : 2 * planes]


def factors(velocity, lx, ux, lcx, ucx, ly, uy, lcy, ucy):
    rows, planes, cols = velocity.shape
    given = (lx, ux, lcx[None, :], ucx[None, :], ly, uy, lcy[None, :], ucy[None, :])
    return call(
        factor_kernel,
        [
            struct(rows, 3 * rows, dtype=BF16),
            struct(3 * cols, cols, dtype=BF16),
            struct(3 * cols, 128, dtype=BF16),
            struct(3 * cols, cols, dtype=BF16),
            struct(3 * cols, 128, dtype=BF16),
            struct(8, rows),
            struct(8, cols),
            struct(8, rows),
            struct(16, rows),
            struct(planes, rows, cols),
            struct(2, planes, cols),
            struct(planes, rows),
            struct(planes, rows),
        ],
        [HBM] * 9,
        8,
        scratch=[pltpu.VMEM(g.shape, F32) for g in given]
        + [
            pltpu.SemaphoreType.DMA((8,)),
            pltpu.SemaphoreType.DMA((planes,)),
        ],
    )(pin(velocity), *[pin(g) for g in given])


def velocity_kernel(some, mx, my_t, aux_t, v_ref, w_ref, s_ref):
    planes, rows, cols = v_ref.shape
    lane = lax.broadcasted_iota(jnp.int32, (rows, LANES), 1)
    total = jnp.zeros((rows, LANES), F32)
    for q in range(0, planes, some):
        flat = right_of(v_ref[q : q + some].reshape(some * rows, cols), 1)
        r = bf16_dot(flat, my_t[...], ((1,), (0,)))
        t = bf16_dot(flat, aux_t[...], ((1,), (0,)))
        for i in range(some):
            p = q + i
            here = slice(i * rows, (i + 1) * rows)
            total = jnp.where((lane == p) | (lane == 64 + p), t[here], total)
            w_ref[p] = bf16_dot(mx[...], right_of(r[here], 0), ((1,), (0,)))
    s_ref[...] = total


def velocity_part(mx, my_t, aux_t, velocity):
    planes, rows, cols = velocity.shape
    return call(
        functools.partial(velocity_kernel, 4),
        [struct(planes, rows, cols), struct(rows, LANES)],
        [VMEM] * 4,
        16,
    )(mx, my_t, aux_t, velocity)


def halos(count, left_ref, right_ref):
    me = lax.axis_index("gy")
    return jnp.where(me > 0, left_ref[...], 0.0), jnp.where(me < count - 1, right_ref[...], 0.0)


def x_edge_kernel(count, room, edge_ref, frows, scal, left_ref, right_ref, *refs):
    payload, (out, chosen_ref, wall_ref) = refs[:count], refs[count:]
    planes, slots, cols = wall_ref.shape
    rows = frows.shape[1]
    width = payload[0].shape[2]
    nblock = cols // width
    lane8 = lax.broadcasted_iota(jnp.int32, (8, slots), 1)
    places = jnp.full((8, slots), -1.0, F32)
    for s in range(count):
        here = payload[s][room][0:8]
        if s:
            here = pltpu.roll(here, s * room, 1)
        places = jnp.where((lane8 >= s * room) & (lane8 < (s + 1) * room), here, places)
    line = jnp.floor(places * (1.0 / nblock))
    half = places - nblock * line
    row_ids = lax.broadcasted_iota(jnp.int32, (rows, slots), 0).astype(F32)
    chosen = jnp.where(row_ids == line[0:1], 1.0, 0.0)
    chosen_ref[...] = chosen.astype(BF16)
    weight = f32_dot(frows[...], chosen, ((1,), (0,)))
    sub8 = lax.broadcasted_iota(jnp.int32, (8, slots), 0)
    column = jnp.where(sub8 == 2, half, weight).T
    step = min(room, 16)
    for s in range(count):
        for g in range(room // step):
            at = slice(s * room + g * step, s * room + (g + 1) * step)
            value = jnp.swapaxes(payload[s][g * step : (g + 1) * step], 0, 1)
            for b in range(nblock):
                keep = jnp.broadcast_to(column[at, 2:3] == b, (step, width))
                wall_ref[:, at, b * width : (b + 1) * width] = jnp.where(keep[None], value, 0.0)
    at = lax.broadcasted_iota(jnp.int32, (planes, cols), 1)
    hl, hr = halos(count, left_ref, right_ref)
    for f in range(2):
        func = frows[f : f + 1, :]
        first = 0.5 * jnp.sum(hl * func, axis=1, keepdims=True)
        last = 0.5 * jnp.sum(hr * func, axis=1, keepdims=True)
        out[f * planes : (f + 1) * planes, :] = (
            edge_ref[f] + jnp.where(at == 0, first, 0.0) + jnp.where(at == cols - 1, last, 0.0)
        )
    spread = [jnp.broadcast_to(column[:, f : f + 1], (slots, LANES)) for f in range(2)]
    for p in range(planes):
        for b in range(cols // LANES):
            lanes = slice(b * LANES, (b + 1) * LANES)
            value = wall_ref[p, :, lanes]
            for f in range(2):
                at = f * planes + p
                out[at : at + 1, lanes] = out[at : at + 1, lanes] + jnp.sum(value * spread[f], axis=0, keepdims=True)
    out[2 * planes : 2 * planes + 8, :] = scal[0:8, :]


def x_edges(edge, frows, scal, left, right, payload, room):
    planes, cols = edge.shape[1:]
    count, rows = len(payload), frows.shape[1]
    slots = count * room
    return call(
        functools.partial(x_edge_kernel, count, room),
        [struct(2 * planes + 8, cols), struct(rows, slots, dtype=BF16), struct(planes, slots, cols)],
        [VMEM] * (5 + count),
        8,
    )(edge, frows, scal, left, right, *payload)


def wall_kernel(count, mx, my, aux, yrows, sv_ref, left_ref, right_ref, chosen_ref, wall_ref, s_ref, zh_ref, sel_ref, high_ref, low_ref):
    planes, slots, cols = wall_ref.shape
    rows = mx.shape[0]
    hl, hr = halos(count, left_ref, right_ref)
    m = mx[...]
    zh = bf16_dot(right_of(jnp.concatenate([hl, hr], 0), 1), m, ((1,), (1,)))
    zh_ref[...] = zh
    chosen = chosen_ref[...]
    sel_high = bf16_dot(m[:, 0:rows], chosen, ((1,), (0,))).astype(BF16)
    sel_low = bf16_dot(m[:, rows : 2 * rows], chosen, ((1,), (0,))).astype(BF16)
    sel = jnp.concatenate([sel_high, sel_low, sel_high], 1)
    sel_ref[...] = sel
    lane = lax.broadcasted_iota(jnp.int32, (slots, LANES), 1)
    total = jnp.zeros((slots, LANES), F32)
    some = 8
    for q in range(0, planes, some):
        flat = wall_ref[q : q + some].reshape(some * slots, cols)
        wc = right_of(flat, 1)
        t = bf16_dot(wc, aux[...], ((1,), (0,)))
        high, low = split(bf16_dot(wc, my[...], ((1,), (0,))))
        high_ref[q : q + some] = high.reshape(some, slots, cols)
        low_ref[q : q + some] = low.reshape(some, slots, cols)
        for i in range(some):
            p = q + i
            total = jnp.where((lane == p) | (lane == 64 + p), t[i * slots : (i + 1) * slots], total)
    left = jnp.concatenate([m, sel], 1)
    turned = bf16_dot(left, jnp.concatenate([right_of(sv_ref[...], 0), right_of(total, 0)], 0), ((1,), (0,))).T
    low, high = turned[0:planes], turned[64 : 64 + planes]
    f0, f1 = yrows[4:5, :], yrows[5:6, :]
    zl, zr = zh[0:planes], zh[planes : 2 * planes]
    s_ref[0:planes, :] = low + 0.5 * (zl * f0[:, 0:1] + zr * f0[:, cols - 1 : cols])
    s_ref[planes : 2 * planes, :] = high + 0.5 * (zl * f1[:, 0:1] + zr * f1[:, cols - 1 : cols])


def wall_edges(count, mx, my, aux, yrows, sv, left, right, chosen, wall):
    rows = mx.shape[0]
    planes, slots, cols = wall.shape
    return call(
        functools.partial(wall_kernel, count),
        [struct(2 * planes, rows), struct(2 * planes, rows), struct(rows, 3 * slots, dtype=BF16)]
        + [struct(*wall.shape, dtype=BF16)] * 2,
        [VMEM] * 9,
        8,
    )(mx, my, aux, yrows, sv, left, right, chosen, wall)


def wall_sweep_kernel(sel, high_ref, low_ref, v_ref, w_ref):
    for p in range(w_ref.shape[0]):
        high = high_ref[p]
        w_ref[p] = v_ref[p] + bf16_dot(sel[...], jnp.concatenate([high, high, low_ref[p]], 0), ((1,), (0,)))


def wall_sweep(sel, high, low, w):
    return call(
        wall_sweep_kernel,
        struct(*w.shape),
        [VMEM] * 4,
        8,
        input_output_aliases={3: 0},
    )(sel, high, low, w)


def chain(parts, count, me, planes, f_in):
    lanes = parts.shape[2]
    zero = jnp.zeros((planes, lanes), F32)
    f, mine_f = zero, zero
    for k in range(count):
        f_in[k] = f
        mine_f = jnp.where(k == me, f, mine_f)
        f = parts[k, 0:planes, :] + parts[k, 2 * planes : 2 * planes + 1, :] * f
    g, mine_g = zero, zero
    for k in range(count - 1, -1, -1):
        scal = parts[k, 2 * planes : 2 * planes + 8, :]
        mine_g = jnp.where(k == me, g, mine_g)
        g = parts[k, planes : 2 * planes, :] + scal[1:2] * f_in[k] + scal[2:3] * g
    return mine_f, mine_g


def pair_kernel(mine, other, out):
    planes = (mine.shape[0] - 8) // 2
    odd = lax.rem(lax.axis_index("gx"), 2) == 1
    left = jnp.where(odd, other[...], mine[...])
    right = jnp.where(odd, mine[...], other[...])
    out[...] = joined(left, right, planes)


def joined(left, right, planes):
    a, b, s = left[0:planes], left[planes : 2 * planes], left[2 * planes :]
    c, d, t = right[0:planes], right[planes : 2 * planes], right[2 * planes :]
    l0, c0, u0 = s[0:1], s[1:2], s[2:3]
    l1, c1, u1 = t[0:1], t[1:2], t[2:3]
    return jnp.concatenate(
        [c + l1 * a, b + u0 * (d + c1 * a), l0 * l1, c0 + u0 * c1 * l0, u0 * u1, t[3:8]],
        0,
    )


def pair(mine, other):
    return call(pair_kernel, struct(*mine.shape), [VMEM, VMEM], 8)(mine, other)


def gather_parts(me, parts, received, shifts):
    count = len(received)
    for shift, value in zip(shifts, received, strict=True):
        parts[pl.ds(lax.rem(me - shift + count, count), 1)] = value[...][None]


def x_join_kernel(count, shifts, my, xrows, yrows, scal, s_ref, mine_ref, other_ref, *refs):
    received, (out, moved, parts, f_in) = refs[:count], refs[count:]
    me = lax.axis_index("gx")
    place = lax.div(me, 2)
    odd = lax.rem(me, 2) == 1
    planes = s_ref.shape[0] // 2
    gather_parts(place, parts, received, shifts)
    f, g = chain(parts, count, place, planes, f_in)
    mine, other = mine_ref[...], other_ref[...]
    left, right = jnp.where(odd, other, mine), jnp.where(odd, mine, other)
    a, ls = left[0:planes], left[2 * planes :]
    d, rs = right[planes : 2 * planes], right[2 * planes :]
    f_mid = a + ls[0:1] * f
    g_mid = d + rs[1:2] * f_mid + rs[2:3] * g
    in_f, in_b = jnp.where(odd, f_mid, f), jnp.where(odd, g, g_mid)
    ms = mine[2 * planes :]
    first = mine[planes : 2 * planes] + ms[1:2] * in_f + ms[2:3] * in_b
    before_s = jnp.where(odd, ls, parts[jnp.maximum(place - 1, 0), 2 * planes : 2 * planes + 8, :])
    before = jnp.where(me > 0, before_s[3:4] * in_f + before_s[4:5] * first, 0.0)
    low, high = s_ref[0:planes, :], s_ref[planes : 2 * planes, :]
    f0, f1 = yrows[4:5, :], yrows[5:6, :]
    for index, value in enumerate((in_f, in_b, before)):
        c = xrows[index : index + 1, :]
        low = low + jnp.sum(value * f0, axis=1, keepdims=True) * c
        high = high + jnp.sum(value * f1, axis=1, keepdims=True) * c
    out[0:planes, :] = low
    out[planes : 2 * planes, :] = high
    out[2 * planes : 2 * planes + 8, :] = scal[8:16, :]
    moved[...] = bf16_dot(right_of(jnp.concatenate([in_f, in_b, before], 0), 1), my[...], ((1,), (0,)))


def x_join(my, xrows, yrows, scal, s, mine, other, received, shifts):
    count = len(received)
    height, cols = received[0].shape
    planes, rows = s.shape[0] // 2, s.shape[1]
    return call(
        functools.partial(x_join_kernel, count, shifts),
        [struct(2 * planes + 8, rows), struct(3 * planes, cols)],
        [VMEM] * (7 + count),
        8,
        scratch=[pltpu.VMEM((count, height, cols), F32), pltpu.VMEM((count, planes, cols), F32)],
    )(my, xrows, yrows, scal, s, mine, other, *received)


def finish_kernel(count, shifts, xrows, yrows, moved, solid, zh_ref, w_ref, *refs):
    received, (out_hbm, parts, f_in, out_ref, out_sem) = refs[:count], refs[count:]
    me = lax.axis_index("gy")
    planes, rows, cols = w_ref.shape

    def out_copy(p):
        return pltpu.make_async_copy(out_ref.at[p], out_hbm.at[:, p, :], out_sem.at[p])

    gather_parts(me, parts, received, shifts)
    in_f, in_b = chain(parts, count, me, planes, f_in)
    y = yrows[0:4, :]
    c = xrows[0:3, :]
    nblock = solid.shape[0]
    marks = jnp.concatenate([solid[...].astype(F32), jnp.zeros((8 - nblock, rows), F32)], 0).T
    width = cols // nblock
    fluid = jnp.concatenate([jnp.broadcast_to(marks[:, b : b + 1] == 0.0, (rows, width)) for b in range(nblock)], 1)
    zero = jnp.zeros((1, rows), F32)
    zero_y = jnp.zeros((1, cols), F32)
    for p in range(planes):
        left = jnp.concatenate(
            [c, in_f[p : p + 1], in_b[p : p + 1], zh_ref[p : p + 1, :], zh_ref[planes + p : planes + p + 1, :], zero], 0
        )
        right = jnp.concatenate(
            [
                moved[p : p + 1, :],
                moved[planes + p : planes + p + 1, :],
                moved[2 * planes + p : 2 * planes + p + 1, :],
                y,
                zero_y,
            ],
            0,
        )
        lh = left.astype(BF16).astype(F32)
        rh = right.astype(BF16).astype(F32)
        lc = jnp.concatenate([lh, lh, left - lh], 0).astype(BF16)
        rc = jnp.concatenate([rh, right - rh, rh], 0).astype(BF16)
        value = w_ref[p] + bf16_dot(lc, rc, ((0,), (0,)))
        out_ref[p] = jnp.where(fluid, value, 0.0)
        if (p + 1) % GROUP == 0:
            for done in range(p + 1 - GROUP, p + 1):
                out_copy(done).start()
    for p in range(planes):
        out_copy(p).wait()


def finish(xrows, yrows, moved, solid, zh, w, received, shifts):
    count = len(received)
    height = received[0].shape[0]
    planes, rows, cols = w.shape
    return call(
        functools.partial(finish_kernel, count, shifts),
        struct(rows, planes, cols),
        [VMEM] * (6 + count),
        12,
        out_specs=HBM,
        scratch=[
            pltpu.VMEM((count, height, rows), F32),
            pltpu.VMEM((count, planes, rows), F32),
            pltpu.VMEM((planes, rows, cols), F32),
            pltpu.SemaphoreType.DMA((planes,)),
        ],
    )(xrows, yrows, moved, solid, zh, w, *received)


def swap(value, axis, mask):
    return lax.ppermute(value, axis, [(i, i ^ mask) for i in range(lax.axis_size(axis))])


def rotate(value, axis, shift):
    count = lax.axis_size(axis)
    return lax.ppermute(value, axis, [(i, (i + shift) % count) for i in range(count)])


def on_device(
    velocity,
    lower_x,
    upper_x,
    lower_carry_x,
    upper_carry_x,
    lower_y,
    upper_y,
    lower_carry_y,
    upper_carry_y,
    wall_force,
    wall_owner,
    wall_offset,
    solid_mask,
):
    rows, planes, cols = velocity.shape
    walls = wall_force.shape[0]
    n_x, n_y = lax.axis_size("gx"), lax.axis_size("gy")
    room = 2 * walls // n_y
    packed = pack(wall_owner[:, 0], wall_offset, wall_force, n_y, room)
    payload = [packed[0]] + [swap(packed[s], "gy", s) for s in range(1, n_y)]
    mx, my, aux, my_t, aux_t, xrows, yrows, frows, scal, v, edge, first, last = factors(
        velocity,
        lower_x,
        upper_x,
        lower_carry_x,
        upper_carry_x,
        lower_y,
        upper_y,
        lower_carry_y,
        upper_carry_y,
    )
    left, right = rotate(last, "gy", 1), rotate(first, "gy", -1)
    w, sv = velocity_part(mx, my_t, aux_t, v)
    w, sv, edge = lax.optimization_barrier((w, sv, edge))
    mine, chosen, wall = x_edges(edge, frows, scal, left, right, payload, room)
    other = swap(mine, "gx", 1)
    both = pair(mine, other)
    shifts = list(range(n_x // 2))
    received = [rotate(both, "gx", 2 * s) if s else both for s in shifts]
    s_edge, zh, sel, high, low = wall_edges(n_y, mx, my, aux, yrows, sv, left, right, chosen, wall)
    mine, moved = x_join(my, xrows, yrows, scal, s_edge, mine, other, received, shifts)
    shifts = list(range(n_y))
    received = [rotate(mine, "gy", s) if s else mine for s in shifts]
    w = wall_sweep(sel, high, low, w)
    return finish(xrows, yrows, moved, solid_mask.T, zh, w, received, shifts)


def solution(mesh):
    placed = (
        P("gx", None, "gy"),
        P("gx", None),
        P("gx", None),
        P("gx"),
        P("gx"),
        P("gy", None),
        P("gy", None),
        P("gy"),
        P("gy"),
        P(("gx", "gy"), None, None),
        P(("gx", "gy"), None),
        P(("gx", "gy")),
        P("gx", "gy"),
    )
    return jax.shard_map(
        on_device, mesh=mesh, in_specs=placed, out_specs=P("gx", None, "gy"), check_vma=False
    )
```

```python
import functools

import jax
import jax.numpy as jnp
from jax import lax
from jax.experimental import pallas as pl
from jax.experimental.pallas import tpu as pltpu
from jax.sharding import PartitionSpec as P

F32 = jnp.float32
BF16 = jnp.bfloat16
HIGHEST = lax.Precision.HIGHEST
VMEM = pl.BlockSpec(memory_space=pltpu.VMEM)
SMEM = pl.BlockSpec(memory_space=pltpu.SMEM)
HBM = pl.BlockSpec(memory_space=pltpu.HBM)
LANES = 128
GROUP = 4


def f32_dot(left, right, dims):
    return lax.dot_general(left, right, (dims, ((), ())), precision=HIGHEST, preferred_element_type=F32)


def split(value):
    high = value.astype(BF16)
    return high, (value - high.astype(F32)).astype(BF16)


def left_of(value, axis):
    high, low = split(value)
    return jnp.concatenate([high, low, high], axis=axis)


def right_of(value, axis):
    high, low = split(value)
    return jnp.concatenate([high, high, low], axis=axis)


def bf16_dot(left, right, dims):
    return lax.dot_general(left, right, (dims, ((), ())), preferred_element_type=F32)


def params(vmem_mib, side_effects=False):
    return pltpu.CompilerParams(vmem_limit_bytes=vmem_mib << 20)


def pin(value):
    return pltpu.with_memory_space_constraint(value, pltpu.HBM)


def call(kernel, out_shape, in_specs, vmem_mib, out_specs=None, scratch=(), flops=0, moved=0, **more):
    if out_specs is None:
        out_specs = jax.tree.map(lambda _: VMEM, out_shape)
    return pl.pallas_call(
        kernel,
        out_shape=out_shape,
        in_specs=in_specs,
        out_specs=out_specs,
        scratch_shapes=list(scratch),
        compiler_params=params(vmem_mib),
        cost_estimate=pl.CostEstimate(flops=flops, bytes_accessed=moved, transcendentals=0),
        **more,
    )


def struct(*shape, dtype=F32):
    return jax.ShapeDtypeStruct(shape, dtype)


def sort_walls(count, room, me, walls, owner_ref, table, taken):
    for shift in range(count):
        taken[shift] = shift * room

    def step(entry, carry):
        shift = owner_ref[entry] ^ me
        slot = taken[shift]
        taken[shift] = slot + 1
        table[slot] = entry
        return carry

    lax.fori_loop(0, walls, step, 0, unroll=8)


def pack_kernel(count, room, owner_ref, offset_ref, force_ref, *refs):
    outs, (table, taken) = refs[:count], refs[count:]
    walls, planes, width = force_ref.shape
    me = lax.axis_index("gy")
    for slot in range(count * room):
        table[slot] = walls
    sort_walls(count, room, me, walls, owner_ref, table, taken)
    lane = lax.broadcasted_iota(jnp.int32, (planes, LANES), 1)
    for shift in list(range(1, count)) + [0]:
        places = jnp.full((planes, LANES), -1, jnp.int32)
        for slot in range(room):
            entry = table[shift * room + slot]
            real = jnp.minimum(entry, walls - 1)
            outs[shift][slot] = jnp.where(entry < walls, force_ref[real], 0.0)
            places = jnp.where(lane == slot, jnp.where(entry < walls, offset_ref[real], -1), places)
        outs[shift][room] = places.astype(F32)


def pack(owner, offset, force, count, room):
    walls, planes, width = force.shape
    return call(
        functools.partial(pack_kernel, count, room),
        [struct(room + 1, planes, width) for s in range(count)],
        [SMEM, SMEM, VMEM],
        8,
        scratch=[pltpu.SMEM((count * room,), jnp.int32), pltpu.SMEM((count,), jnp.int32)],
    )(pin(owner), pin(offset), pin(force))


def row(ref, index):
    base = index // 8 * 8
    return ref[base : base + 8, :][index - base : index - base + 1]


def half_shift_lanes(value):
    length = value.shape[1]
    at = lax.broadcasted_iota(jnp.int32, value.shape, 1)
    before = jnp.where(at == 0, 0.0, pltpu.roll(value, 1, 1))
    after = jnp.where(at == length - 1, 0.0, pltpu.roll(value, length - 1, 1))
    return 0.5 * (before + after)


def half_shift_rows(value):
    length = value.shape[0]
    at = lax.broadcasted_iota(jnp.int32, value.shape, 0)
    before = jnp.where(at == 0, 0.0, pltpu.roll(value, 1, 0))
    after = jnp.where(at == length - 1, 0.0, pltpu.roll(value, length - 1, 0))
    return 0.5 * (before + after)


def factor_kernel(v_hbm, *refs):
    given, (mx, my, aux, my_t, aux_t, xrows, yrows, frows, scal) = refs[:8], refs[8:17]
    v_ref, edge_ref, first_ref, last_ref = refs[17:21]
    fetched, (sem, v_sem) = refs[21:29], refs[29:]
    planes, rows, cols = v_ref.shape
    copies = [pltpu.make_async_copy(given[i], fetched[i], sem.at[i]) for i in range(8)]
    for copy in copies:
        copy.start()

    def v_copy(p):
        return pltpu.make_async_copy(v_hbm.at[:, p, :], v_ref.at[p], v_sem.at[p])

    for p in range(planes):
        v_copy(p).start()
    for copy in copies:
        copy.wait()
    lx, ux, lcx, ucx, ly, uy, lcy, ucy = fetched
    rows_x, rows_y = lx.shape[0], ly.shape[0]
    both = bf16_dot(right_of(ux[...], 1), left_of(lx[...], 0), ((1,), (0,)))
    zero = jnp.zeros((1, rows_x), F32)
    frows[...] = jnp.concatenate([row(lx, rows_x - 1), both[0:8][0:1], zero, zero, zero, zero, zero, zero], 0)
    mx[...] = left_of(half_shift_rows(both), 1)
    both_y = bf16_dot(right_of(uy[...], 1), left_of(ly[...], 0), ((1,), (0,)))
    turned = both_y.T
    my[...] = left_of(turned, 0)
    my_t[...] = left_of(half_shift_rows(turned), 0)
    lc, uc = lcx[...], ucx[...]
    pad = jnp.zeros((7, rows_x), F32)
    u_lc = f32_dot(jnp.concatenate([lc, pad], 0), ux[...], ((1,), (1,)))[0:1]
    at = lax.broadcasted_iota(jnp.int32, (1, rows_x), 1)
    c0 = half_shift_lanes(u_lc)
    c1 = half_shift_lanes(uc) + jnp.where(at == rows_x - 1, 0.5, 0.0)
    c2 = jnp.where(at == 0, 0.5, 0.0)
    xrows[...] = jnp.concatenate([c0, c1, c2, zero, zero, zero, zero, zero], 0)
    lcv, ucv = lcy[...], ucy[...]
    pad_y = jnp.zeros((7, rows_y), F32)
    uy_lc = f32_dot(jnp.concatenate([lcv, pad_y], 0), uy[...], ((1,), (1,)))[0:1]
    f0 = row(ly, rows_y - 1)
    f1 = both_y[0:8][0:1]
    zero_y = jnp.zeros((1, rows_y), F32)
    m0, m1 = 0.5 * turned[0:8][0:1], 0.5 * turned[rows_y - 8 : rows_y][7:8]
    yrows[...] = jnp.concatenate([uy_lc, ucv, m0, m1, f0, f1, zero_y, zero_y], 0)
    lane_y = lax.broadcasted_iota(jnp.int32, (rows_y, 128), 1)
    pair_of = jnp.concatenate([f0, f1, pad_y[:6]], 0).T
    spread_cols = jnp.where(lane_y < 64, pair_of[:, 0:1], pair_of[:, 1:2])
    aux[...] = left_of(spread_cols, 0)
    aux_t[...] = left_of(half_shift_rows(spread_cols), 0)

    def spread(value, index, width):
        return jnp.broadcast_to(value[:, index : index + 1], (1, width))

    last = row(ux, rows_x - 1)
    scal[0:8, :] = jnp.concatenate(
        [
            spread(lc, rows_x - 1, rows_x),
            spread(u_lc, 0, rows_x),
            spread(uc, 0, rows_x),
            spread(last, rows_x - 1, rows_x),
            spread(uc, rows_x - 1, rows_x),
            zero,
            zero,
            zero,
        ],
        0,
    )
    scal[8:16, :] = jnp.concatenate(
        [
            spread(lcv, rows_y - 1, rows_x),
            spread(uy_lc, 0, rows_x),
            spread(ucv, 0, rows_x),
            zero,
            zero,
            zero,
            zero,
            zero,
        ],
        0,
    )


    column = frows[...].T
    weights = [jnp.broadcast_to(column[:, f : f + 1], (rows, LANES)) for f in range(2)]
    lane = lax.broadcasted_iota(jnp.int32, (rows, LANES), 1)
    ends = jnp.zeros((rows, LANES), F32)
    for p in range(planes):
        if p % GROUP == 0:
            for here in range(p, p + GROUP):
                v_copy(here).wait()
        for b in range(cols // LANES):
            lanes = slice(b * LANES, (b + 1) * LANES)
            value = v_ref[p, :, lanes]
            for f in range(2):
                edge_ref[f, p : p + 1, lanes] = jnp.sum(value * weights[f], axis=0, keepdims=True)
        ends = jnp.where(lane == p, pltpu.roll(v_ref[p, :, 0:LANES], p, 1), ends)
        to = planes + p
        ends = jnp.where(lane == to, pltpu.roll(v_ref[p, :, cols - LANES : cols], (to + 1) % LANES, 1), ends)
    for f in range(2):
        edge_ref[f] = half_shift_lanes(edge_ref[f])
    turned_ends = ends.T
    first_ref[...] = turned_ends[0:planes]
    last_ref[...] = turned_ends[planes : 2 * planes]


def factors(velocity, lx, ux, lcx, ucx, ly, uy, lcy, ucy):
    rows, planes, cols = velocity.shape
    given = (lx, ux, lcx[None, :], ucx[None, :], ly, uy, lcy[None, :], ucy[None, :])
    return call(
        factor_kernel,
        [
            struct(rows, 3 * rows, dtype=BF16),
            struct(3 * cols, cols, dtype=BF16),
            struct(3 * cols, 128, dtype=BF16),
            struct(3 * cols, cols, dtype=BF16),
            struct(3 * cols, 128, dtype=BF16),
            struct(8, rows),
            struct(8, cols),
            struct(8, rows),
            struct(16, rows),
            struct(planes, rows, cols),
            struct(2, planes, cols),
            struct(planes, rows),
            struct(planes, rows),
        ],
        [HBM] * 9,
        8,
        scratch=[pltpu.VMEM(g.shape, F32) for g in given]
        + [
            pltpu.SemaphoreType.DMA((8,)),
            pltpu.SemaphoreType.DMA((planes,)),
        ],
    )(pin(velocity), *[pin(g) for g in given])


def velocity_kernel(some, mx, my_t, aux_t, v_ref, w_ref, s_ref):
    planes, rows, cols = v_ref.shape
    lane = lax.broadcasted_iota(jnp.int32, (rows, LANES), 1)
    total = jnp.zeros((rows, LANES), F32)
    for q in range(0, planes, some):
        flat = right_of(v_ref[q : q + some].reshape(some * rows, cols), 1)
        r = bf16_dot(flat, my_t[...], ((1,), (0,)))
        t = bf16_dot(flat, aux_t[...], ((1,), (0,)))
        for i in range(some):
            p = q + i
            here = slice(i * rows, (i + 1) * rows)
            total = jnp.where((lane == p) | (lane == 64 + p), t[here], total)
            w_ref[p] = bf16_dot(mx[...], right_of(r[here], 0), ((1,), (0,)))
    s_ref[...] = total


def velocity_part(mx, my_t, aux_t, velocity):
    planes, rows, cols = velocity.shape
    return call(
        functools.partial(velocity_kernel, 4),
        [struct(planes, rows, cols), struct(rows, LANES)],
        [VMEM] * 4,
        16,
    )(mx, my_t, aux_t, velocity)


def halos(count, left_ref, right_ref):
    me = lax.axis_index("gy")
    return jnp.where(me > 0, left_ref[...], 0.0), jnp.where(me < count - 1, right_ref[...], 0.0)


def x_edge_kernel(count, room, edge_ref, frows, scal, left_ref, right_ref, *refs):
    payload, (out, chosen_ref, wall_ref) = refs[:count], refs[count:]
    planes, slots, cols = wall_ref.shape
    rows = frows.shape[1]
    width = payload[0].shape[2]
    nblock = cols // width
    blocks = cols // LANES
    lane8 = lax.broadcasted_iota(jnp.int32, (8, slots), 1)
    places = jnp.full((8, slots), -1.0, F32)
    for s in range(count):
        here = payload[s][room][0:8]
        if s:
            here = pltpu.roll(here, s * room, 1)
        places = jnp.where((lane8 >= s * room) & (lane8 < (s + 1) * room), here, places)
    line = jnp.floor(places * (1.0 / nblock))
    half = places - nblock * line
    row_ids = lax.broadcasted_iota(jnp.int32, (rows, slots), 0).astype(F32)
    chosen = jnp.where(row_ids == line[0:1], 1.0, 0.0)
    chosen_ref[...] = chosen.astype(BF16)
    weight = f32_dot(frows[...], chosen, ((1,), (0,)))
    sub8 = lax.broadcasted_iota(jnp.int32, (8, slots), 0)
    column = jnp.where(sub8 == 2, half, weight).T
    step = min(room, 16)
    for s in range(count):
        for g in range(room // step):
            at = slice(s * room + g * step, s * room + (g + 1) * step)
            value = jnp.swapaxes(payload[s][g * step : (g + 1) * step], 0, 1)
            for b in range(nblock):
                keep = jnp.broadcast_to(column[at, 2:3] == b, (step, width))
                wall_ref[:, at, b * width : (b + 1) * width] = jnp.where(keep[None], value, 0.0)
    at = lax.broadcasted_iota(jnp.int32, (planes, cols), 1)
    hl, hr = halos(count, left_ref, right_ref)
    for f in range(2):
        func = frows[f : f + 1, :]
        first = 0.5 * jnp.sum(hl * func, axis=1, keepdims=True)
        last = 0.5 * jnp.sum(hr * func, axis=1, keepdims=True)
        edge = edge_ref[f] + jnp.where(at == 0, first, 0.0) + jnp.where(at == cols - 1, last, 0.0)
        for b in range(blocks):
            row = (f * blocks + b) * planes
            out[row : row + planes, :] = edge[:, b * LANES : (b + 1) * LANES]
    spread = [jnp.broadcast_to(column[:, f : f + 1], (slots, LANES)) for f in range(2)]
    for p in range(planes):
        for b in range(blocks):
            lanes = slice(b * LANES, (b + 1) * LANES)
            value = wall_ref[p, :, lanes]
            for f in range(2):
                at = (f * blocks + b) * planes + p
                out[at : at + 1, :] = out[at : at + 1, :] + jnp.sum(value * spread[f], axis=0, keepdims=True)
    out[2 * blocks * planes : 2 * blocks * planes + 8, :] = scal[0:8, 0:LANES]


def x_edges(edge, frows, scal, left, right, payload, room):
    planes, cols = edge.shape[1:]
    count, rows = len(payload), frows.shape[1]
    slots = count * room
    return call(
        functools.partial(x_edge_kernel, count, room),
        [struct(2 * planes * (cols // LANES) + 8, LANES), struct(rows, slots, dtype=BF16), struct(planes, slots, cols)],
        [VMEM] * (5 + count),
        8,
    )(edge, frows, scal, left, right, *payload)


def wall_kernel(count, mx, my, aux, yrows, sv_ref, left_ref, right_ref, chosen_ref, wall_ref, s_ref, zh_ref, sel_ref, high_ref, low_ref):
    planes, slots, cols = wall_ref.shape
    rows = mx.shape[0]
    hl, hr = halos(count, left_ref, right_ref)
    m = mx[...]
    zh = bf16_dot(right_of(jnp.concatenate([hl, hr], 0), 1), m, ((1,), (1,)))
    zh_ref[...] = zh
    chosen = chosen_ref[...]
    sel_high = bf16_dot(m[:, 0:rows], chosen, ((1,), (0,))).astype(BF16)
    sel_low = bf16_dot(m[:, rows : 2 * rows], chosen, ((1,), (0,))).astype(BF16)
    sel = jnp.concatenate([sel_high, sel_low, sel_high], 1)
    sel_ref[...] = sel
    lane = lax.broadcasted_iota(jnp.int32, (slots, LANES), 1)
    total = jnp.zeros((slots, LANES), F32)
    some = 8
    for q in range(0, planes, some):
        flat = wall_ref[q : q + some].reshape(some * slots, cols)
        wc = right_of(flat, 1)
        t = bf16_dot(wc, aux[...], ((1,), (0,)))
        high, low = split(bf16_dot(wc, my[...], ((1,), (0,))))
        high_ref[q : q + some] = high.reshape(some, slots, cols)
        low_ref[q : q + some] = low.reshape(some, slots, cols)
        for i in range(some):
            p = q + i
            total = jnp.where((lane == p) | (lane == 64 + p), t[i * slots : (i + 1) * slots], total)
    left = jnp.concatenate([m, sel], 1)
    turned = bf16_dot(left, jnp.concatenate([right_of(sv_ref[...], 0), right_of(total, 0)], 0), ((1,), (0,))).T
    low, high = turned[0:planes], turned[64 : 64 + planes]
    f0, f1 = yrows[4:5, :], yrows[5:6, :]
    zl, zr = zh[0:planes], zh[planes : 2 * planes]
    s_ref[0:planes, :] = low + 0.5 * (zl * f0[:, 0:1] + zr * f0[:, cols - 1 : cols])
    s_ref[planes : 2 * planes, :] = high + 0.5 * (zl * f1[:, 0:1] + zr * f1[:, cols - 1 : cols])


def wall_edges(count, mx, my, aux, yrows, sv, left, right, chosen, wall):
    rows = mx.shape[0]
    planes, slots, cols = wall.shape
    return call(
        functools.partial(wall_kernel, count),
        [struct(2 * planes, rows), struct(2 * planes, rows), struct(rows, 3 * slots, dtype=BF16)]
        + [struct(*wall.shape, dtype=BF16)] * 2,
        [VMEM] * 9,
        8,
    )(mx, my, aux, yrows, sv, left, right, chosen, wall)


def wall_sweep_kernel(sel, high_ref, low_ref, v_ref, w_ref):
    for p in range(w_ref.shape[0]):
        high = high_ref[p]
        w_ref[p] = v_ref[p] + bf16_dot(sel[...], jnp.concatenate([high, high, low_ref[p]], 0), ((1,), (0,)))


def wall_sweep(sel, high, low, w):
    return call(
        wall_sweep_kernel,
        struct(*w.shape),
        [VMEM] * 4,
        8,
        input_output_aliases={3: 0},
    )(sel, high, low, w)


def pack_edges(first, second, scalars):
    blocks = range(first.shape[1] // LANES)
    pieces = [value[:, b * LANES : (b + 1) * LANES] for value in (first, second) for b in blocks]
    return jnp.concatenate(pieces + [scalars[:, 0:LANES]], 0)


def unpack_edges(flat, planes):
    blocks = (flat.shape[0] - 8) // (2 * planes)
    pieces = [flat[b * planes : (b + 1) * planes] for b in range(2 * blocks)]
    scalars = jnp.concatenate([flat[2 * blocks * planes :]] * blocks, 1)
    return jnp.concatenate(pieces[:blocks], 1), jnp.concatenate(pieces[blocks:], 1), scalars


def chain(parts, count, me, planes, f_in):
    zero = jnp.zeros(f_in.shape[1:], F32)
    edges = [unpack_edges(parts[k], planes) for k in range(count)]
    f, mine_f = zero, zero
    for k in range(count):
        f_in[k] = f
        mine_f = jnp.where(k == me, f, mine_f)
        f = edges[k][0] + edges[k][2][0:1] * f
    g, mine_g = zero, zero
    for k in range(count - 1, -1, -1):
        scal = edges[k][2]
        mine_g = jnp.where(k == me, g, mine_g)
        g = edges[k][1] + scal[1:2] * f_in[k] + scal[2:3] * g
    return mine_f, mine_g


def pair_kernel(planes, mine, other, out):
    odd = lax.rem(lax.axis_index("gx"), 2) == 1
    left = jnp.where(odd, other[...], mine[...])
    right = jnp.where(odd, mine[...], other[...])
    out[...] = joined(left, right, planes)


def joined(left, right, planes):
    a, b, s = unpack_edges(left, planes)
    c, d, t = unpack_edges(right, planes)
    l0, c0, u0 = s[0:1], s[1:2], s[2:3]
    l1, c1, u1 = t[0:1], t[1:2], t[2:3]
    scalars = jnp.concatenate([l0 * l1, c0 + u0 * c1 * l0, u0 * u1, t[3:8]], 0)
    return pack_edges(c + l1 * a, b + u0 * (d + c1 * a), scalars)


def pair(mine, other, planes):
    return call(functools.partial(pair_kernel, planes), struct(*mine.shape), [VMEM, VMEM], 8)(mine, other)


def gather_parts(me, parts, received, shifts):
    count = len(received)
    for shift, value in zip(shifts, received, strict=True):
        parts[pl.ds(lax.rem(me - shift + count, count), 1)] = value[...][None]


def x_join_kernel(count, shifts, my, xrows, yrows, scal, s_ref, mine_ref, other_ref, *refs):
    received, (out, moved, parts, f_in) = refs[:count], refs[count:]
    me = lax.axis_index("gx")
    place = lax.div(me, 2)
    odd = lax.rem(me, 2) == 1
    planes = s_ref.shape[0] // 2
    gather_parts(place, parts, received, shifts)
    f, g = chain(parts, count, place, planes, f_in)
    mine, other = mine_ref[...], other_ref[...]
    left, right = jnp.where(odd, other, mine), jnp.where(odd, mine, other)
    a, _, ls = unpack_edges(left, planes)
    _, d, rs = unpack_edges(right, planes)
    f_mid = a + ls[0:1] * f
    g_mid = d + rs[1:2] * f_mid + rs[2:3] * g
    in_f, in_b = jnp.where(odd, f_mid, f), jnp.where(odd, g, g_mid)
    _, mine_b, ms = unpack_edges(mine, planes)
    first = mine_b + ms[1:2] * in_f + ms[2:3] * in_b
    before_s = jnp.where(odd, ls, unpack_edges(parts[jnp.maximum(place - 1, 0)], planes)[2])
    before = jnp.where(me > 0, before_s[3:4] * in_f + before_s[4:5] * first, 0.0)
    low, high = s_ref[0:planes, :], s_ref[planes : 2 * planes, :]
    f0, f1 = yrows[4:5, :], yrows[5:6, :]
    for index, value in enumerate((in_f, in_b, before)):
        c = xrows[index : index + 1, :]
        low = low + jnp.sum(value * f0, axis=1, keepdims=True) * c
        high = high + jnp.sum(value * f1, axis=1, keepdims=True) * c
    out[...] = pack_edges(low, high, scal[8:16, :])
    moved[...] = bf16_dot(right_of(jnp.concatenate([in_f, in_b, before], 0), 1), my[...], ((1,), (0,)))


def x_join(my, xrows, yrows, scal, s, mine, other, received, shifts):
    count = len(received)
    height, cols = received[0].shape[0], my.shape[1]
    planes, rows = s.shape[0] // 2, s.shape[1]
    return call(
        functools.partial(x_join_kernel, count, shifts),
        [struct(2 * planes * (rows // LANES) + 8, LANES), struct(3 * planes, cols)],
        [VMEM] * (7 + count),
        8,
        scratch=[pltpu.VMEM((count, height, LANES), F32), pltpu.VMEM((count, planes, cols), F32)],
    )(my, xrows, yrows, scal, s, mine, other, *received)


def finish_kernel(count, shifts, xrows, yrows, moved, solid, zh_ref, w_ref, *refs):
    received, (out_hbm, parts, f_in, out_ref, out_sem) = refs[:count], refs[count:]
    me = lax.axis_index("gy")
    planes, rows, cols = w_ref.shape

    def out_copy(p):
        return pltpu.make_async_copy(out_ref.at[p], out_hbm.at[:, p, :], out_sem.at[p])

    gather_parts(me, parts, received, shifts)
    in_f, in_b = chain(parts, count, me, planes, f_in)
    y = yrows[0:4, :]
    c = xrows[0:3, :]
    nblock = solid.shape[0]
    marks = jnp.concatenate([solid[...].astype(F32), jnp.zeros((8 - nblock, rows), F32)], 0).T
    width = cols // nblock
    fluid = jnp.concatenate([jnp.broadcast_to(marks[:, b : b + 1] == 0.0, (rows, width)) for b in range(nblock)], 1)
    zero = jnp.zeros((1, rows), F32)
    zero_y = jnp.zeros((1, cols), F32)
    for p in range(planes):
        left = jnp.concatenate(
            [c, in_f[p : p + 1], in_b[p : p + 1], zh_ref[p : p + 1, :], zh_ref[planes + p : planes + p + 1, :], zero], 0
        )
        right = jnp.concatenate(
            [
                moved[p : p + 1, :],
                moved[planes + p : planes + p + 1, :],
                moved[2 * planes + p : 2 * planes + p + 1, :],
                y,
                zero_y,
            ],
            0,
        )
        lh = left.astype(BF16).astype(F32)
        rh = right.astype(BF16).astype(F32)
        lc = jnp.concatenate([lh, lh, left - lh], 0).astype(BF16)
        rc = jnp.concatenate([rh, right - rh, rh], 0).astype(BF16)
        value = w_ref[p] + bf16_dot(lc, rc, ((0,), (0,)))
        out_ref[p] = jnp.where(fluid, value, 0.0)
        if (p + 1) % GROUP == 0:
            for done in range(p + 1 - GROUP, p + 1):
                out_copy(done).start()
    for p in range(planes):
        out_copy(p).wait()


def finish(xrows, yrows, moved, solid, zh, w, received, shifts):
    count = len(received)
    height = received[0].shape[0]
    planes, rows, cols = w.shape
    return call(
        functools.partial(finish_kernel, count, shifts),
        struct(rows, planes, cols),
        [VMEM] * (6 + count),
        12,
        out_specs=HBM,
        scratch=[
            pltpu.VMEM((count, height, LANES), F32),
            pltpu.VMEM((count, planes, rows), F32),
            pltpu.VMEM((planes, rows, cols), F32),
            pltpu.SemaphoreType.DMA((planes,)),
        ],
    )(xrows, yrows, moved, solid, zh, w, *received)


def swap(value, axis, mask):
    return lax.ppermute(value, axis, [(i, i ^ mask) for i in range(lax.axis_size(axis))])


def rotate(value, axis, shift):
    count = lax.axis_size(axis)
    return lax.ppermute(value, axis, [(i, (i + shift) % count) for i in range(count)])


def on_device(
    velocity,
    lower_x,
    upper_x,
    lower_carry_x,
    upper_carry_x,
    lower_y,
    upper_y,
    lower_carry_y,
    upper_carry_y,
    wall_force,
    wall_owner,
    wall_offset,
    solid_mask,
):
    rows, planes, cols = velocity.shape
    walls = wall_force.shape[0]
    n_x, n_y = lax.axis_size("gx"), lax.axis_size("gy")
    room = 2 * walls // n_y
    packed = pack(wall_owner[:, 0], wall_offset, wall_force, n_y, room)
    payload = [packed[0]] + [swap(packed[s], "gy", s) for s in range(1, n_y)]
    mx, my, aux, my_t, aux_t, xrows, yrows, frows, scal, v, edge, first, last = factors(
        velocity,
        lower_x,
        upper_x,
        lower_carry_x,
        upper_carry_x,
        lower_y,
        upper_y,
        lower_carry_y,
        upper_carry_y,
    )
    left, right = rotate(last, "gy", 1), rotate(first, "gy", -1)
    w, sv = velocity_part(mx, my_t, aux_t, v)
    w, sv, edge = lax.optimization_barrier((w, sv, edge))
    mine, chosen, wall = x_edges(edge, frows, scal, left, right, payload, room)
    other = swap(mine, "gx", 1)
    both = pair(mine, other, planes)
    shifts = list(range(n_x // 2))
    received = [rotate(both, "gx", 2 * s) if s else both for s in shifts]
    s_edge, zh, sel, high, low = wall_edges(n_y, mx, my, aux, yrows, sv, left, right, chosen, wall)
    mine, moved = x_join(my, xrows, yrows, scal, s_edge, mine, other, received, shifts)
    shifts = list(range(n_y))
    received = [rotate(mine, "gy", s) if s else mine for s in shifts]
    w = wall_sweep(sel, high, low, w)
    return finish(xrows, yrows, moved, solid_mask.T, zh, w, received, shifts)


def solution(mesh):
    placed = (
        P("gx", None, "gy"),
        P("gx", None),
        P("gx", None),
        P("gx"),
        P("gx"),
        P("gy", None),
        P("gy", None),
        P("gy"),
        P("gy"),
        P(("gx", "gy"), None, None),
        P(("gx", "gy"), None),
        P(("gx", "gy")),
        P("gx", "gy"),
    )
    return jax.shard_map(
        on_device, mesh=mesh, in_specs=placed, out_specs=P("gx", None, "gy"), check_vma=False
    )
```

```python
import functools

import jax
import jax.numpy as jnp
from jax import lax
from jax.experimental import pallas as pl
from jax.experimental.pallas import tpu as pltpu
from jax.sharding import PartitionSpec as P

F32 = jnp.float32
BF16 = jnp.bfloat16
HIGHEST = lax.Precision.HIGHEST
VMEM = pl.BlockSpec(memory_space=pltpu.VMEM)
SMEM = pl.BlockSpec(memory_space=pltpu.SMEM)
HBM = pl.BlockSpec(memory_space=pltpu.HBM)
LANES = 128
GROUP = 4


def f32_dot(left, right, dims):
    return lax.dot_general(left, right, (dims, ((), ())), precision=HIGHEST, preferred_element_type=F32)


def split(value):
    high = value.astype(BF16)
    return high, (value - high.astype(F32)).astype(BF16)


def left_of(value, axis):
    high, low = split(value)
    return jnp.concatenate([high, low, high], axis=axis)


def right_of(value, axis):
    high, low = split(value)
    return jnp.concatenate([high, high, low], axis=axis)


def bf16_dot(left, right, dims):
    return lax.dot_general(left, right, (dims, ((), ())), preferred_element_type=F32)


def params(vmem_mib, side_effects=False):
    return pltpu.CompilerParams(vmem_limit_bytes=vmem_mib << 20)


def pin(value):
    return pltpu.with_memory_space_constraint(value, pltpu.HBM)


def call(kernel, out_shape, in_specs, vmem_mib, out_specs=None, scratch=(), flops=0, moved=0, **more):
    if out_specs is None:
        out_specs = jax.tree.map(lambda _: VMEM, out_shape)
    return pl.pallas_call(
        kernel,
        out_shape=out_shape,
        in_specs=in_specs,
        out_specs=out_specs,
        scratch_shapes=list(scratch),
        compiler_params=params(vmem_mib),
        cost_estimate=pl.CostEstimate(flops=flops, bytes_accessed=moved, transcendentals=0),
        **more,
    )


def struct(*shape, dtype=F32):
    return jax.ShapeDtypeStruct(shape, dtype)


def sort_walls(count, room, me, walls, owner_ref, table, taken):
    for shift in range(count):
        taken[shift] = shift * room

    def step(entry, carry):
        shift = owner_ref[entry] ^ me
        slot = taken[shift]
        taken[shift] = slot + 1
        table[slot] = entry
        return carry

    lax.fori_loop(0, walls, step, 0, unroll=8)


def pack_kernel(count, room, owner_ref, offset_ref, force_ref, *refs):
    outs, (table, taken) = refs[:count], refs[count:]
    walls, planes, width = force_ref.shape
    me = lax.axis_index("gy")
    for slot in range(count * room):
        table[slot] = walls
    sort_walls(count, room, me, walls, owner_ref, table, taken)
    lane = lax.broadcasted_iota(jnp.int32, (planes, LANES), 1)
    for shift in list(range(1, count)) + [0]:
        places = jnp.full((planes, LANES), -1, jnp.int32)
        for slot in range(room):
            entry = table[shift * room + slot]
            real = jnp.minimum(entry, walls - 1)
            outs[shift][slot] = jnp.where(entry < walls, force_ref[real], 0.0)
            places = jnp.where(lane == slot, jnp.where(entry < walls, offset_ref[real], -1), places)
        outs[shift][room] = places.astype(F32)


def pack(owner, offset, force, count, room):
    walls, planes, width = force.shape
    return call(
        functools.partial(pack_kernel, count, room),
        [struct(room + 1, planes, width) for s in range(count)],
        [SMEM, SMEM, VMEM],
        8,
        scratch=[pltpu.SMEM((count * room,), jnp.int32), pltpu.SMEM((count,), jnp.int32)],
    )(pin(owner), pin(offset), pin(force))


def row(ref, index):
    base = index // 8 * 8
    return ref[base : base + 8, :][index - base : index - base + 1]


def half_shift_lanes(value):
    length = value.shape[1]
    at = lax.broadcasted_iota(jnp.int32, value.shape, 1)
    before = jnp.where(at == 0, 0.0, pltpu.roll(value, 1, 1))
    after = jnp.where(at == length - 1, 0.0, pltpu.roll(value, length - 1, 1))
    return 0.5 * (before + after)


def half_shift_rows(value):
    length = value.shape[0]
    at = lax.broadcasted_iota(jnp.int32, value.shape, 0)
    before = jnp.where(at == 0, 0.0, pltpu.roll(value, 1, 0))
    after = jnp.where(at == length - 1, 0.0, pltpu.roll(value, length - 1, 0))
    return 0.5 * (before + after)


def factor_kernel(v_hbm, *refs):
    given, (mx, my, my_t, xrows, yrows, frows, scal) = refs[:8], refs[8:15]
    v_ref, edge_ref, first_ref, last_ref = refs[15:19]
    fetched, (sem, v_sem) = refs[19:27], refs[27:]
    planes, rows, cols = v_ref.shape
    copies = [pltpu.make_async_copy(given[i], fetched[i], sem.at[i]) for i in range(8)]
    for copy in copies:
        copy.start()

    def v_copy(p):
        return pltpu.make_async_copy(v_hbm.at[:, p, :], v_ref.at[p], v_sem.at[p])

    for p in range(planes):
        v_copy(p).start()
    for copy in copies:
        copy.wait()
    lx, ux, lcx, ucx, ly, uy, lcy, ucy = fetched
    rows_x, rows_y = lx.shape[0], ly.shape[0]
    both = bf16_dot(right_of(ux[...], 1), left_of(lx[...], 0), ((1,), (0,)))
    zero = jnp.zeros((1, rows_x), F32)
    frows[...] = jnp.concatenate([row(lx, rows_x - 1), both[0:8][0:1], zero, zero, zero, zero, zero, zero], 0)
    mx[...] = left_of(half_shift_rows(both), 1)
    both_y = bf16_dot(right_of(uy[...], 1), left_of(ly[...], 0), ((1,), (0,)))
    turned = both_y.T
    my[...] = left_of(turned, 0)
    my_t[...] = left_of(half_shift_rows(turned), 0)
    lc, uc = lcx[...], ucx[...]
    pad = jnp.zeros((7, rows_x), F32)
    u_lc = f32_dot(jnp.concatenate([lc, pad], 0), ux[...], ((1,), (1,)))[0:1]
    at = lax.broadcasted_iota(jnp.int32, (1, rows_x), 1)
    c0 = half_shift_lanes(u_lc)
    c1 = half_shift_lanes(uc) + jnp.where(at == rows_x - 1, 0.5, 0.0)
    c2 = jnp.where(at == 0, 0.5, 0.0)
    xrows[...] = jnp.concatenate([c0, c1, c2, zero, zero, zero, zero, zero], 0)
    lcv, ucv = lcy[...], ucy[...]
    pad_y = jnp.zeros((7, rows_y), F32)
    uy_lc = f32_dot(jnp.concatenate([lcv, pad_y], 0), uy[...], ((1,), (1,)))[0:1]
    f0 = row(ly, rows_y - 1)
    f1 = both_y[0:8][0:1]
    zero_y = jnp.zeros((1, rows_y), F32)
    m0, m1 = 0.5 * turned[0:8][0:1], 0.5 * turned[rows_y - 8 : rows_y][7:8]
    yrows[...] = jnp.concatenate([uy_lc, ucv, m0, m1, f0, f1, zero_y, zero_y], 0)

    def spread(value, index, width):
        return jnp.broadcast_to(value[:, index : index + 1], (1, width))

    last = row(ux, rows_x - 1)
    scal[0:8, :] = jnp.concatenate(
        [
            spread(lc, rows_x - 1, rows_x),
            spread(u_lc, 0, rows_x),
            spread(uc, 0, rows_x),
            spread(last, rows_x - 1, rows_x),
            spread(uc, rows_x - 1, rows_x),
            zero,
            zero,
            zero,
        ],
        0,
    )
    scal[8:16, :] = jnp.concatenate(
        [
            spread(lcv, rows_y - 1, rows_x),
            spread(uy_lc, 0, rows_x),
            spread(ucv, 0, rows_x),
            zero,
            zero,
            zero,
            zero,
            zero,
        ],
        0,
    )


    column = frows[...].T
    weights = [jnp.broadcast_to(column[:, f : f + 1], (rows, LANES)) for f in range(2)]
    lane = lax.broadcasted_iota(jnp.int32, (rows, LANES), 1)
    ends = jnp.zeros((rows, LANES), F32)
    for p in range(planes):
        if p % GROUP == 0:
            for here in range(p, p + GROUP):
                v_copy(here).wait()
        for b in range(cols // LANES):
            lanes = slice(b * LANES, (b + 1) * LANES)
            value = v_ref[p, :, lanes]
            for f in range(2):
                edge_ref[f, p : p + 1, lanes] = jnp.sum(value * weights[f], axis=0, keepdims=True)
        ends = jnp.where(lane == p, pltpu.roll(v_ref[p, :, 0:LANES], p, 1), ends)
        to = planes + p
        ends = jnp.where(lane == to, pltpu.roll(v_ref[p, :, cols - LANES : cols], (to + 1) % LANES, 1), ends)
    for f in range(2):
        edge_ref[f] = half_shift_lanes(edge_ref[f])
    turned_ends = ends.T
    first_ref[...] = turned_ends[0:planes]
    last_ref[...] = turned_ends[planes : 2 * planes]


def factors(velocity, lx, ux, lcx, ucx, ly, uy, lcy, ucy):
    rows, planes, cols = velocity.shape
    given = (lx, ux, lcx[None, :], ucx[None, :], ly, uy, lcy[None, :], ucy[None, :])
    return call(
        factor_kernel,
        [
            struct(rows, 3 * rows, dtype=BF16),
            struct(3 * cols, cols, dtype=BF16),
            struct(3 * cols, cols, dtype=BF16),
            struct(8, rows),
            struct(8, cols),
            struct(8, rows),
            struct(16, rows),
            struct(planes, rows, cols),
            struct(2, planes, cols),
            struct(planes, rows),
            struct(planes, rows),
        ],
        [HBM] * 9,
        8,
        scratch=[pltpu.VMEM(g.shape, F32) for g in given]
        + [
            pltpu.SemaphoreType.DMA((8,)),
            pltpu.SemaphoreType.DMA((planes,)),
        ],
    )(pin(velocity), *[pin(g) for g in given])


def velocity_kernel(some, mx, my_t, yrows, v_ref, w_ref, s_ref):
    planes, rows, cols = v_ref.shape
    lane = lax.broadcasted_iota(jnp.int32, (rows, LANES), 1)
    total = jnp.zeros((rows, LANES), F32)
    last = half_shift_lanes(yrows[4:5, :])
    for q in range(0, planes, some):
        flat = right_of(v_ref[q : q + some].reshape(some * rows, cols), 1)
        r = bf16_dot(flat, my_t[...], ((1,), (0,)))
        for i in range(some):
            p = q + i
            here = slice(i * rows, (i + 1) * rows)
            total = jnp.where(lane == p, jnp.sum(v_ref[p] * last, axis=1, keepdims=True), total)
            total = jnp.where(lane == 64 + p, r[here][:, 0:1], total)
            w_ref[p] = bf16_dot(mx[...], right_of(r[here], 0), ((1,), (0,)))
    s_ref[...] = total


def velocity_part(mx, my_t, yrows, velocity):
    planes, rows, cols = velocity.shape
    return call(
        functools.partial(velocity_kernel, 4),
        [struct(planes, rows, cols), struct(rows, LANES)],
        [VMEM] * 4,
        16,
    )(mx, my_t, yrows, velocity)


def halos(count, left_ref, right_ref):
    me = lax.axis_index("gy")
    return jnp.where(me > 0, left_ref[...], 0.0), jnp.where(me < count - 1, right_ref[...], 0.0)


def x_edge_kernel(count, room, edge_ref, frows, scal, left_ref, right_ref, *refs):
    payload, (out, chosen_ref, wall_ref) = refs[:count], refs[count:]
    planes, slots, cols = wall_ref.shape
    rows = frows.shape[1]
    width = payload[0].shape[2]
    nblock = cols // width
    blocks = cols // LANES
    lane8 = lax.broadcasted_iota(jnp.int32, (8, slots), 1)
    places = jnp.full((8, slots), -1.0, F32)
    for s in range(count):
        here = payload[s][room][0:8]
        if s:
            here = pltpu.roll(here, s * room, 1)
        places = jnp.where((lane8 >= s * room) & (lane8 < (s + 1) * room), here, places)
    line = jnp.floor(places * (1.0 / nblock))
    half = places - nblock * line
    row_ids = lax.broadcasted_iota(jnp.int32, (rows, slots), 0).astype(F32)
    chosen = jnp.where(row_ids == line[0:1], 1.0, 0.0)
    chosen_ref[...] = chosen.astype(BF16)
    weight = f32_dot(frows[...], chosen, ((1,), (0,)))
    sub8 = lax.broadcasted_iota(jnp.int32, (8, slots), 0)
    column = jnp.where(sub8 == 2, half, weight).T
    step = min(room, 16)
    for s in range(count):
        for g in range(room // step):
            at = slice(s * room + g * step, s * room + (g + 1) * step)
            value = jnp.swapaxes(payload[s][g * step : (g + 1) * step], 0, 1)
            for b in range(nblock):
                keep = jnp.broadcast_to(column[at, 2:3] == b, (step, width))
                wall_ref[:, at, b * width : (b + 1) * width] = jnp.where(keep[None], value, 0.0)
    at = lax.broadcasted_iota(jnp.int32, (planes, cols), 1)
    hl, hr = halos(count, left_ref, right_ref)
    for f in range(2):
        func = frows[f : f + 1, :]
        first = 0.5 * jnp.sum(hl * func, axis=1, keepdims=True)
        last = 0.5 * jnp.sum(hr * func, axis=1, keepdims=True)
        edge = edge_ref[f] + jnp.where(at == 0, first, 0.0) + jnp.where(at == cols - 1, last, 0.0)
        for b in range(blocks):
            row = (f * blocks + b) * planes
            out[row : row + planes, :] = edge[:, b * LANES : (b + 1) * LANES]
    spread = [jnp.broadcast_to(column[:, f : f + 1], (slots, LANES)) for f in range(2)]
    for p in range(planes):
        for b in range(blocks):
            lanes = slice(b * LANES, (b + 1) * LANES)
            value = wall_ref[p, :, lanes]
            for f in range(2):
                at = (f * blocks + b) * planes + p
                out[at : at + 1, :] = out[at : at + 1, :] + jnp.sum(value * spread[f], axis=0, keepdims=True)
    out[2 * blocks * planes : 2 * blocks * planes + 8, :] = scal[0:8, 0:LANES]


def x_edges(edge, frows, scal, left, right, payload, room):
    planes, cols = edge.shape[1:]
    count, rows = len(payload), frows.shape[1]
    slots = count * room
    return call(
        functools.partial(x_edge_kernel, count, room),
        [struct(2 * planes * (cols // LANES) + 8, LANES), struct(rows, slots, dtype=BF16), struct(planes, slots, cols)],
        [VMEM] * (5 + count),
        8,
    )(edge, frows, scal, left, right, *payload)


def wall_kernel(count, mx, my, yrows, sv_ref, left_ref, right_ref, chosen_ref, wall_ref, s_ref, zh_ref, sel_ref, high_ref, low_ref):
    planes, slots, cols = wall_ref.shape
    rows = mx.shape[0]
    hl, hr = halos(count, left_ref, right_ref)
    m = mx[...]
    zh = bf16_dot(right_of(jnp.concatenate([hl, hr], 0), 1), m, ((1,), (1,)))
    zh_ref[...] = zh
    chosen = chosen_ref[...]
    sel_high = bf16_dot(m[:, 0:rows], chosen, ((1,), (0,))).astype(BF16)
    sel_low = bf16_dot(m[:, rows : 2 * rows], chosen, ((1,), (0,))).astype(BF16)
    sel = jnp.concatenate([sel_high, sel_low, sel_high], 1)
    sel_ref[...] = sel
    lane = lax.broadcasted_iota(jnp.int32, (slots, LANES), 1)
    total = jnp.zeros((slots, LANES), F32)
    some = 8
    for q in range(0, planes, some):
        flat = wall_ref[q : q + some].reshape(some * slots, cols)
        wc = right_of(flat, 1)
        r = bf16_dot(wc, my[...], ((1,), (0,)))
        high, low = split(r)
        high_ref[q : q + some] = high.reshape(some, slots, cols)
        low_ref[q : q + some] = low.reshape(some, slots, cols)
        for i in range(some):
            p = q + i
            total = jnp.where(lane == p, jnp.sum(wall_ref[p] * yrows[4:5, :], axis=1, keepdims=True), total)
            total = jnp.where(lane == 64 + p, r[i * slots : (i + 1) * slots, 0:1], total)
    left = jnp.concatenate([m, sel], 1)
    turned = bf16_dot(left, jnp.concatenate([right_of(sv_ref[...], 0), right_of(total, 0)], 0), ((1,), (0,))).T
    low, high = turned[0:planes], turned[64 : 64 + planes]
    f0, f1 = yrows[4:5, :], yrows[5:6, :]
    zl, zr = zh[0:planes], zh[planes : 2 * planes]
    s_ref[0:planes, :] = low + 0.5 * (zl * f0[:, 0:1] + zr * f0[:, cols - 1 : cols])
    s_ref[planes : 2 * planes, :] = high + 0.5 * (zl * f1[:, 0:1] + zr * f1[:, cols - 1 : cols])


def wall_edges(count, mx, my, yrows, sv, left, right, chosen, wall):
    rows = mx.shape[0]
    planes, slots, cols = wall.shape
    return call(
        functools.partial(wall_kernel, count),
        [struct(2 * planes, rows), struct(2 * planes, rows), struct(rows, 3 * slots, dtype=BF16)]
        + [struct(*wall.shape, dtype=BF16)] * 2,
        [VMEM] * 8,
        8,
    )(mx, my, yrows, sv, left, right, chosen, wall)


def wall_sweep_kernel(sel, high_ref, low_ref, v_ref, w_ref):
    for p in range(w_ref.shape[0]):
        high = high_ref[p]
        w_ref[p] = v_ref[p] + bf16_dot(sel[...], jnp.concatenate([high, high, low_ref[p]], 0), ((1,), (0,)))


def wall_sweep(sel, high, low, w):
    return call(
        wall_sweep_kernel,
        struct(*w.shape),
        [VMEM] * 4,
        8,
        input_output_aliases={3: 0},
    )(sel, high, low, w)


def pack_edges(first, second, scalars):
    blocks = range(first.shape[1] // LANES)
    pieces = [value[:, b * LANES : (b + 1) * LANES] for value in (first, second) for b in blocks]
    return jnp.concatenate(pieces + [scalars[:, 0:LANES]], 0)


def unpack_edges(flat, planes):
    blocks = (flat.shape[0] - 8) // (2 * planes)
    pieces = [flat[b * planes : (b + 1) * planes] for b in range(2 * blocks)]
    scalars = jnp.concatenate([flat[2 * blocks * planes :]] * blocks, 1)
    return jnp.concatenate(pieces[:blocks], 1), jnp.concatenate(pieces[blocks:], 1), scalars


def chain(parts, count, me, planes, f_in):
    zero = jnp.zeros(f_in.shape[1:], F32)
    edges = [unpack_edges(parts[k], planes) for k in range(count)]
    f, mine_f = zero, zero
    for k in range(count):
        f_in[k] = f
        mine_f = jnp.where(k == me, f, mine_f)
        f = edges[k][0] + edges[k][2][0:1] * f
    g, mine_g = zero, zero
    for k in range(count - 1, -1, -1):
        scal = edges[k][2]
        mine_g = jnp.where(k == me, g, mine_g)
        g = edges[k][1] + scal[1:2] * f_in[k] + scal[2:3] * g
    return mine_f, mine_g


def pair_kernel(planes, mine, other, out):
    odd = lax.rem(lax.axis_index("gx"), 2) == 1
    left = jnp.where(odd, other[...], mine[...])
    right = jnp.where(odd, mine[...], other[...])
    out[...] = joined(left, right, planes)


def joined(left, right, planes):
    a, b, s = unpack_edges(left, planes)
    c, d, t = unpack_edges(right, planes)
    l0, c0, u0 = s[0:1], s[1:2], s[2:3]
    l1, c1, u1 = t[0:1], t[1:2], t[2:3]
    scalars = jnp.concatenate([l0 * l1, c0 + u0 * c1 * l0, u0 * u1, t[3:8]], 0)
    return pack_edges(c + l1 * a, b + u0 * (d + c1 * a), scalars)


def pair(mine, other, planes):
    return call(functools.partial(pair_kernel, planes), struct(*mine.shape), [VMEM, VMEM], 8)(mine, other)


def gather_parts(me, parts, received, shifts):
    count = len(received)
    for shift, value in zip(shifts, received, strict=True):
        parts[pl.ds(lax.rem(me - shift + count, count), 1)] = value[...][None]


def x_join_kernel(count, shifts, my, xrows, yrows, scal, s_ref, mine_ref, other_ref, *refs):
    received, (out, moved, parts, f_in) = refs[:count], refs[count:]
    me = lax.axis_index("gx")
    place = lax.div(me, 2)
    odd = lax.rem(me, 2) == 1
    planes = s_ref.shape[0] // 2
    gather_parts(place, parts, received, shifts)
    f, g = chain(parts, count, place, planes, f_in)
    mine, other = mine_ref[...], other_ref[...]
    left, right = jnp.where(odd, other, mine), jnp.where(odd, mine, other)
    a, _, ls = unpack_edges(left, planes)
    _, d, rs = unpack_edges(right, planes)
    f_mid = a + ls[0:1] * f
    g_mid = d + rs[1:2] * f_mid + rs[2:3] * g
    in_f, in_b = jnp.where(odd, f_mid, f), jnp.where(odd, g, g_mid)
    _, mine_b, ms = unpack_edges(mine, planes)
    first = mine_b + ms[1:2] * in_f + ms[2:3] * in_b
    before_s = jnp.where(odd, ls, unpack_edges(parts[jnp.maximum(place - 1, 0)], planes)[2])
    before = jnp.where(me > 0, before_s[3:4] * in_f + before_s[4:5] * first, 0.0)
    low, high = s_ref[0:planes, :], s_ref[planes : 2 * planes, :]
    f0, f1 = yrows[4:5, :], yrows[5:6, :]
    for index, value in enumerate((in_f, in_b, before)):
        c = xrows[index : index + 1, :]
        low = low + jnp.sum(value * f0, axis=1, keepdims=True) * c
        high = high + jnp.sum(value * f1, axis=1, keepdims=True) * c
    out[...] = pack_edges(low, high, scal[8:16, :])
    moved[...] = bf16_dot(right_of(jnp.concatenate([in_f, in_b, before], 0), 1), my[...], ((1,), (0,)))


def x_join(my, xrows, yrows, scal, s, mine, other, received, shifts):
    count = len(received)
    height, cols = received[0].shape[0], my.shape[1]
    planes, rows = s.shape[0] // 2, s.shape[1]
    return call(
        functools.partial(x_join_kernel, count, shifts),
        [struct(2 * planes * (rows // LANES) + 8, LANES), struct(3 * planes, cols)],
        [VMEM] * (7 + count),
        8,
        scratch=[pltpu.VMEM((count, height, LANES), F32), pltpu.VMEM((count, planes, cols), F32)],
    )(my, xrows, yrows, scal, s, mine, other, *received)


def finish_kernel(count, shifts, xrows, yrows, moved, solid, zh_ref, w_ref, *refs):
    received, (out_hbm, parts, f_in, out_ref, out_sem) = refs[:count], refs[count:]
    me = lax.axis_index("gy")
    planes, rows, cols = w_ref.shape

    def out_copy(p):
        return pltpu.make_async_copy(out_ref.at[p], out_hbm.at[:, p, :], out_sem.at[p])

    gather_parts(me, parts, received, shifts)
    in_f, in_b = chain(parts, count, me, planes, f_in)
    y = yrows[0:4, :]
    c = xrows[0:3, :]
    nblock = solid.shape[0]
    marks = jnp.concatenate([solid[...].astype(F32), jnp.zeros((8 - nblock, rows), F32)], 0).T
    width = cols // nblock
    fluid = jnp.concatenate([jnp.broadcast_to(marks[:, b : b + 1] == 0.0, (rows, width)) for b in range(nblock)], 1)
    zero = jnp.zeros((1, rows), F32)
    zero_y = jnp.zeros((1, cols), F32)
    for p in range(planes):
        left = jnp.concatenate(
            [c, in_f[p : p + 1], in_b[p : p + 1], zh_ref[p : p + 1, :], zh_ref[planes + p : planes + p + 1, :], zero], 0
        )
        right = jnp.concatenate(
            [
                moved[p : p + 1, :],
                moved[planes + p : planes + p + 1, :],
                moved[2 * planes + p : 2 * planes + p + 1, :],
                y,
                zero_y,
            ],
            0,
        )
        lh = left.astype(BF16).astype(F32)
        rh = right.astype(BF16).astype(F32)
        lc = jnp.concatenate([lh, lh, left - lh], 0).astype(BF16)
        rc = jnp.concatenate([rh, right - rh, rh], 0).astype(BF16)
        value = w_ref[p] + bf16_dot(lc, rc, ((0,), (0,)))
        out_ref[p] = jnp.where(fluid, value, 0.0)
        if (p + 1) % GROUP == 0:
            for done in range(p + 1 - GROUP, p + 1):
                out_copy(done).start()
    for p in range(planes):
        out_copy(p).wait()


def finish(xrows, yrows, moved, solid, zh, w, received, shifts):
    count = len(received)
    height = received[0].shape[0]
    planes, rows, cols = w.shape
    return call(
        functools.partial(finish_kernel, count, shifts),
        struct(rows, planes, cols),
        [VMEM] * (6 + count),
        12,
        out_specs=HBM,
        scratch=[
            pltpu.VMEM((count, height, LANES), F32),
            pltpu.VMEM((count, planes, rows), F32),
            pltpu.VMEM((planes, rows, cols), F32),
            pltpu.SemaphoreType.DMA((planes,)),
        ],
    )(xrows, yrows, moved, solid, zh, w, *received)


def swap(value, axis, mask):
    return lax.ppermute(value, axis, [(i, i ^ mask) for i in range(lax.axis_size(axis))])


def rotate(value, axis, shift):
    count = lax.axis_size(axis)
    return lax.ppermute(value, axis, [(i, (i + shift) % count) for i in range(count)])


def on_device(
    velocity,
    lower_x,
    upper_x,
    lower_carry_x,
    upper_carry_x,
    lower_y,
    upper_y,
    lower_carry_y,
    upper_carry_y,
    wall_force,
    wall_owner,
    wall_offset,
    solid_mask,
):
    rows, planes, cols = velocity.shape
    walls = wall_force.shape[0]
    n_x, n_y = lax.axis_size("gx"), lax.axis_size("gy")
    room = 2 * walls // n_y
    packed = pack(wall_owner[:, 0], wall_offset, wall_force, n_y, room)
    payload = [packed[0]] + [swap(packed[s], "gy", s) for s in range(1, n_y)]
    mx, my, my_t, xrows, yrows, frows, scal, v, edge, first, last = factors(
        velocity,
        lower_x,
        upper_x,
        lower_carry_x,
        upper_carry_x,
        lower_y,
        upper_y,
        lower_carry_y,
        upper_carry_y,
    )
    left, right = rotate(last, "gy", 1), rotate(first, "gy", -1)
    w, sv = velocity_part(mx, my_t, yrows, v)
    w, sv, edge = lax.optimization_barrier((w, sv, edge))
    mine, chosen, wall = x_edges(edge, frows, scal, left, right, payload, room)
    other = swap(mine, "gx", 1)
    both = pair(mine, other, planes)
    shifts = list(range(n_x // 2))
    received = [rotate(both, "gx", 2 * s) if s else both for s in shifts]
    s_edge, zh, sel, high, low = wall_edges(n_y, mx, my, yrows, sv, left, right, chosen, wall)
    mine, moved = x_join(my, xrows, yrows, scal, s_edge, mine, other, received, shifts)
    shifts = list(range(n_y))
    received = [rotate(mine, "gy", s) if s else mine for s in shifts]
    w = wall_sweep(sel, high, low, w)
    return finish(xrows, yrows, moved, solid_mask.T, zh, w, received, shifts)


def solution(mesh):
    placed = (
        P("gx", None, "gy"),
        P("gx", None),
        P("gx", None),
        P("gx"),
        P("gx"),
        P("gy", None),
        P("gy", None),
        P("gy"),
        P("gy"),
        P(("gx", "gy"), None, None),
        P(("gx", "gy"), None),
        P(("gx", "gy")),
        P("gx", "gy"),
    )
    return jax.shard_map(
        on_device, mesh=mesh, in_specs=placed, out_specs=P("gx", None, "gy"), check_vma=False
    )
```
